32 devices in a mesh: seq: 4 (over y, core), wsh: 8 (over z, x).
Axes of the slice: x: 2, y: 2, z: 4, core: 2. Of those that a mesh axis runs over, the one named last changes fastest.
Arguments:
- tokens: bfloat16 [8, 1024, 2048], P('wsh', 'seq'), may hold values from -6 to 6
- token_document: int32 [8, 1024], P('wsh', 'seq'), may hold values from 0 to 7, never falling along the last dimension, each value on 1 to 512 neighbouring positions
- document_adapter: int32 [8, 8], P('wsh'), may hold values from 0 to 7
- attention_norm_gain: float32 [2048], replicated, may hold values from 0.5 to 1.5
- feedforward_norm_gain: float32 [2048], replicated, may hold values from 0.5 to 1.5
- query_weight: bfloat16 [2048, 2048], P('wsh'), may hold values from -0.375 to 0.375
- key_weight: bfloat16 [2048, 512], P('wsh'), may hold values from -0.375 to 0.375
- value_weight: bfloat16 [2048, 512], P('wsh'), may hold values from -0.125 to 0.125
- output_weight: bfloat16 [2048, 2048], P('wsh'), may hold values from -1.5 to 1.5
- gate_weight: bfloat16 [2048, 8192], P('wsh'), may hold values from -0.125 to 0.125
- up_weight: bfloat16 [2048, 8192], P('wsh'), may hold values from -0.125 to 0.125
- down_weight: bfloat16 [8192, 2048], P('wsh'), may hold values from -0.375 to 0.375
- attention_down_maps: bfloat16 [2048, 8, 48], replicated, may hold values from -0.125 to 0.125
- query_exit_maps: bfloat16 [8, 16, 2048], replicated, may hold values from -1.5 to 1.5
- key_value_exit_maps: bfloat16 [2, 8, 16, 512], replicated, may hold values from -1.5 to 1.5
- output_entry_maps: bfloat16 [2048, 8, 16], replicated, may hold values from -0.125 to 0.125
- output_exit_maps: bfloat16 [8, 16, 2048], replicated, may hold values from -1.5 to 1.5
- feedforward_entry_maps: bfloat16 [2048, 8, 32], replicated, may hold values from -0.125 to 0.125
- feedforward_exit_maps: bfloat16 [2, 8, 16, 8192], replicated, may hold values from -1.5 to 1.5
- down_entry_maps: bfloat16 [8192, 8, 16], replicated, may hold values from -0.0625 to 0.0625
- down_exit_maps: bfloat16 [8, 16, 2048], replicated, may hold values from -1.5 to 1.5
- cotangent: bfloat16 [8, 1024, 2048], P('wsh', 'seq'), may hold values from -6 to 6
Outputs:
- layer_out: bfloat16 [8, 1024, 2048], P('wsh', 'seq')
- grad_tokens: float32 [8, 1024, 2048], P('wsh', 'seq')
- attention_input_gradient: float32 [2048, 8, 48], replicated
- query_output_gradient: float32 [8, 16, 2048], replicated
- grad_b_kv: float32 [2, 8, 16, 512], replicated
- output_input_gradient: float32 [2048, 8, 16], replicated
- output_output_gradient: float32 [8, 16, 2048], replicated
- feedforward_input_gradient: float32 [2048, 8, 32], replicated
- grad_b_mlp: float32 [2, 8, 16, 8192], replicated
- down_input_gradient: float32 [8192, 8, 16], replicated
- down_output_gradient: float32 [8, 16, 2048], replicated
The draws below stay inside these ranges and needn't reach their ends.
Inputs may be any that keep to these rules, and one draw needn't show every extreme that they name: `token_document`: document numbers of one stream never fall along it; each document has 1 to 512 tokens.
All inputs are finite; a program needn't handle non-finite values.
Results may differ from the reference program's by a relative error of at most 0.018.
Values may be sent and summed in bfloat16 or wider, within the bound.
No kernel may reach another device: no remote copies, remote signals or barrier semaphores. Data moves between devices by JAX's collectives and lax.ppermute only.
A program may use at most 320 MiB of HBM per device.

```python
import math
import jax
import jax.numpy as jnp
import numpy as np
from jax import lax

MODEL_WIDTH = 2048
QUERY_HEADS = 32
KEY_HEADS = 8
HEAD_WIDTH = 64
HIDDEN_UNITS = 8192
ADAPTER_RANK = 16
ADAPTER_COUNT = 8
DOCS = 8
LEN = 1024
STREAMS = 8
MAXDOC = 512


def place_ends(result, rng, low, high):
    longest = result.shape.index(max(result.shape))
    spots = []
    for shift in (0, 1):
        where = [jax.random.randint(jax.random.fold_in(rng, axis), (), 0, length) for axis, length in enumerate(result.shape)]
        where[longest] = (where[longest] + shift) % result.shape[longest]
        spots.append(tuple(where))
    return result.at[spots[0]].set(low).at[spots[1]].set(high)


def levels(key, dims, cuts, smallest, top_value):
    factor_of = 1.0
    for axis_at, parts in cuts:
        steps = jax.random.uniform(jax.random.fold_in(jax.random.fold_in(key, 6), axis_at), (parts,), jnp.float32, smallest / len(cuts), top_value / len(cuts))
        factor_of = factor_of * jnp.repeat(jnp.exp(steps), dims[axis_at] // parts).reshape((-1,) + (1,) * (len(dims) - 1 - axis_at))
    return factor_of


def split_up(amount, total, most, slope):
    weights = [(1 << 20) // math.isqrt(standing ** slope) + 1 for standing in range(2, amount + 1)]
    rest, holding = total - most - (amount - 1), [1] * (amount - 1)
    while rest > 0:
        candidates = [i for i in range(amount - 1) if holding[i] < most]
        pool, budget = sum([weights[i] for i in candidates]), rest
        for i in candidates:
            addition = min(most - holding[i], max(1, budget * weights[i] // pool), rest)
            holding[i] = holding[i] + addition
            rest = rest - addition
    return np.array([most] + holding)


def ragged(rng, number_of, total, limit, slope):
    if number_of == 2:
        one = jax.random.randint(rng, (), max(1, total - limit), min(limit, total - 1) + 1)
        return jnp.stack([one, total - one])
    tallies = jnp.asarray(split_up(number_of, total, limit, slope), jnp.int32)
    pairs = (number_of - 1) // 2
    giver, taker = tallies[1:1 + 2 * pairs:2], tallies[2:2 + 2 * pairs:2]
    room = jnp.minimum(giver - 1, limit - taker)
    moved = jax.random.randint(jax.random.fold_in(rng, 1), (pairs,), 0, 1 << 20) % (room + 1)
    tallies = tallies.at[1:1 + 2 * pairs:2].set(giver - moved).at[2:2 + 2 * pairs:2].set(taker + moved)
    return tallies[jax.random.permutation(jax.random.fold_in(rng, 2), number_of)]


def normal_values(rng, dims, width, bound, pieces=(), held_as=jnp.bfloat16):
    factor_of = levels(rng, dims, pieces, -0.22, 0.18) if pieces else 1.0
    result = jax.random.normal(rng, dims, jnp.float32) * width * factor_of
    return jnp.minimum(jnp.maximum(result, -bound), bound).astype(held_as)


def setup_inputs(seed: int = 0) -> dict:
    key_list = jax.random.split(jax.random.key(seed), 23)
    return {
        "tokens": normal_values(key_list[0], (STREAMS, LEN, MODEL_WIDTH), 1.0, 6.0, ((0, 8), (1, 4))),
        "token_document": jax.vmap(lambda own: jnp.searchsorted(jnp.cumsum(ragged(own, DOCS, LEN, MAXDOC, 2)), jnp.arange(LEN), side="right"))(jax.random.split(key_list[1], STREAMS)).reshape((STREAMS, LEN)).astype(jnp.int32),
        "document_adapter": place_ends(jax.random.randint(key_list[2], (STREAMS, DOCS), 0, ADAPTER_COUNT), jax.random.fold_in(key_list[2], 1), 0, ADAPTER_COUNT - 1).astype(jnp.int32),
        "attention_norm_gain": jnp.clip(1.0 + 0.1 * jax.random.normal(key_list[3], (MODEL_WIDTH,), jnp.float32), 0.5, 1.5),
        "feedforward_norm_gain": jnp.clip(1.0 + 0.1 * jax.random.normal(key_list[4], (MODEL_WIDTH,), jnp.float32), 0.5, 1.5),
        "query_weight": normal_values(key_list[5], (MODEL_WIDTH, QUERY_HEADS * HEAD_WIDTH), (MODEL_WIDTH // 8) ** -0.5, 0.375, ((0, 8),)),
        "key_weight": normal_values(key_list[6], (MODEL_WIDTH, KEY_HEADS * HEAD_WIDTH), (MODEL_WIDTH // 8) ** -0.5, 0.375, ((0, 8),)),
        "value_weight": normal_values(key_list[7], (MODEL_WIDTH, KEY_HEADS * HEAD_WIDTH), MODEL_WIDTH ** -0.5, 0.125, ((0, 8),)),
        "output_weight": normal_values(key_list[8], (QUERY_HEADS * HEAD_WIDTH, MODEL_WIDTH), (max(1, QUERY_HEADS * HEAD_WIDTH // 128)) ** -0.5, 1.5, ((0, 8),)),
        "gate_weight": normal_values(key_list[9], (MODEL_WIDTH, HIDDEN_UNITS), MODEL_WIDTH ** -0.5, 0.125, ((0, 8),)),
        "up_weight": normal_values(key_list[10], (MODEL_WIDTH, HIDDEN_UNITS), MODEL_WIDTH ** -0.5, 0.125, ((0, 8),)),
        "down_weight": normal_values(key_list[11], (HIDDEN_UNITS, MODEL_WIDTH), (HIDDEN_UNITS // 32) ** -0.5, 0.375, ((0, 8),)),
        "attention_down_maps": normal_values(key_list[12], (MODEL_WIDTH, ADAPTER_COUNT, 3 * ADAPTER_RANK), MODEL_WIDTH ** -0.5, 0.125),
        "query_exit_maps": normal_values(key_list[13], (ADAPTER_COUNT, ADAPTER_RANK, QUERY_HEADS * HEAD_WIDTH), ADAPTER_RANK ** -0.5, 1.5),
        "key_value_exit_maps": normal_values(key_list[14], (2, ADAPTER_COUNT, ADAPTER_RANK, KEY_HEADS * HEAD_WIDTH), ADAPTER_RANK ** -0.5, 1.5),
        "output_entry_maps": normal_values(key_list[15], (QUERY_HEADS * HEAD_WIDTH, ADAPTER_COUNT, ADAPTER_RANK), (QUERY_HEADS * HEAD_WIDTH) ** -0.5, 0.125),
        "output_exit_maps": normal_values(key_list[16], (ADAPTER_COUNT, ADAPTER_RANK, MODEL_WIDTH), ADAPTER_RANK ** -0.5, 1.5),
        "feedforward_entry_maps": normal_values(key_list[17], (MODEL_WIDTH, ADAPTER_COUNT, 2 * ADAPTER_RANK), MODEL_WIDTH ** -0.5, 0.125),
        "feedforward_exit_maps": normal_values(key_list[18], (2, ADAPTER_COUNT, ADAPTER_RANK, HIDDEN_UNITS), ADAPTER_RANK ** -0.5, 1.5),
        "down_entry_maps": normal_values(key_list[19], (HIDDEN_UNITS, ADAPTER_COUNT, ADAPTER_RANK), HIDDEN_UNITS ** -0.5, 0.0625),
        "down_exit_maps": normal_values(key_list[20], (ADAPTER_COUNT, ADAPTER_RANK, MODEL_WIDTH), ADAPTER_RANK ** -0.5, 1.5),
        "cotangent": normal_values(key_list[21], (STREAMS, LEN, MODEL_WIDTH), 1.0, 6.0, ((0, 8), (1, 4))),
    }


HIGHEST_PREC = lax.Precision.HIGHEST
EPSILON = 1e-05
RESIDUAL_MULT = 0.22
SCORE_MULT = 0.015625
ROPE_BASE = 10000000.0
MASKED = -1e+30

@jax.custom_vjp
def low(v):
    return lax.optimization_barrier(v.astype(jnp.bfloat16)).astype(jnp.float32)

@jax.custom_vjp
def reduced_backward(v):
    return v

def low_keep(v):
    return (low(v), None)

def low_pass(kept, grad):
    return (grad,)

def back_keep(v):
    return (v, None)

def back_low(kept, grad):
    return (low(grad),)
low.defvjp(low_keep, low_pass)
reduced_backward.defvjp(back_keep, back_low)

def precise_product(left, right):
    return jnp.dot(left, right, precision=HIGHEST_PREC, preferred_element_type=jnp.float32)

def rms_norm(values, gain):
    return values * lax.rsqrt(lax.optimization_barrier(jnp.mean(values * values, axis=-1, keepdims=True)) + EPSILON) * gain

def rope_tables(positions, head_size):
    half_size = head_size // 2
    inv_freq = ROPE_BASE ** (-(jnp.arange(half_size).astype(jnp.float32) * 2.0) / head_size)
    angles = positions.astype(jnp.float32)[:, None] * inv_freq[None, :]
    return (jnp.cos(angles)[:, None, :], jnp.sin(angles)[:, None, :])

def rotate(values, cos_tab, sin_tab):
    half_size = values.shape[-1] // 2
    former = values[..., :half_size]
    latter = values[..., half_size:]
    return jnp.concatenate([former * cos_tab - latter * sin_tab, latter * cos_tab + former * sin_tab], axis=-1)

def rank_of_adapter(inputs, down_flat, choose_adapter, ranks):
    full_rank = precise_product(inputs, down_flat).reshape(inputs.shape[0], -1, ranks)
    return low(reduced_backward(full_rank * choose_adapter[:, :, None]))

def rank_columns(picked, lower, upper):
    return picked[:, :, lower:upper].reshape(picked.shape[0], -1)

def attention(query_projected, key_rows, value_rows, document_line):
    token_length = query_projected.shape[0]
    block_rows = min(512, token_length)
    per_kv = QUERY_HEADS // KEY_HEADS
    query_four = query_projected.reshape(token_length, KEY_HEADS, per_kv, HEAD_WIDTH)
    key_pos = jnp.arange(token_length)

    def one_block(first_row):
        query_rows = lax.dynamic_slice_in_dim(query_four, first_row, block_rows, 0)
        row_docs = lax.dynamic_slice_in_dim(document_line, first_row, block_rows, 0)
        row_pos = first_row + jnp.arange(block_rows)
        allowed = (row_docs[:, None] == document_line[None, :]) & (key_pos[None, :] <= row_pos[:, None])
        raw_scores = jnp.einsum('qkgd,skd->kgqs', query_rows, key_rows, precision=HIGHEST_PREC)
        logits = jnp.where(allowed[None, None], reduced_backward(SCORE_MULT * raw_scores), MASKED)
        row_max = lax.optimization_barrier(jnp.max(logits, axis=-1, keepdims=True))
        shifted = jnp.exp(logits - row_max)
        probs_low = low(shifted / lax.optimization_barrier(jnp.sum(shifted, axis=-1, keepdims=True)))
        mixed_rows = jnp.einsum('kgqs,skd->qkgd', probs_low, value_rows, precision=HIGHEST_PREC)
        return mixed_rows.reshape(block_rows, QUERY_HEADS * HEAD_WIDTH)
    starts = (jnp.arange(token_length // block_rows) * block_rows).astype(jnp.int32)
    return lax.map(jax.checkpoint(one_block), starts).reshape(token_length, QUERY_HEADS * HEAD_WIDTH)

def forward_layer(hidden_state, adapter_params, document_line, choose_adapter, frozen_weights):
    attention_norm_gain, feedforward_norm_gain, query_weight, key_weight, value_weight, output_weight, gate_weight, up_weight, down_weight = frozen_weights
    attention_down_maps, query_exit_maps, key_value_exit_maps, output_entry_maps, output_exit_maps, feedforward_entry_maps, feedforward_exit_maps, down_entry_maps, down_exit_maps = adapter_params
    token_length = hidden_state.shape[0]
    flattened_rank = ADAPTER_COUNT * ADAPTER_RANK
    cos_tab, sin_tab = rope_tables(jnp.arange(token_length), HEAD_WIDTH)
    first_normed = low(rms_norm(hidden_state, attention_norm_gain))
    selected_first = rank_of_adapter(first_normed, attention_down_maps.reshape(MODEL_WIDTH, -1), choose_adapter, 3 * ADAPTER_RANK)
    query_projected = precise_product(first_normed, query_weight) + precise_product(rank_columns(selected_first, 0, ADAPTER_RANK), query_exit_maps.reshape(flattened_rank, -1))
    key_projected = precise_product(first_normed, key_weight) + precise_product(rank_columns(selected_first, ADAPTER_RANK, 2 * ADAPTER_RANK), key_value_exit_maps[0].reshape(flattened_rank, -1))
    value_projected = precise_product(first_normed, value_weight) + precise_product(rank_columns(selected_first, 2 * ADAPTER_RANK, 3 * ADAPTER_RANK), key_value_exit_maps[1].reshape(flattened_rank, -1))
    query_rot = low(reduced_backward(rotate(reduced_backward(query_projected).reshape(token_length, QUERY_HEADS, HEAD_WIDTH), cos_tab, sin_tab)))
    key_rot = low(reduced_backward(rotate(reduced_backward(key_projected).reshape(token_length, KEY_HEADS, HEAD_WIDTH), cos_tab, sin_tab)))
    value_low = low(reduced_backward(value_projected.reshape(token_length, KEY_HEADS, HEAD_WIDTH)))
    attention_result = low(reduced_backward(attention(query_rot, key_rot, value_low, document_line)))
    selected_output = rank_of_adapter(attention_result, output_entry_maps.reshape(QUERY_HEADS * HEAD_WIDTH, -1), choose_adapter, ADAPTER_RANK)
    attention_path = reduced_backward(precise_product(attention_result, output_weight) + precise_product(selected_output.reshape(token_length, -1), output_exit_maps.reshape(flattened_rank, -1)))
    middle = hidden_state + RESIDUAL_MULT * attention_path
    second_normed = low(rms_norm(middle, feedforward_norm_gain))
    selected_second = rank_of_adapter(second_normed, feedforward_entry_maps.reshape(MODEL_WIDTH, -1), choose_adapter, 2 * ADAPTER_RANK)
    gate_activation = reduced_backward(precise_product(second_normed, gate_weight) + precise_product(rank_columns(selected_second, 0, ADAPTER_RANK), feedforward_exit_maps[0].reshape(flattened_rank, -1)))
    upward_activation = reduced_backward(precise_product(second_normed, up_weight) + precise_product(rank_columns(selected_second, ADAPTER_RANK, 2 * ADAPTER_RANK), feedforward_exit_maps[1].reshape(flattened_rank, -1)))
    combined_activation = low(gate_activation * jax.nn.sigmoid(gate_activation) * upward_activation)
    selected_down = rank_of_adapter(combined_activation, down_entry_maps.reshape(HIDDEN_UNITS, -1), choose_adapter, ADAPTER_RANK)
    feedforward_path = reduced_backward(precise_product(combined_activation, down_weight) + precise_product(selected_down.reshape(token_length, -1), down_exit_maps.reshape(flattened_rank, -1)))
    return middle + RESIDUAL_MULT * feedforward_path

def pairwise_add(former, latter):
    return former + latter

def reference(tokens, token_document, document_adapter, attention_norm_gain, feedforward_norm_gain, query_weight, key_weight, value_weight, output_weight, gate_weight, up_weight, down_weight, attention_down_maps, query_exit_maps, key_value_exit_maps, output_entry_maps, output_exit_maps, feedforward_entry_maps, feedforward_exit_maps, down_entry_maps, down_exit_maps, cotangent):
    frozen_weights = tuple((weight_argument.astype(jnp.float32) for weight_argument in (attention_norm_gain, feedforward_norm_gain, query_weight, key_weight, value_weight, output_weight, gate_weight, up_weight, down_weight)))
    adapter_params = tuple((weight_argument.astype(jnp.float32) for weight_argument in (attention_down_maps, query_exit_maps, key_value_exit_maps, output_entry_maps, output_exit_maps, feedforward_entry_maps, feedforward_exit_maps, down_entry_maps, down_exit_maps)))

    def per_stream(running_totals, stream):
        hidden_state, document_line, owners, output_gradient = stream
        owner_row = owners[document_line]
        choose_adapter = (owner_row[:, None] == jnp.arange(ADAPTER_COUNT)[None, :]).astype(jnp.float32)

        def execute_layer(hidden_input, adapter_input):
            return forward_layer(hidden_input, adapter_input, document_line, choose_adapter, frozen_weights)
        layer_result, backward_function = jax.vjp(execute_layer, hidden_state, adapter_params)
        hidden_gradient, adapter_gradient = backward_function(output_gradient)
        return (jax.tree.map(pairwise_add, running_totals, adapter_gradient), (layer_result.astype(jnp.bfloat16), hidden_gradient))
    zeroed_gradients = tuple((jnp.zeros(weight_argument.shape, jnp.float32) for weight_argument in adapter_params))
    running_totals, outputs = lax.scan(per_stream, zeroed_gradients, (tokens.astype(jnp.float32), token_document, document_adapter, cotangent.astype(jnp.float32)))
    layer_out, grad_tokens = outputs
    return (layer_out, grad_tokens, running_totals[0], running_totals[1], running_totals[2], running_totals[3], running_totals[4], running_totals[5], running_totals[6], running_totals[7], running_totals[8])
```

```python
import functools

import jax
import jax.numpy as jnp
from jax import lax
from jax.experimental import pallas as pl
from jax.experimental.pallas import tpu as pltpu
from jax.sharding import PartitionSpec as P

QUERY_HEADS = 32
KEY_HEADS = 8
HEAD_WIDTH = 64
LANES = 128
PACK = 512
TILE = 256

EPSILON = 1e-05
RESIDUAL_MULT = 0.22
SCORE_MULT = 0.015625
ROPE_BASE = 10000000.0
MASKED = -1e30

BF = jnp.bfloat16
F32 = jnp.float32

CORE_SWAP = [(s, s ^ 1) for s in range(4)]
Y_SWAP = [(s, s ^ 2) for s in range(4)]
X_SWAP = [(w, w ^ 1) for w in range(8)]


def z_shift(steps):
    return [(2 * z + x, 2 * ((z + steps) % 4) + x) for z in range(4) for x in range(2)]


def low_dot(left, right):
    return jnp.dot(left, right, preferred_element_type=F32)


def gradient_product(left, right):
    return lax.dot_general(left, right, (((0,), (0,)), ((), ())), preferred_element_type=F32)


def reverse_product(left, right):
    return lax.dot_general(left, right, (((1,), (1,)), ((), ())), preferred_element_type=F32)


def normed(values, gain):
    norm_scale = lax.rsqrt(jnp.mean(values * values, axis=-1, keepdims=True) + EPSILON)
    return (values * norm_scale * gain, norm_scale)


def normed_back(values, norm_scale, gain, grad_in):
    scaled = grad_in * gain
    cubed = norm_scale * norm_scale * norm_scale
    return norm_scale * scaled - values * cubed * jnp.mean(scaled * values, axis=-1, keepdims=True)


def rope_tables(positions, head_size):
    half_size = head_size // 2
    inv_freq = ROPE_BASE ** (-(jnp.arange(half_size).astype(F32) * 2.0) / head_size)
    angles = positions.astype(F32)[:, None] * inv_freq[None, :]
    return (jnp.cos(angles)[:, None, :], jnp.sin(angles)[:, None, :])


def rotate(values, cos_tab, sin_tab):
    half_size = values.shape[-1] // 2
    former = values[..., :half_size]
    latter = values[..., half_size:]
    return jnp.concatenate(
        [former * cos_tab - latter * sin_tab, latter * cos_tab + former * sin_tab], axis=-1
    )


def cut(values, start, size, axis):
    return lax.dynamic_slice_in_dim(values, start, size, axis)


def pick(values, index, axis):
    return lax.dynamic_index_in_dim(values, index, axis, keepdims=False)


def adapter_mask(owner, ranks, adapters):
    lane = jnp.arange(adapters * ranks, dtype=jnp.int32) // ranks
    return (owner[:, None] == lane[None, :]).astype(F32)


def fold(masked, ranks, offset):
    rows = jnp.arange(masked.shape[1], dtype=jnp.int32) % ranks
    lanes = jnp.arange(LANES, dtype=jnp.int32) - offset
    return low_dot(masked.astype(BF), (rows[:, None] == lanes[None, :]).astype(BF))


def spread(folded, owner, ranks, offset, adapters):
    rows = jnp.arange(LANES, dtype=jnp.int32) - offset
    lanes = jnp.arange(adapters * ranks, dtype=jnp.int32) % ranks
    wide = low_dot(folded.astype(BF), (rows[:, None] == lanes[None, :]).astype(BF))
    return (wide * adapter_mask(owner, ranks, adapters)).astype(BF)


def pack(values):
    parts = [values[:, i : i + PACK] for i in range(0, values.shape[1], PACK)]
    return jnp.concatenate(parts, axis=0)


class Mover:
    def __init__(self, seq_size, wsh_size):
        self.seq_size, self.wsh_size = seq_size, wsh_size
        self.fast = seq_size == 4 and wsh_size == 8
        self.s, self.w = lax.axis_index("seq"), lax.axis_index("wsh")
        self.y, self.c = self.s // 2, self.s % 2
        self.z, self.x = self.w // 2, self.w % 2
        self.lanes = {"x": [], "y": [], "z": []}
        self.depth = 6

    def send(self, values, axis, pairs, lane, depth=2):
        sent = self.lanes[lane]
        if len(sent) >= depth:
            values, _ = lax.optimization_barrier((values, sent[-depth]))
        result = lax.ppermute(values, axis, pairs)
        sent.append(result)
        return result

    def gather_rows(self, chunk):
        if not self.fast:
            return lax.all_gather(chunk, "wsh", axis=0, tiled=True)
        slots = []
        for r in range(4):
            held = chunk
            if r:
                held = self.send(chunk, "wsh", z_shift(r), "z", self.depth)
            slots += [held, self.send(held, "wsh", X_SWAP, "x", self.depth)]
        return jnp.concatenate(slots, axis=0)

    def slot_owner(self, k):
        if not self.fast:
            return k
        return 2 * ((self.z - k // 2) % 4) + (self.x ^ (k % 2))

    def slot_of(self, w):
        if not self.fast:
            return w
        return 2 * ((self.z - w // 2) % 4) + (self.x ^ (w % 2))

    def to_slots(self, values, block):
        if not self.fast:
            return values
        parts = [cut(values, self.slot_owner(k) * block, block, 1) for k in range(self.wsh_size)]
        return jnp.concatenate(parts, axis=1)

    def from_slots(self, values, block):
        if not self.fast:
            return values
        parts = [cut(values, self.slot_of(w) * block, block, 1) for w in range(self.wsh_size)]
        return jnp.concatenate(parts, axis=1)

    def head_rows(self, weight):
        rows = weight.shape[0]
        per = self.wsh_size // self.seq_size
        if not self.fast:
            return cut(
                lax.all_gather(weight, "wsh", axis=0, tiled=True),
                self.s * per * rows,
                per * rows,
                0,
            )
        piece = rows // 4
        mine = jnp.where(self.z == self.s, cut(weight, self.z * piece, piece, 0), 0)
        for r in range(1, 4):
            pairs = [
                (8 * s + 2 * s + x, 8 * s + 2 * ((s + r) % 4) + x)
                for s in range(4)
                for x in range(2)
            ]
            out = cut(weight, ((self.z + r) % 4) * piece, piece, 0)
            mine = mine + self.send(out, ("seq", "wsh"), pairs, "z", self.depth)
        return mine

    def head_rows_done(self, slots, rows):
        if not self.fast:
            return slots
        piece = rows // 4
        blocks = slots.reshape(4, 2, piece, slots.shape[1])
        out = []
        for shard in range(2):
            for j in range(4):
                one = pick(blocks, (self.z - j) % 4, 0)
                out.append(pick(one, self.x ^ shard, 0))
        return jnp.concatenate(out, axis=0)

    def gather_tokens(self, values):
        if not self.fast:
            return lax.all_gather(values, "seq", axis=0, tiled=True)
        other = self.send(values, "seq", Y_SWAP, "y")
        first = self.y == 0
        column = jnp.stack([jnp.where(first, values, other), jnp.where(first, other, values)])
        partner = lax.ppermute(column, "seq", CORE_SWAP)
        first = self.c == 0
        whole = jnp.stack(
            [jnp.where(first, column, partner), jnp.where(first, partner, column)], axis=1
        )
        return whole.reshape((4 * values.shape[0],) + values.shape[1:])

    def scatter_tokens(self, *partials):
        if not self.fast:
            return [
                lax.psum_scatter(v.astype(BF), "seq", scatter_dimension=0, tiled=True).astype(F32)
                for v in partials
            ]
        rows = partials[0].shape[0] // 4
        blocks = [v.reshape(2, 2, rows, v.shape[1]) for v in partials]
        out = jnp.concatenate([pick(v, 1 - self.c, 1).astype(BF) for v in blocks], axis=2)
        got = lax.ppermute(out, "seq", CORE_SWAP).astype(F32)
        mine = jnp.concatenate([pick(v, self.c, 1) for v in blocks], axis=2)
        away = (pick(mine, 1 - self.y, 0) + pick(got, 1 - self.y, 0)).astype(BF)
        other = self.send(away, "seq", Y_SWAP, "y").astype(F32)
        total = pick(mine, self.y, 0) + pick(got, self.y, 0) + other
        found, at = [], 0
        for v in partials:
            found.append(total[:, at : at + v.shape[1]])
            at += v.shape[1]
        return found

    def sum_small(self, partial):
        if not self.fast:
            return lax.psum(partial, "seq")
        total = partial.astype(F32) + lax.ppermute(partial, "seq", CORE_SWAP).astype(F32)
        other = self.send(total.astype(BF), "seq", Y_SWAP, "y")
        return total + other.astype(F32)

    def sum_plain(self, grad):
        total = lax.psum(grad.astype(BF), "wsh")
        return lax.all_gather(total.astype(BF), "seq", axis=0).astype(F32)

    def sum_hidden(self, grads, hid_block):
        if not self.fast:
            found = []
            for grad in grads:
                rows = grad.shape[0]
                wide = self.sum_plain(grad).reshape(self.seq_size, rows, self.wsh_size, hid_block)
                found.append(wide.transpose(1, 2, 0, 3).reshape(rows, -1))
            return [jnp.stack(found[:2]), found[2]]
        parts = self.sum_gather(jnp.concatenate([pack(v) for v in grads], axis=0))
        s = self.s.astype(jnp.int32)[None]
        return [
            final_hidden(parts, s, 0, 2),
            final_hidden(parts, s, 8 * LANES, 1)[0],
        ]

    def sum_features(self, grads, key=None, value=None):
        if not self.fast:
            grads = grads + ([key, value] if key is not None else [])
            found = []
            for grad in grads:
                found.append(self.sum_plain(grad).transpose(1, 0, 2).reshape(grad.shape[0], -1))
            return found[:-2] + [jnp.stack(found[-2:])] if key is not None else found
        packed = list(grads)
        if key is not None:
            rest = jnp.zeros((key.shape[0], PACK - 2 * LANES), F32)
            packed.append(jnp.concatenate([key, value, rest], axis=1))
        parts = self.sum_gather(jnp.concatenate(packed, axis=0))
        s = self.s.astype(jnp.int32)[None]
        found, at = [], 0
        for grad in grads:
            found.append(final_features(parts, s, at, grad.shape[0]))
            at += grad.shape[0]
        if key is not None:
            found.append(final_kv(parts, s, at))
        return found

    def sum_gather(self, packed):
        rows = packed.shape[0]
        halves = packed.reshape(2, rows // 2, PACK)
        got = self.send(pick(halves, 1 - self.x, 0).astype(BF), "wsh", X_SWAP, "x")
        half = pick(halves, self.x, 0) + got.astype(F32)
        blocks = half.reshape(4, rows // 8, PACK)
        total = pick(blocks, self.z, 0)
        for r in range(1, 4):
            out = pick(blocks, (self.z + r) % 4, 0).astype(BF)
            total = total + self.send(out, "wsh", z_shift(r), "z", 3).astype(F32)
        own = total.astype(BF)
        got = [own] + [self.send(own, "wsh", z_shift(r), "z", 3) for r in range(1, 4)]
        ring = jnp.stack(got)
        half = jnp.concatenate([pick(ring, (self.z - j) % 4, 0) for j in range(4)], axis=0)
        other = self.send(half, "wsh", X_SWAP, "x")
        first = self.x == 0
        part = jnp.concatenate([jnp.where(first, half, other), jnp.where(first, other, half)])
        core = lax.ppermute(part, "seq", CORE_SWAP)
        other = self.send(part, "seq", Y_SWAP, "y")
        return part, core, other, lax.ppermute(other, "seq", CORE_SWAP)


def choose_part(s_ref, parts, out_ref, axis):
    k = s_ref[0] ^ pl.program_id(axis)
    low = jnp.where(k % 2 == 0, parts[0][...], parts[1][...])
    high = jnp.where(k % 2 == 0, parts[2][...], parts[3][...])
    value = jnp.where(k < 2, low, high).astype(F32)
    out_ref[...] = value.reshape(out_ref.shape)


def final_call(parts, s, grid, part_block, part_map, out_shape, out_block, out_map):
    def body(s_ref, a, b, c, d, out_ref):
        choose_part(s_ref, (a, b, c, d), out_ref, len(grid) - 1)

    return pl.pallas_call(
        body,
        grid_spec=pltpu.PrefetchScalarGridSpec(
            num_scalar_prefetch=1,
            grid=grid,
            in_specs=[pl.BlockSpec(part_block, part_map)] * 4,
            out_specs=pl.BlockSpec(out_block, out_map),
        ),
        out_shape=jax.ShapeDtypeStruct(out_shape, F32),
        name="finish",
    )(s, *parts)


def final_features(parts, s, row, rows):
    at = row // LANES
    return final_call(
        parts,
        s,
        (rows // LANES, 4),
        (LANES, PACK),
        lambda i, j, _: (at + i, 0),
        (rows, 4 * PACK),
        (LANES, PACK),
        lambda i, j, _: (i, j),
    )


def final_hidden(parts, s, row, count):
    at = row // LANES
    return final_call(
        parts,
        s,
        (count, 8, 4),
        (LANES, TILE),
        lambda n, w, j, _: (at + 4 * n + w // 2, w % 2),
        (count, LANES, 32 * TILE),
        (1, LANES, TILE),
        lambda n, w, j, _: (n, 0, 4 * w + j),
    )


def final_kv(parts, s, row):
    at = row // LANES
    return final_call(
        parts,
        s,
        (2, 4),
        (LANES, LANES),
        lambda n, j, _: (at, n),
        (2, LANES, 4 * LANES),
        (1, LANES, LANES),
        lambda n, j, _: (n, 0, j),
    )


def half_lanes(rows, half):
    lane = lax.broadcasted_iota(jnp.int32, (rows, LANES), 1)
    return (lane < HEAD_WIDTH) if half == 0 else (lane >= HEAD_WIDTH)


def turn(values, cos_tab, sin_tab):
    lane = lax.broadcasted_iota(jnp.int32, values.shape, 1)
    swapped = jnp.where(
        lane % HEAD_WIDTH < HEAD_WIDTH // 2,
        pltpu.roll(values, LANES - HEAD_WIDTH // 2, 1),
        pltpu.roll(values, HEAD_WIDTH // 2, 1),
    )
    return values * cos_tab + swapped * sin_tab


def twice(values, half):
    other = pltpu.roll(values, HEAD_WIDTH, 1)
    first = half_lanes(values.shape[0], 0)
    return jnp.where(first, values, other) if half == 0 else jnp.where(first, other, values)


def qkv_body(x_ref, w_ref, la_q, la_k, la_v, exit_q, exit_kv, cos_ref, sin_ref, q_ref, k_ref, v_ref):
    cos_tab, sin_tab = cos_ref[...], sin_ref[...]
    product = low_dot(x_ref[...], w_ref[...])
    q_cols = q_ref.shape[1]
    query = product[:, :q_cols] + low_dot(la_q[...], exit_q[...])
    for i in range(0, q_cols, LANES):
        q_ref[:, i : i + LANES] = turn(query[:, i : i + LANES], cos_tab, sin_tab).astype(BF)
    key = product[:, q_cols : q_cols + LANES] + low_dot(la_k[...], exit_kv[0])
    key = turn(key, cos_tab, sin_tab)
    value = product[:, q_cols + LANES :] + low_dot(la_v[...], exit_kv[1])
    for half in range(2):
        k_ref[:, half * LANES : (half + 1) * LANES] = twice(key, half).astype(BF)
        v_ref[:, half * LANES : (half + 1) * LANES] = twice(value, half).astype(BF)


def qkv_call(x, weights, la_q, la_k, la_v, exit_q, exit_kv, cos_tab, sin_tab):
    rows, width = x.shape[0], weights.shape[0]
    q_cols = exit_q.shape[1]

    def tile(columns):
        return pl.BlockSpec((TILE, columns), lambda i: (i, 0))

    return pl.pallas_call(
        qkv_body,
        grid=(rows // TILE,),
        in_specs=[
            tile(width),
            pl.BlockSpec(weights.shape, lambda i: (0, 0)),
            tile(LANES),
            tile(LANES),
            tile(LANES),
            pl.BlockSpec(exit_q.shape, lambda i: (0, 0)),
            pl.BlockSpec(exit_kv.shape, lambda i: (0, 0, 0)),
            tile(LANES),
            tile(LANES),
        ],
        out_specs=[tile(q_cols), tile(2 * LANES), tile(2 * LANES)],
        out_shape=[
            jax.ShapeDtypeStruct((rows, q_cols), BF),
            jax.ShapeDtypeStruct((rows, 2 * LANES), BF),
            jax.ShapeDtypeStruct((rows, 2 * LANES), BF),
        ],
        name="qkv",
        cost_estimate=pl.CostEstimate(
            flops=2 * rows * width * weights.shape[1], bytes_accessed=12 << 20, transcendentals=0
        ),
    )(x, weights, la_q, la_k, la_v, exit_q, exit_kv, cos_tab, sin_tab)


def allowed_pairs(i, t, doc_col, doc_row):
    start = pl.multiple_of(t * TILE, TILE)
    rows = i * TILE + lax.broadcasted_iota(jnp.int32, (TILE, TILE), 0)
    keys = start + lax.broadcasted_iota(jnp.int32, (TILE, TILE), 1)
    return (doc_col[...] == doc_row[:, pl.ds(start, TILE)]) & (keys <= rows)


def forward_body(first_ref, q_ref, k_ref, v_ref, doc_col, doc_row, o_ref, lse_ref, m_s, l_s, acc_s):
    i = pl.program_id(1)
    m_s[...] = jnp.full_like(m_s, MASKED)
    l_s[...] = jnp.zeros_like(l_s)
    acc_s[...] = jnp.zeros_like(acc_s)

    def step(t, carry):
        allowed = allowed_pairs(i, t, doc_col, doc_row)
        start = pl.multiple_of(t * TILE, TILE)
        keys, vals = k_ref[pl.ds(start, TILE), :], v_ref[pl.ds(start, TILE), :]
        for h in range(4):
            pair = q_ref[:, (h // 2) * LANES : (h // 2 + 1) * LANES]
            query = jnp.where(half_lanes(TILE, h % 2), pair, jnp.zeros_like(pair))
            logits = jnp.where(allowed, SCORE_MULT * reverse_product(query, keys), MASKED)
            old = m_s[h]
            top = jnp.maximum(old, jnp.max(logits, axis=1, keepdims=True))
            shrink = jnp.exp(old - top)
            shifted = jnp.exp(logits - top)
            m_s[h] = top
            l_s[h] = l_s[h] * shrink + jnp.sum(shifted, axis=1, keepdims=True)
            acc_s[h] = acc_s[h] * shrink + low_dot(shifted.astype(BF), vals)
        return carry

    lax.fori_loop(first_ref[i], i + 1, step, 0)
    lane = lax.broadcasted_iota(jnp.int32, (TILE, LANES), 1)
    total = jnp.zeros((TILE, LANES), F32)
    for p in range(2):
        both = [acc_s[2 * p + n] / l_s[2 * p + n] for n in range(2)]
        o_ref[:, p * LANES : (p + 1) * LANES] = jnp.where(
            half_lanes(TILE, 0), both[0], both[1]
        ).astype(BF)
    for h in range(4):
        total = jnp.where(lane == h, m_s[h] + jnp.log(l_s[h]), total)
    lse_ref[...] = total


def attention_call(first, query, keys, values, doc_col, doc_row):
    rows = query.shape[0]
    group = query.shape[1] // 2
    return pl.pallas_call(
        forward_body,
        grid_spec=pltpu.PrefetchScalarGridSpec(
            num_scalar_prefetch=1,
            grid=(2, rows // TILE),
            in_specs=[
                pl.BlockSpec((TILE, group), lambda j, i, _: (i, j)),
                pl.BlockSpec((rows, LANES), lambda j, i, _: (0, j)),
                pl.BlockSpec((rows, LANES), lambda j, i, _: (0, j)),
                pl.BlockSpec((TILE, 1), lambda j, i, _: (i, 0)),
                pl.BlockSpec((1, rows), lambda j, i, _: (0, 0)),
            ],
            out_specs=[
                pl.BlockSpec((TILE, group), lambda j, i, _: (i, j)),
                pl.BlockSpec((TILE, LANES), lambda j, i, _: (i, j)),
            ],
            scratch_shapes=[
                pltpu.VMEM((4, TILE, 1), F32),
                pltpu.VMEM((4, TILE, 1), F32),
                pltpu.VMEM((4, TILE, LANES), F32),
            ],
        ),
        out_shape=[
            jax.ShapeDtypeStruct(query.shape, BF),
            jax.ShapeDtypeStruct((rows, 2 * LANES), F32),
        ],
        name="attention",
        cost_estimate=pl.CostEstimate(
            flops=8 * 4 * rows * rows * LANES,
            bytes_accessed=6 << 20,
            transcendentals=8 * rows * rows,
        ),
    )(first, query, keys, values, doc_col, doc_row)


def backward_body(
    first_ref, q_ref, k_ref, v_ref, do_ref, o_ref, lse_ref, doc_col, doc_row, cos_ref, sin_ref,
    cos_all, sin_all, dq_ref, dk_ref, dv_ref, dq_s, dk_s, dv_s,
):
    i = pl.program_id(1)

    @pl.when(i == 0)
    def _():
        dk_s[...] = jnp.zeros_like(dk_s)
        dv_s[...] = jnp.zeros_like(dv_s)

    dq_s[...] = jnp.zeros_like(dq_s)
    queries, grads, deltas = [], [], []
    for h in range(4):
        at = slice((h // 2) * LANES, (h // 2 + 1) * LANES)
        half = half_lanes(TILE, h % 2)
        pair, grad = q_ref[:, at], do_ref[:, at]
        queries.append(jnp.where(half, pair, jnp.zeros_like(pair)))
        grads.append(jnp.where(half, grad, jnp.zeros_like(grad)))
        product = grads[h].astype(F32) * o_ref[:, at].astype(F32)
        deltas.append(jnp.sum(product, axis=1, keepdims=True))

    def step(t, carry):
        allowed = allowed_pairs(i, t, doc_col, doc_row)
        start = pl.multiple_of(t * TILE, TILE)
        at = pl.ds(start, TILE)
        keys, vals = k_ref[at, :], v_ref[at, :]
        dk, dv = dk_s[at, :], dv_s[at, :]
        for h in range(4):
            logits = jnp.where(allowed, SCORE_MULT * reverse_product(queries[h], keys), MASKED)
            probs = jnp.exp(logits - lse_ref[:, h : h + 1])
            d_probs = reverse_product(grads[h], vals)
            d_logits = (probs * (d_probs - deltas[h])).astype(BF)
            dq_s[h] = dq_s[h] + low_dot(d_logits, keys)
            dk = dk + gradient_product(d_logits, queries[h])
            dv = dv + gradient_product(probs.astype(BF), grads[h])
        dk_s[at, :] = dk
        dv_s[at, :] = dv
        return carry

    lax.fori_loop(first_ref[i], i + 1, step, 0)
    for p in range(2):
        both = jnp.where(half_lanes(TILE, 0), dq_s[2 * p], dq_s[2 * p + 1])
        both = (SCORE_MULT * both).astype(BF).astype(F32)
        dq_ref[:, p * LANES : (p + 1) * LANES] = turn(both, cos_ref[...], -sin_ref[...]).astype(BF)

    @pl.when(i == pl.num_programs(1) - 1)
    def _():
        def finish(t, carry):
            at = pl.ds(pl.multiple_of(t * TILE, TILE), TILE)
            dk, dv = dk_s[at, :], dv_s[at, :]
            dk = (SCORE_MULT * (dk + pltpu.roll(dk, HEAD_WIDTH, 1))).astype(BF).astype(F32)
            dk_ref[at, :] = turn(dk, cos_all[at, :], -sin_all[at, :]).astype(BF)
            dv_ref[at, :] = (dv + pltpu.roll(dv, HEAD_WIDTH, 1)).astype(BF)
            return carry

        lax.fori_loop(0, pl.num_programs(1), finish, 0)


def attention_back_call(
    first, query, keys, values, d_out, out, lse, doc_col, doc_row, cos_tab, sin_tab
):
    rows = query.shape[0]
    group = query.shape[1] // 2
    whole = pl.BlockSpec((rows, LANES), lambda j, i, _: (0, j))
    tile = pl.BlockSpec((TILE, group), lambda j, i, _: (i, j))
    table = pl.BlockSpec((TILE, LANES), lambda j, i, _: (i, 0))
    table_all = pl.BlockSpec((rows, LANES), lambda j, i, _: (0, 0))
    return pl.pallas_call(
        backward_body,
        grid_spec=pltpu.PrefetchScalarGridSpec(
            num_scalar_prefetch=1,
            grid=(2, rows // TILE),
            in_specs=[
                tile,
                whole,
                whole,
                tile,
                tile,
                pl.BlockSpec((TILE, LANES), lambda j, i, _: (i, j)),
                pl.BlockSpec((TILE, 1), lambda j, i, _: (i, 0)),
                pl.BlockSpec((1, rows), lambda j, i, _: (0, 0)),
                table,
                table,
                table_all,
                table_all,
            ],
            out_specs=[tile, whole, whole],
            scratch_shapes=[
                pltpu.VMEM((4, TILE, LANES), F32),
                pltpu.VMEM((rows, LANES), F32),
                pltpu.VMEM((rows, LANES), F32),
            ],
        ),
        out_shape=[
            jax.ShapeDtypeStruct(query.shape, BF),
            jax.ShapeDtypeStruct((rows, 2 * LANES), BF),
            jax.ShapeDtypeStruct((rows, 2 * LANES), BF),
        ],
        name="attention_back",
        cost_estimate=pl.CostEstimate(
            flops=8 * 10 * rows * rows * LANES,
            bytes_accessed=10 << 20,
            transcendentals=8 * rows * rows,
        ),
    )(first, query, keys, values, d_out, out, lse, doc_col, doc_row, cos_tab, sin_tab, cos_tab, sin_tab)


def fast_attention(x, weights, la_q, la_k, la_v, exit_q, exit_k, exit_v, document_line):
    rows = x.shape[0]
    half = HEAD_WIDTH // 2
    cos_tab, sin_tab = rope_tables(jnp.arange(rows, dtype=jnp.int32), HEAD_WIDTH)
    cos_tab = jnp.tile(cos_tab.reshape(rows, half), (1, 4))
    sin_tab = sin_tab.reshape(rows, half)
    sin_tab = jnp.tile(jnp.concatenate([-sin_tab, sin_tab], axis=1), (1, 2))
    first_docs = document_line[::TILE]
    first = jnp.sum((document_line[None, :] < first_docs[:, None]).astype(jnp.int32), axis=1)
    first = first // TILE
    doc_col, doc_row = document_line[:, None], document_line[None, :]
    query, keys, values = qkv_call(
        x, weights, la_q, la_k, la_v, exit_q, jnp.stack([exit_k, exit_v]), cos_tab, sin_tab
    )
    attended, lse = attention_call(first, query, keys, values, doc_col, doc_row)

    def backward(d_heads):
        d_query, d_keys, d_values = attention_back_call(
            first, query, keys, values, d_heads, attended, lse, doc_col, doc_row, cos_tab, sin_tab
        )
        lane = jnp.arange(LANES, dtype=jnp.int32)[None, :] < HEAD_WIDTH
        d_key = jnp.where(lane, d_keys[:, :LANES], d_keys[:, LANES:])
        d_value = jnp.where(lane, d_values[:, :LANES], d_values[:, LANES:])
        return d_query, d_key, d_value

    return attended, backward


def attention_forward(query_heads, key_heads, value_heads, document_line):
    token_length = query_heads.shape[0]
    kv_dev = key_heads.shape[1] // HEAD_WIDTH
    per_kv = query_heads.shape[1] // key_heads.shape[1]
    block_rows = min(512, token_length)
    query_four = query_heads.reshape(token_length, kv_dev, per_kv, HEAD_WIDTH)
    key_three = key_heads.reshape(token_length, kv_dev, HEAD_WIDTH)
    value_three = value_heads.reshape(token_length, kv_dev, HEAD_WIDTH)
    key_pos = jnp.arange(token_length, dtype=jnp.int32)

    def scores_of(first_row):
        query_rows = lax.dynamic_slice_in_dim(query_four, first_row, block_rows, 0)
        row_docs = lax.dynamic_slice_in_dim(document_line, first_row, block_rows, 0)
        row_pos = first_row + jnp.arange(block_rows, dtype=jnp.int32)
        allowed = (row_docs[:, None] == document_line[None, :]) & (
            key_pos[None, :] <= row_pos[:, None]
        )
        raw_scores = jnp.einsum(
            "qkgd,skd->kgqs", query_rows, key_three, preferred_element_type=F32
        )
        return (jnp.where(allowed[None, None], SCORE_MULT * raw_scores, MASKED), query_rows)

    def forward_block(running_totals, block_index):
        logits, query_rows = scores_of(block_index * block_rows)
        row_max = jnp.max(logits, axis=-1, keepdims=True)
        shifted = jnp.exp(logits - row_max)
        row_sum = jnp.sum(shifted, axis=-1, keepdims=True)
        probs_low = (shifted / row_sum).astype(BF)
        mixed_rows = jnp.einsum(
            "kgqs,skd->qkgd", probs_low, value_three, preferred_element_type=F32
        )
        log_total = row_max[..., 0] + jnp.log(row_sum[..., 0])
        return (running_totals, (mixed_rows.reshape(block_rows, -1).astype(BF), log_total))

    block_ids = jnp.arange(token_length // block_rows, dtype=jnp.int32)
    _, (attn_blocks, log_totals) = lax.scan(forward_block, 0, block_ids)

    def backward(d_heads):
        d_heads_four = d_heads.reshape(token_length, kv_dev, per_kv, HEAD_WIDTH)

        def backward_block(running_totals, block_items):
            d_key_sum, d_value_sum = running_totals
            block_index, log_total = block_items
            first_row = block_index * block_rows
            logits, query_rows = scores_of(first_row)
            probs = jnp.exp(logits - log_total[..., None])
            d_rows = lax.dynamic_slice_in_dim(d_heads_four, first_row, block_rows, 0)
            d_probs = jnp.einsum(
                "qkgd,skd->kgqs", d_rows, value_three, preferred_element_type=F32
            )
            inner = jnp.sum(probs * d_probs, axis=-1, keepdims=True)
            d_logits = (probs * (d_probs - inner)).astype(BF)
            d_query_rows = SCORE_MULT * jnp.einsum(
                "kgqs,skd->qkgd", d_logits, key_three, preferred_element_type=F32
            )
            d_key_sum = d_key_sum + SCORE_MULT * jnp.einsum(
                "kgqs,qkgd->skd", d_logits, query_rows, preferred_element_type=F32
            )
            d_value_sum = d_value_sum + jnp.einsum(
                "kgqs,qkgd->skd", probs.astype(BF), d_rows, preferred_element_type=F32
            )
            return (
                (d_key_sum, d_value_sum),
                d_query_rows.astype(BF).reshape(block_rows, -1),
            )

        zero_keys = jnp.zeros((token_length, kv_dev, HEAD_WIDTH), F32)
        (d_key_sum, d_value_sum), d_query_blocks = lax.scan(
            backward_block, (zero_keys, zero_keys), (block_ids, log_totals)
        )
        return (
            d_query_blocks.reshape(token_length, -1),
            d_key_sum.astype(BF).reshape(token_length, -1),
            d_value_sum.astype(BF).reshape(token_length, -1),
        )

    return attn_blocks.reshape(token_length, -1), backward


def rope(values, cos_tab, sin_tab):
    rows, width = values.shape
    heads = values.astype(F32).reshape(rows, width // HEAD_WIDTH, HEAD_WIDTH)
    return rotate(heads, cos_tab, sin_tab).astype(BF).reshape(rows, width)


def plain_attention(x, weights, la_q, la_k, la_v, exit_q, exit_k, exit_v, document_line):
    rows = x.shape[0]
    q_cols, kv_cols = exit_q.shape[1], exit_k.shape[1]
    projected = low_dot(x, weights)
    cos_tab, sin_tab = rope_tables(jnp.arange(rows, dtype=jnp.int32), HEAD_WIDTH)
    query_rot = rope(projected[:, :q_cols] + low_dot(la_q, exit_q), cos_tab, sin_tab)
    key_rot = rope(
        projected[:, q_cols : q_cols + kv_cols] + low_dot(la_k, exit_k), cos_tab, sin_tab
    )
    value_low = (projected[:, q_cols + kv_cols :] + low_dot(la_v, exit_v)).astype(BF)
    attended, attention_back = attention_forward(query_rot, key_rot, value_low, document_line)

    def backward(d_heads):
        d_query, d_key, d_value = attention_back(d_heads)
        return rope(d_query, cos_tab, -sin_tab), rope(d_key, cos_tab, -sin_tab), d_value

    return attended, backward


def layer(mover, args):
    (
        tokens,
        token_document,
        document_adapter,
        attention_norm_gain,
        feedforward_norm_gain,
        query_weight,
        key_weight,
        value_weight,
        output_weight,
        gate_weight,
        up_weight,
        down_weight,
        attention_down_maps,
        query_exit_maps,
        key_value_exit_maps,
        output_entry_maps,
        output_exit_maps,
        feedforward_entry_maps,
        feedforward_exit_maps,
        down_entry_maps,
        down_exit_maps,
        cotangent,
    ) = args
    seq_size, wsh_size, s = mover.seq_size, mover.wsh_size, mover.s
    own_rows = tokens.shape[1]
    width = tokens.shape[2]
    adapters = attention_down_maps.shape[1]
    rank = query_exit_maps.shape[1]
    flat = adapters * rank
    doc_count = document_adapter.shape[1]
    q_cols = query_weight.shape[1] // seq_size
    kv_cols = key_weight.shape[1] // seq_size
    feature = width // seq_size
    row_block = width // wsh_size
    hidden = gate_weight.shape[1]
    hid_block = hidden // (wsh_size * seq_size)
    hid_own = hidden // seq_size

    def owners(docs):
        hot = (docs[:, None] == jnp.arange(doc_count, dtype=jnp.int32)[None, :]).astype(jnp.int32)
        return jnp.sum(hot * document_adapter[0][None, :], axis=1)

    def turned(maps):
        return maps.transpose(1, 2, 0).reshape(-1, maps.shape[0])

    def own_hidden(values, lower=0, upper=hid_own):
        parts, at = [], lower
        while at < upper:
            w = at // hid_block
            stop = min(upper, (w + 1) * hid_block)
            start = (w * seq_size + s) * hid_block + at - w * hid_block
            parts.append(cut(values, start, stop - at, 1))
            at = stop
        return parts

    qkv_local = jnp.concatenate(
        [
            cut(query_weight, s * q_cols, q_cols, 1),
            cut(key_weight, s * kv_cols, kv_cols, 1),
            cut(value_weight, s * kv_cols, kv_cols, 1),
        ],
        axis=1,
    )
    qkv_full = mover.gather_rows(qkv_local)
    local_docs = token_document[0]
    own_owner = owners(local_docs)
    hidden_state = tokens[0].astype(F32)
    first_normed, scale_one = normed(hidden_state, attention_norm_gain)
    first_normed = first_normed.astype(BF)
    input_maps = turned(attention_down_maps)
    picked_first = reverse_product(first_normed, input_maps)
    picked_first = picked_first * adapter_mask(own_owner, 3 * rank, adapters)
    picked_first = fold(picked_first, 3 * rank, 0).astype(BF)
    first_all = mover.gather_tokens(
        jnp.concatenate([mover.to_slots(first_normed, row_block), picked_first], axis=1)
    )
    document_line = mover.gather_tokens(local_docs[None, :].T)[:, 0]
    owner = owners(document_line)
    mask_rank = adapter_mask(owner, rank, adapters)
    output_gradient = cotangent[0].astype(F32)
    d_mlp_local = (RESIDUAL_MULT * output_gradient).astype(BF)
    d_mlp = mover.gather_tokens(d_mlp_local)

    half_width = width // 2
    down_local = cut(down_weight, s * hid_block, hid_block, 0)
    chunk = hid_own // 4
    chunk_bounds = [(0, chunk), (chunk, 2 * chunk), (2 * chunk, 3 * chunk)]
    chunk_bounds += [(3 * chunk, 7 * chunk // 2), (7 * chunk // 2, 4 * chunk)]

    def gate_up(lower, upper):
        return jnp.concatenate(
            own_hidden(gate_weight, lower, upper) + own_hidden(up_weight, lower, upper), axis=1
        )

    out_piece = mover.head_rows(output_weight)
    down_low = mover.gather_rows(down_local[:, :half_width])
    if mover.fast:
        out_full = mover.head_rows_done(mover.gather_rows(out_piece), output_weight.shape[0])
    else:
        out_full = out_piece
    down_high = mover.gather_rows(down_local[:, half_width:])
    chunk_weights = [mover.gather_rows(gate_up(*bounds)) for bounds in chunk_bounds]

    query_exit = cut(query_exit_maps.reshape(flat, -1), s * q_cols, q_cols, 1)
    key_exit = cut(key_value_exit_maps[0].reshape(flat, -1), s * kv_cols, kv_cols, 1)
    value_exit = cut(key_value_exit_maps[1].reshape(flat, -1), s * kv_cols, kv_cols, 1)
    first_slots = first_all[:, :width]
    la_one = first_all[:, width:]
    la_q = spread(la_one, owner, rank, 0, adapters)
    la_k = spread(la_one, owner, rank, rank, adapters)
    la_v = spread(la_one, owner, rank, 2 * rank, adapters)
    token_length = first_all.shape[0]
    attend = fast_attention if mover.fast else plain_attention
    attended, attention_back = attend(
        first_slots, qkv_full, la_q, la_k, la_v, query_exit, key_exit, value_exit, document_line
    )

    out_entry = cut(turned(output_entry_maps), s * q_cols, q_cols, 1)
    out_exit = output_exit_maps.reshape(flat, -1)
    la_out_part = fold(reverse_product(attended, out_entry) * mask_rank, rank, 0)
    attn_sum = mover.scatter_tokens(low_dot(attended, out_full), la_out_part)
    la_out_own = attn_sum[1].astype(BF)
    attention_path = attn_sum[0] + low_dot(
        spread(la_out_own, own_owner, rank, 0, adapters), out_exit
    )
    middle = hidden_state + RESIDUAL_MULT * attention_path

    second_normed, scale_two = normed(middle, feedforward_norm_gain)
    second_normed = second_normed.astype(BF)
    entry_maps = turned(feedforward_entry_maps)
    picked_second = reverse_product(second_normed, entry_maps) * adapter_mask(
        own_owner, 2 * rank, adapters
    )
    picked_second = fold(picked_second, 2 * rank, rank) + la_out_own.astype(F32)
    second_all = mover.gather_tokens(
        jnp.concatenate(
            [mover.to_slots(second_normed, row_block), picked_second.astype(BF)], axis=1
        )
    )
    second_slots = second_all[:, :width]
    la_out = spread(second_all[:, width:], owner, rank, 0, adapters)
    la_gate = spread(second_all[:, width:], owner, rank, rank, adapters)
    la_up = spread(second_all[:, width:], owner, rank, 2 * rank, adapters)

    down_exit = down_exit_maps.reshape(flat, -1)
    d_la_d = (reverse_product(d_mlp, down_exit) * mask_rank).astype(BF)
    d_mixed_slots = reverse_product(d_mlp[:, :half_width], down_low) + reverse_product(
        d_mlp[:, half_width:], down_high
    )
    down_entry = jnp.concatenate(own_hidden(turned(down_entry_maps)), axis=1)
    all_exits = feedforward_exit_maps.reshape(2, flat, -1)
    exits = [jnp.concatenate(own_hidden(all_exits[i]), axis=1) for i in range(2)]
    d_second = jnp.zeros((token_length, width), F32)
    d_la_gate = jnp.zeros((token_length, flat), F32)
    d_la_up = jnp.zeros((token_length, flat), F32)
    mixed_parts, gate_grads, up_grads, entry_grads = [], [], [], []
    for (lower, upper), weights in zip(chunk_bounds, chunk_weights):
        size = upper - lower
        both = low_dot(second_slots, weights)
        gate = both[:, :size] + low_dot(la_gate, exits[0][:, lower:upper])
        up = both[:, size:] + low_dot(la_up, exits[1][:, lower:upper])
        d_parts = []
        at = lower
        while at < upper:
            owner_w = at // hid_block
            stop = min(upper, (owner_w + 1) * hid_block)
            start = mover.slot_of(owner_w) * hid_block + (at - owner_w * hid_block)
            d_parts.append(cut(d_mixed_slots, start, stop - at, 1))
            at = stop
        d_mixed = jnp.concatenate(d_parts, axis=1) + low_dot(d_la_d, down_entry[:, lower:upper])
        sigma = jax.nn.sigmoid(gate)
        swish = gate * sigma
        mixed = (swish * up).astype(BF)
        d_gate = (d_mixed * up * sigma * (1.0 + gate * (1.0 - sigma))).astype(BF)
        d_up = (d_mixed * swish).astype(BF)
        d_second = d_second + reverse_product(jnp.concatenate([d_gate, d_up], axis=1), weights)
        d_la_gate = d_la_gate + reverse_product(d_gate, exits[0][:, lower:upper])
        d_la_up = d_la_up + reverse_product(d_up, exits[1][:, lower:upper])
        mixed_parts.append(mixed)
        gate_grads.append(gradient_product(la_gate, d_gate))
        up_grads.append(gradient_product(la_up, d_up))
        entry_grads.append(gradient_product(d_la_d, mixed))
    d_la_two_part = fold(d_la_gate * mask_rank, rank, 0) + fold(d_la_up * mask_rank, rank, rank)
    d_second_sum = mover.scatter_tokens(d_second, d_la_two_part)
    d_la_two_own = d_second_sum[1].astype(BF)
    d_second_own = mover.from_slots(d_second_sum[0], row_block) + low_dot(
        spread(d_la_two_own, own_owner, 2 * rank, 0, adapters), entry_maps
    )
    grad_middle = output_gradient + normed_back(
        middle, scale_two, feedforward_norm_gain, d_second_own
    )
    d_attn_own = (RESIDUAL_MULT * grad_middle).astype(BF)
    d_attn_all = mover.gather_tokens(jnp.concatenate([d_attn_own, d_la_two_own], axis=1))
    d_attn = d_attn_all[:, :width]
    gate_grad = jnp.concatenate(gate_grads, axis=1)
    up_grad = jnp.concatenate(up_grads, axis=1)
    down_in_grad = jnp.concatenate(entry_grads, axis=1)
    hidden_grads = mover.sum_hidden([gate_grad, up_grad, down_in_grad], hid_block)

    mixed_slots = mover.to_slots(jnp.concatenate(mixed_parts, axis=1), hid_block)
    mixed_all = jnp.concatenate(mixed_parts, axis=1)
    la_down_part = fold(reverse_product(mixed_all, down_entry) * mask_rank, rank, 0)
    mlp_sum = mover.scatter_tokens(
        jnp.concatenate([low_dot(mixed_slots, down_low), low_dot(mixed_slots, down_high)], axis=1),
        la_down_part,
    )
    la_down_own = mlp_sum[1].astype(BF)
    feedforward_path = mlp_sum[0] + low_dot(
        spread(la_down_own, own_owner, rank, 0, adapters), down_exit
    )
    layer_out = (middle + RESIDUAL_MULT * feedforward_path).astype(BF)[None]
    la_down = spread(mover.gather_tokens(la_down_own), owner, rank, 0, adapters)

    def own_features(slots):
        per = wsh_size // seq_size
        parts = [
            cut(slots, mover.slot_of(s * per + i) * row_block, row_block, 1) for i in range(per)
        ]
        return jnp.concatenate(parts, axis=1)

    d_la_two = spread(d_attn_all[:, width:], owner, 2 * rank, 0, adapters)
    entry_grad = gradient_product(d_la_two, own_features(second_slots))
    down_out_grad = gradient_product(la_down, cut(d_mlp, s * feature, feature, 1))
    d_la_o = (reverse_product(d_attn, out_exit) * mask_rank).astype(BF)
    out_in_grad = gradient_product(d_la_o, attended)
    out_out_grad = gradient_product(la_out, cut(d_attn, s * feature, feature, 1))
    feature_grads = mover.sum_features([entry_grad, down_out_grad, out_in_grad, out_out_grad])

    d_attended = (reverse_product(d_attn, out_full) + low_dot(d_la_o, out_entry)).astype(BF)
    d_query, d_key, d_value = attention_back(d_attended)
    d_la_one_part = (
        fold(reverse_product(d_query, query_exit) * mask_rank, rank, 0)
        + fold(reverse_product(d_key, key_exit) * mask_rank, rank, rank)
        + fold(reverse_product(d_value, value_exit) * mask_rank, rank, 2 * rank)
    )
    d_la_one = mover.sum_small(d_la_one_part.astype(BF)).astype(BF)
    d_first_part = reverse_product(jnp.concatenate([d_query, d_key, d_value], axis=1), qkv_full)
    (d_first_sum,) = mover.scatter_tokens(d_first_part)
    d_la_one_own = cut(d_la_one, s * own_rows, own_rows, 0)
    d_first = mover.from_slots(d_first_sum, row_block) + low_dot(
        spread(d_la_one_own, own_owner, 3 * rank, 0, adapters), input_maps
    )
    hidden_gradient = grad_middle + normed_back(
        hidden_state, scale_one, attention_norm_gain, d_first
    )
    attention_in_grad = gradient_product(
        spread(d_la_one, owner, 3 * rank, 0, adapters), own_features(first_slots)
    )
    query_out_grad = gradient_product(la_q, d_query)
    key_out_grad = gradient_product(la_k, d_key)
    value_out_grad = gradient_product(la_v, d_value)
    last_grads = mover.sum_features(
        [attention_in_grad, query_out_grad], key_out_grad, value_out_grad
    )

    def back(values, shape):
        return values.reshape(shape[1], shape[2], shape[0]).transpose(2, 0, 1)

    return (
        layer_out,
        hidden_gradient[None],
        back(last_grads[0], attention_down_maps.shape),
        last_grads[1].reshape(query_exit_maps.shape),
        last_grads[2].reshape(key_value_exit_maps.shape),
        back(feature_grads[2], output_entry_maps.shape),
        feature_grads[3].reshape(output_exit_maps.shape),
        back(feature_grads[0], feedforward_entry_maps.shape),
        hidden_grads[0].reshape(feedforward_exit_maps.shape),
        back(hidden_grads[1], down_entry_maps.shape),
        feature_grads[1].reshape(down_exit_maps.shape),
    )


def solution(mesh):
    seq_size, wsh_size = mesh.shape["seq"], mesh.shape["wsh"]

    def on_device(*args):
        return layer(Mover(seq_size, wsh_size), args)

    rows = P("wsh", None)
    stream = P("wsh", "seq", None)
    in_specs = (stream, P("wsh", "seq"), rows, P(), P()) + (rows,) * 7 + (P(),) * 9 + (stream,)
    out_specs = (stream, stream) + (P(),) * 9
    return jax.shard_map(
        on_device, mesh=mesh, in_specs=in_specs, out_specs=out_specs, check_vma=False
    )
```

```python
import jax
import jax.numpy as jnp
from jax import lax
from jax.experimental import pallas as pl
from jax.experimental.pallas import tpu as pltpu
from jax.sharding import PartitionSpec as P

QUERY_HEADS = 32
KEY_HEADS = 8
HEAD_WIDTH = 64
LANES = 128
PACK = 512
TILE = 256

EPSILON = 1e-05
RESIDUAL_MULT = 0.22
SCORE_MULT = 0.015625
ROPE_BASE = 10000000.0
MASKED = -1e30

BF = jnp.bfloat16
F32 = jnp.float32

CORE_SWAP = [(s, s ^ 1) for s in range(4)]
Y_SWAP = [(s, s ^ 2) for s in range(4)]
X_SWAP = [(w, w ^ 1) for w in range(8)]
NEAR_SWAP = [(w, w ^ 2) for w in range(8)]
FAR_SWAP = [(w, w ^ 4) for w in range(8)]


def z_shift(steps):
    return [(2 * z + x, 2 * ((z + steps) % 4) + x) for z in range(4) for x in range(2)]


def low_dot(left, right):
    return jnp.dot(left, right, preferred_element_type=F32)


def gradient_product(left, right):
    return lax.dot_general(left, right, (((0,), (0,)), ((), ())), preferred_element_type=F32)


def reverse_product(left, right):
    return lax.dot_general(left, right, (((1,), (1,)), ((), ())), preferred_element_type=F32)


def normed(values, gain):
    norm_scale = lax.rsqrt(jnp.mean(values * values, axis=-1, keepdims=True) + EPSILON)
    return (values * norm_scale * gain, norm_scale)


def normed_back(values, norm_scale, gain, grad_in):
    scaled = grad_in * gain
    cubed = norm_scale * norm_scale * norm_scale
    return norm_scale * scaled - values * cubed * jnp.mean(scaled * values, axis=-1, keepdims=True)


def rope_tables(positions, head_size):
    half_size = head_size // 2
    inv_freq = ROPE_BASE ** (-(jnp.arange(half_size).astype(F32) * 2.0) / head_size)
    angles = positions.astype(F32)[:, None] * inv_freq[None, :]
    return (jnp.cos(angles)[:, None, :], jnp.sin(angles)[:, None, :])


def rotate(values, cos_tab, sin_tab):
    half_size = values.shape[-1] // 2
    former = values[..., :half_size]
    latter = values[..., half_size:]
    return jnp.concatenate(
        [former * cos_tab - latter * sin_tab, latter * cos_tab + former * sin_tab], axis=-1
    )


def cut(values, start, size, axis):
    return lax.dynamic_slice_in_dim(values, start, size, axis)


def pick(values, index, axis):
    return lax.dynamic_index_in_dim(values, index, axis, keepdims=False)


def adapter_mask(owner, ranks, adapters):
    lane = jnp.arange(adapters * ranks, dtype=jnp.int32) // ranks
    return (owner[:, None] == lane[None, :]).astype(F32)


def fold(masked, ranks, offset):
    rows = jnp.arange(masked.shape[1], dtype=jnp.int32) % ranks
    lanes = jnp.arange(LANES, dtype=jnp.int32) - offset
    return low_dot(masked.astype(BF), (rows[:, None] == lanes[None, :]).astype(BF))


def spread(folded, owner, ranks, offset, adapters):
    rows = jnp.arange(LANES, dtype=jnp.int32) - offset
    lanes = jnp.arange(adapters * ranks, dtype=jnp.int32) % ranks
    wide = low_dot(folded.astype(BF), (rows[:, None] == lanes[None, :]).astype(BF))
    return (wide * adapter_mask(owner, ranks, adapters)).astype(BF)


def pack(values):
    parts = [values[:, i : i + PACK] for i in range(0, values.shape[1], PACK)]
    return jnp.concatenate(parts, axis=0)


def after(values, *deps):
    deps = [d for d in deps if d is not None]
    if not deps:
        return values
    return lax.optimization_barrier((values, tuple(deps)))[0]


class Mover:
    def __init__(self, seq_size, wsh_size):
        self.seq_size, self.wsh_size = seq_size, wsh_size
        self.fast = seq_size == 4 and wsh_size == 8
        self.s, self.w = lax.axis_index("seq"), lax.axis_index("wsh")
        self.y, self.c = self.s // 2, self.s % 2
        self.z, self.x = self.w // 2, self.w % 2
        self.marks = {}

    def far(self, chunk, *deps):
        chunk = after(chunk, *deps)
        if not self.fast:
            return chunk
        return jnp.concatenate([chunk, lax.ppermute(chunk, "wsh", FAR_SWAP)], axis=0)

    def near(self, pair, *deps):
        pair = after(pair, *deps)
        if not self.fast:
            return pair
        return jnp.concatenate([pair, lax.ppermute(pair, "wsh", NEAR_SWAP)], axis=0)

    def across(self, four, *deps):
        four = after(four, *deps)
        if not self.fast:
            return (lax.all_gather(four, "wsh", axis=0, tiled=True),)
        return four, lax.ppermute(four, "wsh", X_SWAP)

    def swap_bits(self, d):
        return d // 2 + 2 * (d % 2)

    def slot_owner(self, k):
        if not self.fast:
            return k
        return 2 * (self.z ^ self.swap_bits(k % 4)) + (self.x ^ (k // 4))

    def slot_of(self, w):
        if not self.fast:
            return w
        return self.z_slot(w // 2) + 4 * (self.x ^ (w % 2))

    def z_slot(self, z):
        return self.swap_bits(self.z ^ z)

    def to_slots(self, values, block):
        if not self.fast:
            return values
        parts = [cut(values, self.slot_owner(k) * block, block, 1) for k in range(self.wsh_size)]
        return jnp.concatenate(parts, axis=1)

    def from_slots(self, values, block):
        if not self.fast:
            return values
        parts = [cut(values, self.slot_of(w) * block, block, 1) for w in range(self.wsh_size)]
        return jnp.concatenate(parts, axis=1)

    def head_rows(self, weight):
        rows = weight.shape[0]
        per = self.wsh_size // self.seq_size
        if not self.fast:
            return cut(
                lax.all_gather(weight, "wsh", axis=0, tiled=True),
                self.s * per * rows,
                per * rows,
                0,
            )
        piece = rows // 4

        def part(z):
            return cut(weight, z * piece, piece, 0)

        def pairs(senders, step):
            return [
                (8 * s + 2 * (s ^ sender) + x, 8 * s + 2 * (s ^ sender ^ step) + x)
                for s in range(4)
                for sender in senders
                for x in range(2)
            ]

        z, axes = self.z, ("seq", "wsh")
        away = jnp.concatenate([part(z ^ 2), part(z ^ 3)], axis=0)
        got = lax.ppermute(away, axes, pairs((0,), 2))
        first = z == self.s
        mine = jnp.where(first, part(z), got[:piece])
        away = jnp.where(first, part(z ^ 1), got[piece:])
        got = lax.ppermute(away, axes, pairs((0, 2), 1))
        return jnp.where(first | (z == (self.s ^ 2)), mine, got)

    def head_rows_done(self, halves, rows):
        piece = rows // 4
        out = []
        for shard in range(2):
            half = jnp.where(self.x == shard, halves[0], halves[1])
            blocks = half.reshape(4, piece, half.shape[1])
            out += [pick(blocks, self.z_slot(j), 0) for j in range(4)]
        return jnp.concatenate(out, axis=0)

    def gather_tokens(self, values):
        if not self.fast:
            return lax.all_gather(values, "seq", axis=0, tiled=True)
        return self.gather_rest(values, lax.ppermute(values, "seq", Y_SWAP))

    def gather_rest(self, values, other):
        first = self.y == 0
        column = jnp.stack([jnp.where(first, values, other), jnp.where(first, other, values)])
        partner = lax.ppermute(column, "seq", CORE_SWAP)
        first = self.c == 0
        whole = jnp.stack(
            [jnp.where(first, column, partner), jnp.where(first, partner, column)], axis=1
        )
        return whole.reshape((4 * values.shape[0],) + values.shape[1:])

    def scatter_tokens(self, *partials, deps=(), late=(), mark=None):
        if not self.fast:
            return [
                lax.psum_scatter(v.astype(BF), "seq", scatter_dimension=0, tiled=True).astype(F32)
                for v in partials
            ]
        rows = partials[0].shape[0] // 4
        blocks = [v.reshape(2, 2, rows, v.shape[1]) for v in partials]
        out = jnp.concatenate([pick(v, 1 - self.c, 1).astype(BF) for v in blocks], axis=2)
        got = lax.ppermute(out, "seq", CORE_SWAP).astype(F32)
        mine = jnp.concatenate([pick(v, self.c, 1) for v in blocks], axis=2)
        away = (pick(mine, 1 - self.y, 0) + pick(got, 1 - self.y, 0)).astype(BF)
        other = lax.ppermute(after(away, *deps), "seq", Y_SWAP)
        self.marks[mark] = other
        other = after(other, *late).astype(F32)
        total = pick(mine, self.y, 0) + pick(got, self.y, 0) + other
        found, at = [], 0
        for v in partials:
            found.append(total[:, at : at + v.shape[1]])
            at += v.shape[1]
        return found

    def sum_small(self, partial):
        if not self.fast:
            return lax.psum(partial, "seq")
        total = partial.astype(F32) + lax.ppermute(partial, "seq", CORE_SWAP).astype(F32)
        other = lax.ppermute(total.astype(BF), "seq", Y_SWAP)
        return total + other.astype(F32)

    def sum_plain(self, grad):
        total = lax.psum(grad.astype(BF), "wsh")
        return lax.all_gather(total.astype(BF), "seq", axis=0).astype(F32)

    def sum_hidden(self, grads, hid_block, deps=(), mark=None, early=()):
        if not self.fast:
            found = []
            for grad in grads:
                rows = grad.shape[0]
                wide = self.sum_plain(grad).reshape(self.seq_size, rows, self.wsh_size, hid_block)
                found.append(wide.transpose(1, 2, 0, 3).reshape(rows, -1))
            return [jnp.stack(found[:2]), found[2]]
        parts = self.sum_gather(jnp.concatenate([pack(v) for v in grads], axis=0), deps, (), mark, early)
        s = self.s.astype(jnp.int32)[None]
        return [
            final_hidden(parts, s, 0, 2),
            final_hidden(parts, s, 8 * LANES, 1)[0],
        ]

    def sum_features(self, grads, key=None, value=None, late=()):
        if not self.fast:
            grads = grads + ([key, value] if key is not None else [])
            found = []
            for grad in grads:
                found.append(self.sum_plain(grad).transpose(1, 0, 2).reshape(grad.shape[0], -1))
            return found[:-2] + [jnp.stack(found[-2:])] if key is not None else found
        packed = list(grads)
        if key is not None:
            rest = jnp.zeros((key.shape[0], PACK - 2 * LANES), F32)
            packed.append(jnp.concatenate([key, value, rest], axis=1))
        parts = self.sum_gather(jnp.concatenate(packed, axis=0), (), late)
        s = self.s.astype(jnp.int32)[None]
        found, at = [], 0
        for grad in grads:
            found.append(final_features(parts, s, at, grad.shape[0]))
            at += grad.shape[0]
        if key is not None:
            found.append(final_kv(parts, s, at))
        return found

    def sum_gather(self, packed, deps=(), late=(), mark=None, early=()):
        rows = packed.shape[0]
        halves = packed.reshape(2, rows // 2, PACK)
        got = lax.ppermute(pick(halves, 1 - self.x, 0).astype(BF), "wsh", X_SWAP)
        half = pick(halves, self.x, 0) + got.astype(F32)
        blocks = half.reshape(4, rows // 8, PACK)
        total = pick(blocks, self.z, 0)
        for r in range(1, 4):
            out = pick(blocks, (self.z + r) % 4, 0).astype(BF)
            total = total + lax.ppermute(out, "wsh", z_shift(r)).astype(F32)
        own = total.astype(BF)
        got = [own] + [lax.ppermute(own, "wsh", z_shift(r)) for r in range(1, 4)]
        ring = jnp.stack(got)
        half = jnp.concatenate([pick(ring, (self.z - j) % 4, 0) for j in range(4)], axis=0)
        half = after(half, *early)
        other = lax.ppermute(half, "wsh", X_SWAP)
        first = self.x == 0
        part = jnp.concatenate([jnp.where(first, half, other), jnp.where(first, other, half)])
        core = lax.ppermute(part, "seq", CORE_SWAP)
        if mark is None:
            other = lax.ppermute(after(part, *deps), "seq", Y_SWAP)
        else:
            top = lax.ppermute(after(part[: rows // 2], *deps), "seq", Y_SWAP)
            rest = lax.ppermute(after(part[rows // 2 :], top), "seq", Y_SWAP)
            self.marks[mark] = (top, rest)
            other = jnp.concatenate([top, rest], axis=0)
        other = after(other, *late)
        return part, core, other, lax.ppermute(other, "seq", CORE_SWAP)


def final_body(s_ref, own, core, other, last, out_ref):
    columns = own.shape[-1]
    for k in range(4):
        place = s_ref[0] ^ k
        low = jnp.where(place % 2 == 0, own[...], core[...])
        high = jnp.where(place % 2 == 0, other[...], last[...])
        value = jnp.where(place < 2, low, high).astype(F32)
        at = slice(k * columns, (k + 1) * columns)
        if len(out_ref.shape) == 3:
            out_ref[0, :, at] = value
        else:
            out_ref[:, at] = value


def final_call(parts, s, grid, part_block, part_map, out_shape, out_block, out_map):
    return pl.pallas_call(
        final_body,
        grid_spec=pltpu.PrefetchScalarGridSpec(
            num_scalar_prefetch=1,
            grid=grid,
            in_specs=[pl.BlockSpec(part_block, part_map)] * 4,
            out_specs=pl.BlockSpec(out_block, out_map),
        ),
        out_shape=jax.ShapeDtypeStruct(out_shape, F32),
        name="finish",
    )(s, *parts)


def final_features(parts, s, row, rows):
    at = row // LANES
    return final_call(
        parts,
        s,
        (rows // LANES,),
        (LANES, PACK),
        lambda i, _: (at + i, 0),
        (rows, 4 * PACK),
        (LANES, 4 * PACK),
        lambda i, _: (i, 0),
    )


def final_hidden(parts, s, row, count):
    at = row // LANES
    return final_call(
        parts,
        s,
        (count, 8),
        (LANES, TILE),
        lambda n, w, _: (at + 4 * n + w // 2, w % 2),
        (count, LANES, 32 * TILE),
        (1, LANES, 4 * TILE),
        lambda n, w, _: (n, 0, w),
    )


def final_kv(parts, s, row):
    at = row // LANES
    return final_call(
        parts,
        s,
        (2,),
        (LANES, LANES),
        lambda n, _: (at, n),
        (2, LANES, 4 * LANES),
        (1, LANES, 4 * LANES),
        lambda n, _: (n, 0, 0),
    )


def half_lanes(rows, half):
    lane = lax.broadcasted_iota(jnp.int32, (rows, LANES), 1)
    return (lane < HEAD_WIDTH) if half == 0 else (lane >= HEAD_WIDTH)


def turn(values, cos_tab, sin_tab):
    lane = lax.broadcasted_iota(jnp.int32, values.shape, 1)
    swapped = jnp.where(
        lane % HEAD_WIDTH < HEAD_WIDTH // 2,
        pltpu.roll(values, LANES - HEAD_WIDTH // 2, 1),
        pltpu.roll(values, HEAD_WIDTH // 2, 1),
    )
    return values * cos_tab + swapped * sin_tab


def twice(values, half):
    other = pltpu.roll(values, HEAD_WIDTH, 1)
    first = half_lanes(values.shape[0], 0)
    return jnp.where(first, values, other) if half == 0 else jnp.where(first, other, values)


def qkv_body(x_ref, w_own, w_other, la_q, la_k, la_v, exit_q, exit_kv, cos_ref, sin_ref, q_ref, k_ref, v_ref):
    cos_tab, sin_tab = cos_ref[...], sin_ref[...]
    half = w_own.shape[0]
    product = low_dot(x_ref[:, :half], w_own[...]) + low_dot(x_ref[:, half:], w_other[...])
    q_cols = q_ref.shape[1]
    query = product[:, :q_cols] + low_dot(la_q[...], exit_q[...])
    for i in range(0, q_cols, LANES):
        q_ref[:, i : i + LANES] = turn(query[:, i : i + LANES], cos_tab, sin_tab).astype(BF)
    key = product[:, q_cols : q_cols + LANES] + low_dot(la_k[...], exit_kv[0])
    key = turn(key, cos_tab, sin_tab)
    value = product[:, q_cols + LANES :] + low_dot(la_v[...], exit_kv[1])
    for half in range(2):
        k_ref[:, half * LANES : (half + 1) * LANES] = twice(key, half).astype(BF)
        v_ref[:, half * LANES : (half + 1) * LANES] = twice(value, half).astype(BF)


def qkv_call(x, weights, la_q, la_k, la_v, exit_q, exit_kv, cos_tab, sin_tab):
    rows, width = x.shape[0], 2 * weights[0].shape[0]
    q_cols = exit_q.shape[1]

    def tile(columns):
        return pl.BlockSpec((TILE, columns), lambda i: (i, 0))

    return pl.pallas_call(
        qkv_body,
        grid=(rows // TILE,),
        in_specs=[
            tile(width),
            pl.BlockSpec(weights[0].shape, lambda i: (0, 0)),
            pl.BlockSpec(weights[1].shape, lambda i: (0, 0)),
            tile(LANES),
            tile(LANES),
            tile(LANES),
            pl.BlockSpec(exit_q.shape, lambda i: (0, 0)),
            pl.BlockSpec(exit_kv.shape, lambda i: (0, 0, 0)),
            tile(LANES),
            tile(LANES),
        ],
        out_specs=[tile(q_cols), tile(2 * LANES), tile(2 * LANES)],
        out_shape=[
            jax.ShapeDtypeStruct((rows, q_cols), BF),
            jax.ShapeDtypeStruct((rows, 2 * LANES), BF),
            jax.ShapeDtypeStruct((rows, 2 * LANES), BF),
        ],
        name="qkv",
        cost_estimate=pl.CostEstimate(
            flops=2 * rows * width * weights[0].shape[1], bytes_accessed=12 << 20, transcendentals=0
        ),
    )(x, *weights, la_q, la_k, la_v, exit_q, exit_kv, cos_tab, sin_tab)


def allowed_pairs(i, t, doc_col, doc_row):
    start = pl.multiple_of(t * TILE, TILE)
    rows = i * TILE + lax.broadcasted_iota(jnp.int32, (TILE, TILE), 0)
    keys = start + lax.broadcasted_iota(jnp.int32, (TILE, TILE), 1)
    return (doc_col[...] == doc_row[:, pl.ds(start, TILE)]) & (keys <= rows)


def forward_body(first_ref, q_ref, k_ref, v_ref, doc_col, doc_row, o_ref, lse_ref, m_s, l_s, acc_s):
    i = pl.program_id(0)
    m_s[...] = jnp.full_like(m_s, MASKED)
    l_s[...] = jnp.zeros_like(l_s)
    acc_s[...] = jnp.zeros_like(acc_s)

    def step(t, carry):
        allowed = allowed_pairs(i, t, doc_col, doc_row)
        start = pl.multiple_of(t * TILE, TILE)
        keys, vals = k_ref[pl.ds(start, TILE), :], v_ref[pl.ds(start, TILE), :]
        for h in range(4):
            pair = q_ref[:, (h // 2) * LANES : (h // 2 + 1) * LANES]
            query = jnp.where(half_lanes(TILE, h % 2), pair, jnp.zeros_like(pair))
            logits = jnp.where(allowed, SCORE_MULT * reverse_product(query, keys), MASKED)
            old = m_s[h]
            top = jnp.maximum(old, jnp.max(logits, axis=1, keepdims=True))
            shrink = jnp.exp(old - top)
            shifted = jnp.exp(logits - top)
            m_s[h] = top
            l_s[h] = l_s[h] * shrink + jnp.sum(shifted, axis=1, keepdims=True)
            acc_s[h] = acc_s[h] * shrink + low_dot(shifted.astype(BF), vals)
        return carry

    lax.fori_loop(first_ref[i], i + 1, step, 0)
    lane = lax.broadcasted_iota(jnp.int32, (TILE, LANES), 1)
    total = jnp.zeros((TILE, LANES), F32)
    for p in range(2):
        both = [acc_s[2 * p + n] / l_s[2 * p + n] for n in range(2)]
        o_ref[:, p * LANES : (p + 1) * LANES] = jnp.where(
            half_lanes(TILE, 0), both[0], both[1]
        ).astype(BF)
    for h in range(4):
        total = jnp.where(lane == h, m_s[h] + jnp.log(l_s[h]), total)
    lse_ref[...] = total


def attention_call(j, first, query, keys, values, doc_col, doc_row):
    rows = query.shape[0]
    group = query.shape[1] // 2
    return pl.pallas_call(
        forward_body,
        grid_spec=pltpu.PrefetchScalarGridSpec(
            num_scalar_prefetch=1,
            grid=(rows // TILE,),
            in_specs=[
                pl.BlockSpec((TILE, group), lambda i, _: (i, j)),
                pl.BlockSpec((rows, LANES), lambda i, _: (0, j)),
                pl.BlockSpec((rows, LANES), lambda i, _: (0, j)),
                pl.BlockSpec((TILE, 1), lambda i, _: (i, 0)),
                pl.BlockSpec((1, rows), lambda i, _: (0, 0)),
            ],
            out_specs=[
                pl.BlockSpec((TILE, group), lambda i, _: (i, 0)),
                pl.BlockSpec((TILE, LANES), lambda i, _: (i, 0)),
            ],
            scratch_shapes=[
                pltpu.VMEM((4, TILE, 1), F32),
                pltpu.VMEM((4, TILE, 1), F32),
                pltpu.VMEM((4, TILE, LANES), F32),
            ],
        ),
        out_shape=[
            jax.ShapeDtypeStruct((rows, group), BF),
            jax.ShapeDtypeStruct((rows, LANES), F32),
        ],
        name="attention",
        cost_estimate=pl.CostEstimate(
            flops=4 * 4 * rows * rows * LANES,
            bytes_accessed=3 << 20,
            transcendentals=4 * rows * rows,
        ),
    )(first, query, keys, values, doc_col, doc_row)


def backward_body(
    first_ref, q_ref, k_ref, v_ref, do_ref, o_ref, lse_ref, doc_col, doc_row, cos_ref, sin_ref,
    cos_all, sin_all, dq_ref, dk_ref, dv_ref, dq_s, dk_s, dv_s,
):
    i = pl.program_id(0)

    @pl.when(i == 0)
    def _():
        dk_s[...] = jnp.zeros_like(dk_s)
        dv_s[...] = jnp.zeros_like(dv_s)

    dq_s[...] = jnp.zeros_like(dq_s)
    queries, grads, deltas = [], [], []
    for h in range(4):
        at = slice((h // 2) * LANES, (h // 2 + 1) * LANES)
        half = half_lanes(TILE, h % 2)
        pair, grad = q_ref[:, at], do_ref[:, at]
        queries.append(jnp.where(half, pair, jnp.zeros_like(pair)))
        grads.append(jnp.where(half, grad, jnp.zeros_like(grad)))
        product = grads[h].astype(F32) * o_ref[:, at].astype(F32)
        deltas.append(jnp.sum(product, axis=1, keepdims=True))

    def step(t, carry):
        allowed = allowed_pairs(i, t, doc_col, doc_row)
        start = pl.multiple_of(t * TILE, TILE)
        at = pl.ds(start, TILE)
        keys, vals = k_ref[at, :], v_ref[at, :]
        dk, dv = dk_s[at, :], dv_s[at, :]
        for h in range(4):
            logits = jnp.where(allowed, SCORE_MULT * reverse_product(queries[h], keys), MASKED)
            probs = jnp.exp(logits - lse_ref[:, h : h + 1])
            d_probs = reverse_product(grads[h], vals)
            d_logits = (probs * (d_probs - deltas[h])).astype(BF)
            dq_s[h] = dq_s[h] + low_dot(d_logits, keys)
            dk = dk + gradient_product(d_logits, queries[h])
            dv = dv + gradient_product(probs.astype(BF), grads[h])
        dk_s[at, :] = dk
        dv_s[at, :] = dv
        return carry

    lax.fori_loop(first_ref[i], i + 1, step, 0)
    for p in range(2):
        both = jnp.where(half_lanes(TILE, 0), dq_s[2 * p], dq_s[2 * p + 1])
        both = (SCORE_MULT * both).astype(BF).astype(F32)
        dq_ref[:, p * LANES : (p + 1) * LANES] = turn(both, cos_ref[...], -sin_ref[...]).astype(BF)

    @pl.when(i == pl.num_programs(0) - 1)
    def _():
        def finish(t, carry):
            at = pl.ds(pl.multiple_of(t * TILE, TILE), TILE)
            dk, dv = dk_s[at, :], dv_s[at, :]
            dk = (SCORE_MULT * (dk + pltpu.roll(dk, HEAD_WIDTH, 1))).astype(BF).astype(F32)
            dk_ref[at, :] = turn(dk, cos_all[at, :], -sin_all[at, :]).astype(BF)
            dv_ref[at, :] = (dv + pltpu.roll(dv, HEAD_WIDTH, 1)).astype(BF)
            return carry

        lax.fori_loop(0, pl.num_programs(0), finish, 0)


def attention_back_call(
    j, first, query, keys, values, d_out, out, lse, doc_col, doc_row, cos_tab, sin_tab
):
    rows = query.shape[0]
    group = query.shape[1] // 2
    whole = pl.BlockSpec((rows, LANES), lambda i, _: (0, j))
    tile = pl.BlockSpec((TILE, group), lambda i, _: (i, j))
    table = pl.BlockSpec((TILE, LANES), lambda i, _: (i, 0))
    table_all = pl.BlockSpec((rows, LANES), lambda i, _: (0, 0))
    own_tile = pl.BlockSpec((TILE, group), lambda i, _: (i, 0))
    return pl.pallas_call(
        backward_body,
        grid_spec=pltpu.PrefetchScalarGridSpec(
            num_scalar_prefetch=1,
            grid=(rows // TILE,),
            in_specs=[
                tile,
                whole,
                whole,
                tile,
                own_tile,
                table,
                pl.BlockSpec((TILE, 1), lambda i, _: (i, 0)),
                pl.BlockSpec((1, rows), lambda i, _: (0, 0)),
                table,
                table,
                table_all,
                table_all,
            ],
            out_specs=[own_tile, table_all, table_all],
            scratch_shapes=[
                pltpu.VMEM((4, TILE, LANES), F32),
                pltpu.VMEM((rows, LANES), F32),
                pltpu.VMEM((rows, LANES), F32),
            ],
        ),
        out_shape=[
            jax.ShapeDtypeStruct((rows, group), BF),
            jax.ShapeDtypeStruct((rows, LANES), BF),
            jax.ShapeDtypeStruct((rows, LANES), BF),
        ],
        name="attention_back",
        cost_estimate=pl.CostEstimate(
            flops=4 * 10 * rows * rows * LANES,
            bytes_accessed=5 << 20,
            transcendentals=4 * rows * rows,
        ),
    )(first, query, keys, values, d_out, out, lse, doc_col, doc_row, cos_tab, sin_tab, cos_tab, sin_tab)


def fast_attention(
    x, weights, la_q, la_k, la_v, exit_q, exit_k, exit_v, document_line
):
    rows = x.shape[0]
    half = HEAD_WIDTH // 2
    cos_tab, sin_tab = rope_tables(jnp.arange(rows, dtype=jnp.int32), HEAD_WIDTH)
    cos_tab = jnp.tile(cos_tab.reshape(rows, half), (1, 4))
    sin_tab = sin_tab.reshape(rows, half)
    sin_tab = jnp.tile(jnp.concatenate([-sin_tab, sin_tab], axis=1), (1, 2))
    first_docs = document_line[::TILE]
    first = jnp.sum((document_line[None, :] < first_docs[:, None]).astype(jnp.int32), axis=1)
    first = first // TILE
    doc_col, doc_row = document_line[:, None], document_line[None, :]
    query, keys, values = qkv_call(
        x, weights, la_q, la_k, la_v, exit_q, jnp.stack([exit_k, exit_v]), cos_tab, sin_tab
    )
    early = attention_call(0, first, query, keys, values, doc_col, doc_row)
    found = [early]

    def finish(*deps):
        query_late = after(query, early[0], *deps)
        found.append(attention_call(1, first, query_late, keys, values, doc_col, doc_row))
        return jnp.concatenate([early[0], found[1][0]], axis=1)

    def backward(d_heads, between, behind):
        back = []
        for j in range(2):
            if j:
                d_heads = after(d_heads, back[0][1], *between)
            args = (first, query, keys, values, d_heads, *found[j], doc_col, doc_row)
            back.append(attention_back_call(j, *args, cos_tab, sin_tab))
        back[1] = after(back[1], *behind)
        lane = jnp.arange(LANES, dtype=jnp.int32)[None, :] < HEAD_WIDTH
        d_query = jnp.concatenate([back[0][0], back[1][0]], axis=1)
        d_key = jnp.where(lane, back[0][1], back[1][1])
        d_value = jnp.where(lane, back[0][2], back[1][2])
        return d_query, d_key, d_value

    return early[0], finish, backward


def units_rows(at_own, own, other):
    return jnp.where(at_own, own[...], other[...])


def mlp_body(owners, add, sc, n2, w_own, w_other, la_gate, la_up, exit_gate, exit_up, d_mlp,
             low_own, low_other, high_own, high_other, d_la_d, entry, *rest):
    if add:
        sum_in, la_in, mixed_ref, gate_ref, up_ref, sum_ref, la_ref = rest
    else:
        mixed_ref, gate_ref, up_ref, sum_ref, la_ref = rest
    half = w_own.shape[0]
    size = TILE * len(owners)
    both = low_dot(n2[:, :half], w_own[...]) + low_dot(n2[:, half:], w_other[...])
    gate = both[:, :size] + low_dot(la_gate[...], exit_gate[...])
    up = both[:, size:] + low_dot(la_up[...], exit_up[...])
    parts = []
    for w in owners:
        at_own = sc[1] == w % 2
        parts.append(
            reverse_product(d_mlp[:, :half], units_rows(at_own, low_own, low_other))
            + reverse_product(d_mlp[:, half:], units_rows(at_own, high_own, high_other))
        )
    d_mixed = jnp.concatenate(parts, axis=1) + low_dot(d_la_d[...], entry[...])
    sigma = jax.nn.sigmoid(gate)
    swish = gate * sigma
    mixed_ref[...] = (swish * up).astype(BF)
    d_gate = (d_mixed * up * sigma * (1.0 + gate * (1.0 - sigma))).astype(BF)
    d_up = (d_mixed * swish).astype(BF)
    gate_ref[...] = d_gate
    up_ref[...] = d_up
    d_both = jnp.concatenate([d_gate, d_up], axis=1)
    sum_own, sum_other = reverse_product(d_both, w_own[...]), reverse_product(d_both, w_other[...])
    back_gate, back_up = reverse_product(d_gate, exit_gate[...]), reverse_product(d_up, exit_up[...])
    if add:
        sum_own, sum_other = sum_own + sum_in[:, :half], sum_other + sum_in[:, half:]
        back_gate, back_up = back_gate + la_in[:, :LANES], back_up + la_in[:, LANES:]
    sum_ref[:, :half] = sum_own
    sum_ref[:, half:] = sum_other
    la_ref[:, :LANES] = back_gate
    la_ref[:, LANES:] = back_up


def mlp_call(owners, block, x, n2, weights, la_gate, la_up, exit_gate, exit_up, d_mlp, low, high,
             d_la_d, entry, sums):
    rows = d_mlp.shape[0]
    half = weights[0].shape[0]
    size = TILE * len(owners)

    def tile(columns):
        return pl.BlockSpec((TILE, columns), lambda t, _: (t, 0))

    def whole(array):
        return pl.BlockSpec(array.shape, lambda t, _: (0, 0))

    units = pl.BlockSpec((TILE, half), lambda t, sc: (sc[0], 0))
    args = [n2, *weights, la_gate, la_up, exit_gate, exit_up, d_mlp, *low, *high, d_la_d, entry]
    in_specs = [tile(2 * half), whole(weights[0]), whole(weights[1]), tile(LANES), tile(LANES)]
    in_specs += [whole(exit_gate), whole(exit_up), tile(2 * half)] + [units] * 4
    in_specs += [tile(LANES), whole(entry)]
    aliases = {}
    if sums is not None:
        aliases = {1 + len(args): 3, 2 + len(args): 4}
        args += sums
        in_specs += [tile(2 * half), tile(2 * LANES)]
    return pl.pallas_call(
        lambda *refs: mlp_body(owners, sums is not None, *refs),
        grid_spec=pltpu.PrefetchScalarGridSpec(
            num_scalar_prefetch=1,
            grid=(rows // TILE,),
            in_specs=in_specs,
            out_specs=[tile(size)] * 3 + [tile(2 * half), tile(2 * LANES)],
        ),
        out_shape=[jax.ShapeDtypeStruct((rows, size), BF)] * 3
        + [
            jax.ShapeDtypeStruct((rows, 2 * half), F32),
            jax.ShapeDtypeStruct((rows, 2 * LANES), F32),
        ],
        input_output_aliases=aliases,
        name="units",
        cost_estimate=pl.CostEstimate(
            flops=20 * rows * half * size, bytes_accessed=32 << 20, transcendentals=rows * size
        ),
    )(jnp.stack([block, x]).astype(jnp.int32), *args)


def mlp_out_body(chunks, sc, *refs):
    mixed = refs[: len(chunks)]
    low_own, low_other, high_own, high_other, out_ref = refs[len(chunks) :]
    half = low_own.shape[1]
    low = high = None
    for (owners, ref) in zip(chunks, mixed):
        for n, w in enumerate(owners):
            at = pl.ds(pl.multiple_of(sc[w // 2] * TILE, TILE), TILE)
            at_own = sc[4] == w % 2
            part = ref[:, n * TILE : (n + 1) * TILE]
            more_low = low_dot(part, jnp.where(at_own, low_own[at, :], low_other[at, :]))
            more_high = low_dot(part, jnp.where(at_own, high_own[at, :], high_other[at, :]))
            low = more_low if low is None else low + more_low
            high = more_high if high is None else high + more_high
    out_ref[:, :half] = low
    out_ref[:, half:] = high


def mlp_out_call(chunks, z_slots, x, mixed, low, high):
    rows, half = mixed[0].shape[0], low[0].shape[1]
    places = jnp.stack([*z_slots, x]).astype(jnp.int32)
    return pl.pallas_call(
        lambda *refs: mlp_out_body(chunks, *refs),
        grid_spec=pltpu.PrefetchScalarGridSpec(
            num_scalar_prefetch=1,
            grid=(rows // TILE,),
            in_specs=[pl.BlockSpec((TILE, m.shape[1]), lambda t, _: (t, 0)) for m in mixed]
            + [pl.BlockSpec(low[0].shape, lambda t, _: (0, 0))] * 4,
            out_specs=pl.BlockSpec((TILE, 2 * half), lambda t, _: (t, 0)),
        ),
        out_shape=jax.ShapeDtypeStruct((rows, 2 * half), F32),
        name="units_out",
        cost_estimate=pl.CostEstimate(
            flops=4 * rows * half * 8 * TILE, bytes_accessed=20 << 20, transcendentals=0
        ),
    )(places, *mixed, *low, *high)


def attention_forward(query_heads, key_heads, value_heads, document_line):
    token_length = query_heads.shape[0]
    kv_dev = key_heads.shape[1] // HEAD_WIDTH
    per_kv = query_heads.shape[1] // key_heads.shape[1]
    block_rows = min(512, token_length)
    query_four = query_heads.reshape(token_length, kv_dev, per_kv, HEAD_WIDTH)
    key_three = key_heads.reshape(token_length, kv_dev, HEAD_WIDTH)
    value_three = value_heads.reshape(token_length, kv_dev, HEAD_WIDTH)
    key_pos = jnp.arange(token_length, dtype=jnp.int32)

    def scores_of(first_row):
        query_rows = lax.dynamic_slice_in_dim(query_four, first_row, block_rows, 0)
        row_docs = lax.dynamic_slice_in_dim(document_line, first_row, block_rows, 0)
        row_pos = first_row + jnp.arange(block_rows, dtype=jnp.int32)
        allowed = (row_docs[:, None] == document_line[None, :]) & (
            key_pos[None, :] <= row_pos[:, None]
        )
        raw_scores = jnp.einsum(
            "qkgd,skd->kgqs", query_rows, key_three, preferred_element_type=F32
        )
        return (jnp.where(allowed[None, None], SCORE_MULT * raw_scores, MASKED), query_rows)

    def forward_block(running_totals, block_index):
        logits, query_rows = scores_of(block_index * block_rows)
        row_max = jnp.max(logits, axis=-1, keepdims=True)
        shifted = jnp.exp(logits - row_max)
        row_sum = jnp.sum(shifted, axis=-1, keepdims=True)
        probs_low = (shifted / row_sum).astype(BF)
        mixed_rows = jnp.einsum(
            "kgqs,skd->qkgd", probs_low, value_three, preferred_element_type=F32
        )
        log_total = row_max[..., 0] + jnp.log(row_sum[..., 0])
        return (running_totals, (mixed_rows.reshape(block_rows, -1).astype(BF), log_total))

    block_ids = jnp.arange(token_length // block_rows, dtype=jnp.int32)
    _, (attn_blocks, log_totals) = lax.scan(forward_block, 0, block_ids)

    def backward(d_heads):
        d_heads_four = d_heads.reshape(token_length, kv_dev, per_kv, HEAD_WIDTH)

        def backward_block(running_totals, block_items):
            d_key_sum, d_value_sum = running_totals
            block_index, log_total = block_items
            first_row = block_index * block_rows
            logits, query_rows = scores_of(first_row)
            probs = jnp.exp(logits - log_total[..., None])
            d_rows = lax.dynamic_slice_in_dim(d_heads_four, first_row, block_rows, 0)
            d_probs = jnp.einsum(
                "qkgd,skd->kgqs", d_rows, value_three, preferred_element_type=F32
            )
            inner = jnp.sum(probs * d_probs, axis=-1, keepdims=True)
            d_logits = (probs * (d_probs - inner)).astype(BF)
            d_query_rows = SCORE_MULT * jnp.einsum(
                "kgqs,skd->qkgd", d_logits, key_three, preferred_element_type=F32
            )
            d_key_sum = d_key_sum + SCORE_MULT * jnp.einsum(
                "kgqs,qkgd->skd", d_logits, query_rows, preferred_element_type=F32
            )
            d_value_sum = d_value_sum + jnp.einsum(
                "kgqs,qkgd->skd", probs.astype(BF), d_rows, preferred_element_type=F32
            )
            return (
                (d_key_sum, d_value_sum),
                d_query_rows.astype(BF).reshape(block_rows, -1),
            )

        zero_keys = jnp.zeros((token_length, kv_dev, HEAD_WIDTH), F32)
        (d_key_sum, d_value_sum), d_query_blocks = lax.scan(
            backward_block, (zero_keys, zero_keys), (block_ids, log_totals)
        )
        return (
            d_query_blocks.reshape(token_length, -1),
            d_key_sum.astype(BF).reshape(token_length, -1),
            d_value_sum.astype(BF).reshape(token_length, -1),
        )

    return attn_blocks.reshape(token_length, -1), backward


def rope(values, cos_tab, sin_tab):
    rows, width = values.shape
    heads = values.astype(F32).reshape(rows, width // HEAD_WIDTH, HEAD_WIDTH)
    return rotate(heads, cos_tab, sin_tab).astype(BF).reshape(rows, width)


def plain_attention(
    x, weights, la_q, la_k, la_v, exit_q, exit_k, exit_v, document_line, *_
):
    rows = x.shape[0]
    q_cols, kv_cols = exit_q.shape[1], exit_k.shape[1]
    projected = low_dot(x[:, : weights[0].shape[0]], weights[0])
    cos_tab, sin_tab = rope_tables(jnp.arange(rows, dtype=jnp.int32), HEAD_WIDTH)
    query_rot = rope(projected[:, :q_cols] + low_dot(la_q, exit_q), cos_tab, sin_tab)
    key_rot = rope(
        projected[:, q_cols : q_cols + kv_cols] + low_dot(la_k, exit_k), cos_tab, sin_tab
    )
    value_low = (projected[:, q_cols + kv_cols :] + low_dot(la_v, exit_v)).astype(BF)
    attended, attention_back = attention_forward(query_rot, key_rot, value_low, document_line)

    def backward(d_heads, *_):
        d_query, d_key, d_value = attention_back(d_heads)
        return rope(d_query, cos_tab, -sin_tab), rope(d_key, cos_tab, -sin_tab), d_value

    return attended, lambda: attended, backward


def layer(mover, args):
    (
        tokens,
        token_document,
        document_adapter,
        attention_norm_gain,
        feedforward_norm_gain,
        query_weight,
        key_weight,
        value_weight,
        output_weight,
        gate_weight,
        up_weight,
        down_weight,
        attention_down_maps,
        query_exit_maps,
        key_value_exit_maps,
        output_entry_maps,
        output_exit_maps,
        feedforward_entry_maps,
        feedforward_exit_maps,
        down_entry_maps,
        down_exit_maps,
        cotangent,
    ) = args
    seq_size, wsh_size, s = mover.seq_size, mover.wsh_size, mover.s
    own_rows = tokens.shape[1]
    width = tokens.shape[2]
    adapters = attention_down_maps.shape[1]
    rank = query_exit_maps.shape[1]
    flat = adapters * rank
    doc_count = document_adapter.shape[1]
    q_cols = query_weight.shape[1] // seq_size
    kv_cols = key_weight.shape[1] // seq_size
    feature = width // seq_size
    row_block = width // wsh_size
    hidden = gate_weight.shape[1]
    hid_block = hidden // (wsh_size * seq_size)
    hid_own = hidden // seq_size

    def owners(docs):
        hot = (docs[:, None] == jnp.arange(doc_count, dtype=jnp.int32)[None, :]).astype(jnp.int32)
        return jnp.sum(hot * document_adapter[0][None, :], axis=1)

    def turned(maps):
        return maps.transpose(1, 2, 0).reshape(-1, maps.shape[0])

    def own_hidden(values, lower=0, upper=hid_own):
        parts, at = [], lower
        while at < upper:
            w = at // hid_block
            stop = min(upper, (w + 1) * hid_block)
            start = (w * seq_size + s) * hid_block + at - w * hid_block
            parts.append(cut(values, start, stop - at, 1))
            at = stop
        return parts

    qkv_local = jnp.concatenate(
        [
            cut(query_weight, s * q_cols, q_cols, 1),
            cut(key_weight, s * kv_cols, kv_cols, 1),
            cut(value_weight, s * kv_cols, kv_cols, 1),
        ],
        axis=1,
    )
    local_docs = token_document[0]
    own_owner = owners(local_docs)
    hidden_state = tokens[0].astype(F32)
    first_normed, scale_one = normed(hidden_state, attention_norm_gain)
    first_normed = first_normed.astype(BF)
    input_maps = turned(attention_down_maps)
    picked_first = reverse_product(first_normed, input_maps)
    picked_first = picked_first * adapter_mask(own_owner, 3 * rank, adapters)
    picked_first = fold(picked_first, 3 * rank, 0)
    last_lane = jnp.arange(LANES, dtype=jnp.int32)[None, :] == LANES - 1
    picked_first = jnp.where(last_lane, local_docs.astype(F32)[:, None], picked_first).astype(BF)

    half_width = width // 2
    down_local = cut(down_weight, s * hid_block, hid_block, 0)
    if mover.fast:
        chunks = [(0, 1), (2, 3), (4, 5), (6,), (7,)]
    else:
        chunks = [tuple(range(wsh_size))]
    chunk_bounds = [(c[0] * hid_block, (c[-1] + 1) * hid_block) for c in chunks]

    def gate_up_far(i, *deps):
        gate_late, up_late = after((gate_weight, up_weight), *deps)
        parts = own_hidden(gate_late, *chunk_bounds[i]) + own_hidden(up_late, *chunk_bounds[i])
        return mover.far(jnp.concatenate(parts, axis=1))

    output_gradient = cotangent[0].astype(F32)
    d_mlp_local = (RESIDUAL_MULT * output_gradient).astype(BF)
    first_cols = jnp.concatenate([mover.to_slots(first_normed, row_block), picked_first], axis=1)
    qkv_pair = mover.far(qkv_local)
    if mover.fast:
        d_mlp_other = lax.ppermute(d_mlp_local, "seq", Y_SWAP)
        first_other = after(lax.ppermute(first_cols, "seq", Y_SWAP), d_mlp_other)
        out_piece = mover.head_rows(output_weight)
        qkv_four = mover.near(qkv_pair)
        out_pair = mover.far(out_piece, qkv_pair)
        qkv_full = mover.across(qkv_four)
        first_all = mover.gather_rest(first_cols, first_other)
        out_four = mover.near(out_pair, qkv_four)
        low_pair = mover.far(down_local[:, :half_width], qkv_four)
        out_swapped = mover.across(out_four, qkv_full[1])
        out_full = mover.head_rows_done(out_swapped, output_weight.shape[0])
        d_mlp = mover.gather_rest(d_mlp_local, after(d_mlp_other, first_all))
        low_four = mover.near(low_pair, out_four)
        high_pair = mover.far(down_local[:, half_width:], low_pair, qkv_full[1])
        first_all = after(first_all, d_mlp)
    else:
        qkv_full = mover.across(qkv_pair)
        first_all = mover.gather_tokens(first_cols)
        d_mlp = mover.gather_tokens(d_mlp_local)
        out_full = mover.head_rows(output_weight)
        down_full = mover.across(down_local)[0]
    document_line = first_all[:, width + LANES - 1].astype(jnp.int32)
    owner = owners(document_line)
    mask_rank = adapter_mask(owner, rank, adapters)

    (
        query_exit_maps,
        key_value_exit_maps,
    ) = after((query_exit_maps, key_value_exit_maps), first_normed)
    query_exit = cut(query_exit_maps.reshape(flat, -1), s * q_cols, q_cols, 1)
    key_exit = cut(key_value_exit_maps[0].reshape(flat, -1), s * kv_cols, kv_cols, 1)
    value_exit = cut(key_value_exit_maps[1].reshape(flat, -1), s * kv_cols, kv_cols, 1)
    la_one = first_all[:, width:]
    la_q = spread(la_one, owner, rank, 0, adapters)
    la_k = spread(la_one, owner, rank, rank, adapters)
    la_v = spread(la_one, owner, rank, 2 * rank, adapters)
    token_length = first_all.shape[0]
    attend = fast_attention if mover.fast else plain_attention
    early, attend_rest, attention_back = attend(
        first_all, qkv_full, la_q, la_k, la_v, query_exit, key_exit, value_exit, document_line,
    )

    (
        feedforward_entry_maps,
        feedforward_exit_maps,
        down_entry_maps,
        down_exit_maps,
        output_entry_maps,
        output_exit_maps,
    ) = after(
        (
            feedforward_entry_maps,
            feedforward_exit_maps,
            down_entry_maps,
            down_exit_maps,
            output_entry_maps,
            output_exit_maps,
        ),
        early,
    )
    if mover.fast:
        low_rows = low_four.shape[0] // 2
        low_early = after(low_four[:low_rows], out_swapped[1], early)
        low_other = [
            lax.ppermute(low_early, "wsh", X_SWAP),
            lax.ppermute(low_four[low_rows:], "wsh", X_SWAP),
        ]
        down_low = (low_four, jnp.concatenate(low_other, axis=0))
        high_four = mover.near(high_pair, low_four, early)
        attended = attend_rest(out_full, high_pair)
        chunk_pairs = [gate_up_far(0, high_four)]
        attended = after(attended, high_four, low_other[0])
        down_high = mover.across(high_four)
        chunk_fours = [mover.near(chunk_pairs[0], high_four)]
        chunk_pairs.append(gate_up_far(1, chunk_pairs[0]))
    else:
        attended = attend_rest()

    out_entry = cut(turned(output_entry_maps), s * q_cols, q_cols, 1)
    out_exit = output_exit_maps.reshape(flat, -1)
    la_out_part = fold(reverse_product(attended, out_entry) * mask_rank, rank, 0)
    attn_sum = mover.scatter_tokens(low_dot(attended, out_full), la_out_part)
    la_out_own = attn_sum[1].astype(BF)
    attention_path = attn_sum[0] + low_dot(
        spread(la_out_own, own_owner, rank, 0, adapters), out_exit
    )
    middle = hidden_state + RESIDUAL_MULT * attention_path
    if mover.fast:
        middle = after(middle, low_other[1], chunk_pairs[0])

    second_normed, scale_two = normed(middle, feedforward_norm_gain)
    second_normed = second_normed.astype(BF)
    entry_maps = turned(feedforward_entry_maps)
    picked_second = reverse_product(second_normed, entry_maps) * adapter_mask(
        own_owner, 2 * rank, adapters
    )
    picked_second = fold(picked_second, 2 * rank, rank) + la_out_own.astype(F32)
    second_cols = jnp.concatenate(
        [mover.to_slots(second_normed, row_block), picked_second.astype(BF)], axis=1
    )
    if mover.fast:
        second_other = lax.ppermute(second_cols, "seq", Y_SWAP)
        second_all = mover.gather_rest(
            second_cols, after(second_other, down_high[1], chunk_fours[0], chunk_pairs[1])
        )
    else:
        second_all = mover.gather_tokens(second_cols)
    la_out = spread(second_all[:, width:], owner, rank, 0, adapters)
    la_gate = spread(second_all[:, width:], owner, rank, rank, adapters)
    la_up = spread(second_all[:, width:], owner, rank, 2 * rank, adapters)

    down_exit = down_exit_maps.reshape(flat, -1)
    d_la_d = (reverse_product(d_mlp, down_exit) * mask_rank).astype(BF)
    down_entry = jnp.concatenate(own_hidden(turned(down_entry_maps)), axis=1)
    all_exits = feedforward_exit_maps.reshape(2, flat, -1)
    exits = [jnp.concatenate(own_hidden(all_exits[i]), axis=1) for i in range(2)]
    mixed_parts, gate_grads, up_grads, entry_grads = [], [], [], []
    if mover.fast:
        chunk_weights = [mover.across(chunk_fours[0])]
        sums = None
        for i, units in enumerate(chunks):
            if i + 1 < len(chunks):
                deps = [chunk_fours[i]] + ([] if sums is None else [sums[0]])
                chunk_fours.append(mover.near(chunk_pairs[i + 1], *deps))
                chunk_weights.append(mover.across(chunk_fours[i + 1]))
            if i + 2 < len(chunks):
                deps = [chunk_pairs[i + 1], down_high[1] if sums is None else sums[0]]
                chunk_pairs.append(gate_up_far(i + 2, *deps))
            lower, upper = chunk_bounds[i]
            units_in = after(second_all, *chunk_fours[i + 1 : i + 2], *chunk_pairs[i + 2 : i + 3])
            mixed, d_gate, d_up, *sums = mlp_call(
                units,
                mover.z_slot(units[0] // 2),
                mover.x,
                units_in,
                chunk_weights[i],
                la_gate,
                la_up,
                exits[0][:, lower:upper],
                exits[1][:, lower:upper],
                d_mlp,
                down_low,
                down_high,
                d_la_d,
                down_entry[:, lower:upper],
                sums,
            )
            mixed_parts.append(mixed)
            gate_grads.append(gradient_product(la_gate, d_gate))
            up_grads.append(gradient_product(la_up, d_up))
            entry_grads.append(gradient_product(d_la_d, mixed))
        d_second, d_la_both = sums
        d_la_gate, d_la_up = d_la_both[:, :flat], d_la_both[:, flat:]
    else:
        weights = mover.across(gate_up_far(0))[0]
        both = low_dot(second_all[:, :width], weights)
        gate = both[:, :hid_own] + low_dot(la_gate, exits[0])
        up = both[:, hid_own:] + low_dot(la_up, exits[1])
        d_mixed = reverse_product(d_mlp, down_full) + low_dot(d_la_d, down_entry)
        sigma = jax.nn.sigmoid(gate)
        swish = gate * sigma
        mixed = (swish * up).astype(BF)
        d_gate = (d_mixed * up * sigma * (1.0 + gate * (1.0 - sigma))).astype(BF)
        d_up = (d_mixed * swish).astype(BF)
        d_second = reverse_product(jnp.concatenate([d_gate, d_up], axis=1), weights)
        d_la_gate = reverse_product(d_gate, exits[0])
        d_la_up = reverse_product(d_up, exits[1])
        mixed_parts.append(mixed)
        gate_grads.append(gradient_product(la_gate, d_gate))
        up_grads.append(gradient_product(la_up, d_up))
        entry_grads.append(gradient_product(d_la_d, mixed))
    d_la_two_part = fold(d_la_gate * mask_rank, rank, 0) + fold(d_la_up * mask_rank, rank, rank)
    d_second_sum = mover.scatter_tokens(d_second, d_la_two_part)
    d_la_two_own = d_second_sum[1].astype(BF)
    d_second_own = mover.from_slots(d_second_sum[0], row_block) + low_dot(
        spread(d_la_two_own, own_owner, 2 * rank, 0, adapters), entry_maps
    )
    grad_middle = output_gradient + normed_back(
        middle, scale_two, feedforward_norm_gain, d_second_own
    )
    d_attn_own = (RESIDUAL_MULT * grad_middle).astype(BF)
    d_attn_all = mover.gather_tokens(jnp.concatenate([d_attn_own, d_la_two_own], axis=1))
    d_attn = d_attn_all[:, :width]
    gate_grad = jnp.concatenate(gate_grads, axis=1)
    up_grad = jnp.concatenate(up_grads, axis=1)
    down_in_grad = jnp.concatenate(entry_grads, axis=1)

    mixed_all = jnp.concatenate(mixed_parts, axis=1)
    la_down_part = fold(reverse_product(mixed_all, down_entry) * mask_rank, rank, 0)
    if mover.fast:
        mlp_part = mlp_out_call(
            chunks, [mover.z_slot(i) for i in range(4)], mover.x, mixed_parts, down_low, down_high
        )
    else:
        mlp_part = low_dot(mixed_all, down_full)
    mlp_sum = mover.scatter_tokens(mlp_part, la_down_part, deps=(d_attn_all,), mark="mlp")
    hidden_grads = mover.sum_hidden(
        [gate_grad, up_grad, down_in_grad], hid_block, (mover.marks.get("mlp"),), "hidden", (d_attn_all,)
    )
    hidden_sent = mover.marks.get("hidden", (None, None))
    la_down_own = mlp_sum[1].astype(BF)
    feedforward_path = mlp_sum[0] + low_dot(
        spread(la_down_own, own_owner, rank, 0, adapters), down_exit
    )
    layer_out = (middle + RESIDUAL_MULT * feedforward_path).astype(BF)[None]
    la_down = spread(mover.gather_tokens(la_down_own), owner, rank, 0, adapters)

    def own_features(slots):
        per = wsh_size // seq_size
        parts = [
            cut(slots, mover.slot_of(s * per + i) * row_block, row_block, 1) for i in range(per)
        ]
        return jnp.concatenate(parts, axis=1)

    d_la_two = spread(d_attn_all[:, width:], owner, 2 * rank, 0, adapters)
    entry_grad = gradient_product(d_la_two, own_features(second_all))
    down_out_grad = gradient_product(la_down, cut(d_mlp, s * feature, feature, 1))
    d_la_o = (reverse_product(d_attn, out_exit) * mask_rank).astype(BF)
    out_in_grad = gradient_product(d_la_o, attended)
    out_out_grad = gradient_product(la_out, cut(d_attn, s * feature, feature, 1))

    d_attended = (reverse_product(d_attn, out_full) + low_dot(d_la_o, out_entry)).astype(BF)
    d_query, d_key, d_value = attention_back(
        d_attended, (mover.marks.get("mlp"),), hidden_sent[:1]
    )
    d_la_one_part = (
        fold(reverse_product(d_query, query_exit) * mask_rank, rank, 0)
        + fold(reverse_product(d_key, key_exit) * mask_rank, rank, rank)
        + fold(reverse_product(d_value, value_exit) * mask_rank, rank, 2 * rank)
    )
    d_la_one = mover.sum_small(d_la_one_part.astype(BF)).astype(BF)
    d_qkv = jnp.concatenate([d_query, d_key, d_value], axis=1)
    d_qkv = after(d_qkv, d_la_one_part)
    d_first_sum = jnp.concatenate(
        mover.scatter_tokens(
            *[reverse_product(d_qkv, half) for half in qkv_full],
            deps=(d_la_one, hidden_sent[1]),
            late=hidden_grads,
        ),
        axis=1,
    )
    d_la_one_own = cut(d_la_one, s * own_rows, own_rows, 0)
    d_first = mover.from_slots(d_first_sum, row_block) + low_dot(
        spread(d_la_one_own, own_owner, 3 * rank, 0, adapters), input_maps
    )
    hidden_gradient = grad_middle + normed_back(
        hidden_state, scale_one, attention_norm_gain, d_first
    )
    attention_in_grad = gradient_product(
        spread(d_la_one, owner, 3 * rank, 0, adapters), own_features(first_all)
    )
    query_out_grad = gradient_product(la_q, d_query)
    key_out_grad = gradient_product(la_k, d_key)
    value_out_grad = gradient_product(la_v, d_value)
    last_grads = mover.sum_features(
        [attention_in_grad, query_out_grad, down_out_grad, entry_grad, out_in_grad, out_out_grad],
        key_out_grad,
        value_out_grad,
        (d_first_sum,),
    )

    def back(values, shape):
        return values.reshape(shape[1], shape[2], shape[0]).transpose(2, 0, 1)

    return (
        layer_out,
        hidden_gradient[None],
        back(last_grads[0], attention_down_maps.shape),
        last_grads[1].reshape(query_exit_maps.shape),
        last_grads[6].reshape(key_value_exit_maps.shape),
        back(last_grads[4], output_entry_maps.shape),
        last_grads[5].reshape(output_exit_maps.shape),
        back(last_grads[3], feedforward_entry_maps.shape),
        hidden_grads[0].reshape(feedforward_exit_maps.shape),
        back(hidden_grads[1], down_entry_maps.shape),
        last_grads[2].reshape(down_exit_maps.shape),
    )


def solution(mesh):
    seq_size, wsh_size = mesh.shape["seq"], mesh.shape["wsh"]

    def on_device(*args):
        return layer(Mover(seq_size, wsh_size), args)

    rows = P("wsh", None)
    stream = P("wsh", "seq", None)
    in_specs = (stream, P("wsh", "seq"), rows, P(), P()) + (rows,) * 7 + (P(),) * 9 + (stream,)
    out_specs = (stream, stream) + (P(),) * 9
    return jax.shard_map(
        on_device, mesh=mesh, in_specs=in_specs, out_specs=out_specs, check_vma=False
    )
```

```python
import jax
import jax.numpy as jnp
from jax import lax
from jax.experimental import pallas as pl
from jax.experimental.pallas import tpu as pltpu
from jax.sharding import PartitionSpec as P

QUERY_HEADS = 32
KEY_HEADS = 8
HEAD_WIDTH = 64
LANES = 128
PACK = 512
TILE = 256

EPSILON = 1e-05
RESIDUAL_MULT = 0.22
SCORE_MULT = 0.015625
ROPE_BASE = 10000000.0
MASKED = -1e30

BF = jnp.bfloat16
F32 = jnp.float32

CORE_SWAP = [(s, s ^ 1) for s in range(4)]
Y_SWAP = [(s, s ^ 2) for s in range(4)]
X_SWAP = [(w, w ^ 1) for w in range(8)]
NEAR_SWAP = [(w, w ^ 2) for w in range(8)]
FAR_SWAP = [(w, w ^ 4) for w in range(8)]


def z_shift(steps):
    return [(2 * z + x, 2 * ((z + steps) % 4) + x) for z in range(4) for x in range(2)]


def low_dot(left, right):
    return jnp.dot(left, right, preferred_element_type=F32)


def gradient_product(left, right):
    return lax.dot_general(left, right, (((0,), (0,)), ((), ())), preferred_element_type=F32)


def reverse_product(left, right):
    return lax.dot_general(left, right, (((1,), (1,)), ((), ())), preferred_element_type=F32)


def normed(values, gain):
    norm_scale = lax.rsqrt(jnp.mean(values * values, axis=-1, keepdims=True) + EPSILON)
    return (values * norm_scale * gain, norm_scale)


def normed_back(values, norm_scale, gain, grad_in):
    scaled = grad_in * gain
    cubed = norm_scale * norm_scale * norm_scale
    return norm_scale * scaled - values * cubed * jnp.mean(scaled * values, axis=-1, keepdims=True)


def rope_tables(positions, head_size):
    half_size = head_size // 2
    inv_freq = ROPE_BASE ** (-(jnp.arange(half_size).astype(F32) * 2.0) / head_size)
    angles = positions.astype(F32)[:, None] * inv_freq[None, :]
    return (jnp.cos(angles)[:, None, :], jnp.sin(angles)[:, None, :])


def rotate(values, cos_tab, sin_tab):
    half_size = values.shape[-1] // 2
    former = values[..., :half_size]
    latter = values[..., half_size:]
    return jnp.concatenate(
        [former * cos_tab - latter * sin_tab, latter * cos_tab + former * sin_tab], axis=-1
    )


def cut(values, start, size, axis):
    return lax.dynamic_slice_in_dim(values, start, size, axis)


def pick(values, index, axis):
    return lax.dynamic_index_in_dim(values, index, axis, keepdims=False)


def adapter_mask(owner, ranks, adapters):
    lane = jnp.arange(adapters * ranks, dtype=jnp.int32) // ranks
    return (owner[:, None] == lane[None, :]).astype(F32)


def fold(masked, ranks, offset):
    rows = jnp.arange(masked.shape[1], dtype=jnp.int32) % ranks
    lanes = jnp.arange(LANES, dtype=jnp.int32) - offset
    return low_dot(masked.astype(BF), (rows[:, None] == lanes[None, :]).astype(BF))


def spread(folded, owner, ranks, offset, adapters):
    rows = jnp.arange(LANES, dtype=jnp.int32) - offset
    lanes = jnp.arange(adapters * ranks, dtype=jnp.int32) % ranks
    wide = low_dot(folded.astype(BF), (rows[:, None] == lanes[None, :]).astype(BF))
    return (wide * adapter_mask(owner, ranks, adapters)).astype(BF)


def pack(values):
    parts = [values[:, i : i + PACK] for i in range(0, values.shape[1], PACK)]
    return jnp.concatenate(parts, axis=0)


def after(values, *deps):
    deps = [d for d in deps if d is not None]
    if not deps:
        return values
    return lax.optimization_barrier((values, tuple(deps)))[0]


class Mover:
    def __init__(self, seq_size, wsh_size):
        self.seq_size, self.wsh_size = seq_size, wsh_size
        self.fast = seq_size == 4 and wsh_size == 8
        self.s, self.w = lax.axis_index("seq"), lax.axis_index("wsh")
        self.y, self.c = self.s // 2, self.s % 2
        self.z, self.x = self.w // 2, self.w % 2
        self.marks = {}

    def far(self, chunk, *deps):
        chunk = after(chunk, *deps)
        if not self.fast:
            return chunk
        return jnp.concatenate([chunk, lax.ppermute(chunk, "wsh", FAR_SWAP)], axis=0)

    def near(self, pair, *deps):
        pair = after(pair, *deps)
        if not self.fast:
            return pair
        return jnp.concatenate([pair, lax.ppermute(pair, "wsh", NEAR_SWAP)], axis=0)

    def across(self, four, *deps):
        four = after(four, *deps)
        if not self.fast:
            return (lax.all_gather(four, "wsh", axis=0, tiled=True),)
        return four, lax.ppermute(four, "wsh", X_SWAP)

    def across_parts(self, four, *deps):
        rows = four.shape[0] // 2
        parts = [four[:rows], four[rows:]]
        parts = [lax.ppermute(after(v, *deps), "wsh", X_SWAP) for v in parts]
        return (four, jnp.concatenate(parts, axis=0)), parts

    def swap_bits(self, d):
        return d // 2 + 2 * (d % 2)

    def slot_owner(self, k):
        if not self.fast:
            return k
        return 2 * (self.z ^ self.swap_bits(k % 4)) + (self.x ^ (k // 4))

    def slot_of(self, w):
        if not self.fast:
            return w
        return self.z_slot(w // 2) + 4 * (self.x ^ (w % 2))

    def z_slot(self, z):
        return self.swap_bits(self.z ^ z)

    def to_slots(self, values, block):
        if not self.fast:
            return values
        parts = [cut(values, self.slot_owner(k) * block, block, 1) for k in range(self.wsh_size)]
        return jnp.concatenate(parts, axis=1)

    def from_slots(self, values, block):
        if not self.fast:
            return values
        parts = [cut(values, self.slot_of(w) * block, block, 1) for w in range(self.wsh_size)]
        return jnp.concatenate(parts, axis=1)

    def head_rows(self, weight):
        rows = weight.shape[0]
        per = self.wsh_size // self.seq_size
        if not self.fast:
            return cut(
                lax.all_gather(weight, "wsh", axis=0, tiled=True),
                self.s * per * rows,
                per * rows,
                0,
            )
        piece = rows // 4

        def part(z):
            return cut(weight, z * piece, piece, 0)

        def pairs(senders, step):
            return [
                (8 * s + 2 * (s ^ sender) + x, 8 * s + 2 * (s ^ sender ^ step) + x)
                for s in range(4)
                for sender in senders
                for x in range(2)
            ]

        z, axes = self.z, ("seq", "wsh")
        away = jnp.concatenate([part(z ^ 2), part(z ^ 3)], axis=0)
        got = lax.ppermute(away, axes, pairs((0,), 2))
        first = z == self.s
        mine = jnp.where(first, part(z), got[:piece])
        away = jnp.where(first, part(z ^ 1), got[piece:])
        got = lax.ppermute(away, axes, pairs((0, 2), 1))
        return jnp.where(first | (z == (self.s ^ 2)), mine, got)

    def head_rows_done(self, halves, rows):
        piece = rows // 4
        out = []
        for shard in range(2):
            half = jnp.where(self.x == shard, halves[0], halves[1])
            blocks = half.reshape(4, piece, half.shape[1])
            out += [pick(blocks, self.z_slot(j), 0) for j in range(4)]
        return jnp.concatenate(out, axis=0)

    def gather_tokens(self, values):
        if not self.fast:
            return lax.all_gather(values, "seq", axis=0, tiled=True)
        return self.gather_rest(values, lax.ppermute(values, "seq", Y_SWAP))

    def gather_rest(self, values, other):
        first = self.y == 0
        column = jnp.stack([jnp.where(first, values, other), jnp.where(first, other, values)])
        partner = lax.ppermute(column, "seq", CORE_SWAP)
        first = self.c == 0
        whole = jnp.stack(
            [jnp.where(first, column, partner), jnp.where(first, partner, column)], axis=1
        )
        return whole.reshape((4 * values.shape[0],) + values.shape[1:])

    def scatter_tokens(self, *partials, deps=(), late=(), mark=None):
        if not self.fast:
            return [
                lax.psum_scatter(v.astype(BF), "seq", scatter_dimension=0, tiled=True).astype(F32)
                for v in partials
            ]
        rows = partials[0].shape[0] // 4
        blocks = [v.reshape(2, 2, rows, v.shape[1]) for v in partials]
        out = jnp.concatenate([pick(v, 1 - self.c, 1).astype(BF) for v in blocks], axis=2)
        got = lax.ppermute(out, "seq", CORE_SWAP).astype(F32)
        mine = jnp.concatenate([pick(v, self.c, 1) for v in blocks], axis=2)
        away = (pick(mine, 1 - self.y, 0) + pick(got, 1 - self.y, 0)).astype(BF)
        other = lax.ppermute(after(away, *deps), "seq", Y_SWAP)
        self.marks[mark] = other
        if mark is not None:
            self.marks[mark + "_away"] = away
        other = after(other, *late).astype(F32)
        total = pick(mine, self.y, 0) + pick(got, self.y, 0) + other
        found, at = [], 0
        for v in partials:
            found.append(total[:, at : at + v.shape[1]])
            at += v.shape[1]
        return found

    def sum_small(self, partial, deps=()):
        if not self.fast:
            return lax.psum(partial, "seq")
        total = partial.astype(F32) + lax.ppermute(partial, "seq", CORE_SWAP).astype(F32)
        other = lax.ppermute(after(total.astype(BF), *deps), "seq", Y_SWAP)
        return total + other.astype(F32)

    def sum_plain(self, grad):
        total = lax.psum(grad.astype(BF), "wsh")
        return lax.all_gather(total.astype(BF), "seq", axis=0).astype(F32)

    def plain_hidden(self, grads, hid_block):
        found = []
        for grad in grads:
            rows = grad.shape[0]
            wide = self.sum_plain(grad).reshape(self.seq_size, rows, self.wsh_size, hid_block)
            found.append(wide.transpose(1, 2, 0, 3).reshape(rows, -1))
        return [jnp.stack(found[:2]), found[2]]

    def sum_hidden(self, half, deps, mark, early):
        parts = self.sum_end(half, deps, mark, early)
        s = self.s.astype(jnp.int32)[None]
        return [
            final_hidden(parts, s, 0, 2),
            final_hidden(parts, s, 8 * LANES, 1)[0],
        ]

    def sum_features(self, grads, key=None, value=None, mid=(), deps=()):
        if not self.fast:
            grads = grads + ([key, value] if key is not None else [])
            found = []
            for grad in grads:
                found.append(self.sum_plain(grad).transpose(1, 0, 2).reshape(grad.shape[0], -1))
            return found[:-2] + [jnp.stack(found[-2:])] if key is not None else found
        packed = list(grads)
        if key is not None:
            rest = jnp.zeros((key.shape[0], PACK - 2 * LANES), F32)
            packed.append(jnp.concatenate([key, value, rest], axis=1))
        parts = self.sum_end(self.sum_start(jnp.concatenate(packed, axis=0), mid), deps)
        s = self.s.astype(jnp.int32)[None]
        found, at = [], 0
        for grad in grads:
            found.append(final_features(parts, s, at, grad.shape[0]))
            at += grad.shape[0]
        if key is not None:
            found.append(final_kv(parts, s, at))
        return found

    def sum_start(self, packed, mid=()):
        rows = packed.shape[0]
        halves = packed.reshape(2, rows // 2, PACK)
        got = lax.ppermute(pick(halves, 1 - self.x, 0).astype(BF), "wsh", X_SWAP)
        half = pick(halves, self.x, 0) + got.astype(F32)
        blocks = after(half, *mid).reshape(4, rows // 8, PACK)
        total = pick(blocks, self.z, 0)
        for r in range(1, 4):
            out = pick(blocks, (self.z + r) % 4, 0).astype(BF)
            total = total + lax.ppermute(out, "wsh", z_shift(r)).astype(F32)
        own = total.astype(BF)
        got = [own] + [lax.ppermute(own, "wsh", z_shift(r)) for r in range(1, 4)]
        ring = jnp.stack(got)
        return jnp.concatenate([pick(ring, (self.z - j) % 4, 0) for j in range(4)], axis=0)

    def sum_end(self, half, deps=(), mark=None, early=()):
        rows = 2 * half.shape[0]
        half = after(half, *early)
        other = lax.ppermute(half, "wsh", X_SWAP)
        first = self.x == 0
        part = jnp.concatenate([jnp.where(first, half, other), jnp.where(first, other, half)])
        core = lax.ppermute(part, "seq", CORE_SWAP)
        if mark is None:
            other = lax.ppermute(after(part, *deps), "seq", Y_SWAP)
        else:
            top = lax.ppermute(after(part[: rows // 2], *deps), "seq", Y_SWAP)
            rest = lax.ppermute(after(part[rows // 2 :], top), "seq", Y_SWAP)
            self.marks[mark] = (top, rest)
            other = jnp.concatenate([top, rest], axis=0)
        return part, core, other, lax.ppermute(other, "seq", CORE_SWAP)


def final_body(s_ref, own, core, other, last, out_ref):
    columns = own.shape[-1]
    for k in range(4):
        place = s_ref[0] ^ k
        low = jnp.where(place % 2 == 0, own[...], core[...])
        high = jnp.where(place % 2 == 0, other[...], last[...])
        value = jnp.where(place < 2, low, high).astype(F32)
        at = slice(k * columns, (k + 1) * columns)
        if len(out_ref.shape) == 3:
            out_ref[0, :, at] = value
        else:
            out_ref[:, at] = value


def final_call(parts, s, grid, part_block, part_map, out_shape, out_block, out_map):
    return pl.pallas_call(
        final_body,
        grid_spec=pltpu.PrefetchScalarGridSpec(
            num_scalar_prefetch=1,
            grid=grid,
            in_specs=[pl.BlockSpec(part_block, part_map)] * 4,
            out_specs=pl.BlockSpec(out_block, out_map),
        ),
        out_shape=jax.ShapeDtypeStruct(out_shape, F32),
        name="finish",
    )(s, *parts)


def final_features(parts, s, row, rows):
    at = row // LANES
    return final_call(
        parts,
        s,
        (rows // LANES,),
        (LANES, PACK),
        lambda i, _: (at + i, 0),
        (rows, 4 * PACK),
        (LANES, 4 * PACK),
        lambda i, _: (i, 0),
    )


def final_hidden(parts, s, row, count):
    at = row // LANES
    return final_call(
        parts,
        s,
        (count, 8),
        (LANES, TILE),
        lambda n, w, _: (at + 4 * n + w // 2, w % 2),
        (count, LANES, 32 * TILE),
        (1, LANES, 4 * TILE),
        lambda n, w, _: (n, 0, w),
    )


def final_kv(parts, s, row):
    at = row // LANES
    return final_call(
        parts,
        s,
        (2,),
        (LANES, LANES),
        lambda n, _: (at, n),
        (2, LANES, 4 * LANES),
        (1, LANES, 4 * LANES),
        lambda n, _: (n, 0, 0),
    )


def half_lanes(rows, half):
    lane = lax.broadcasted_iota(jnp.int32, (rows, LANES), 1)
    return (lane < HEAD_WIDTH) if half == 0 else (lane >= HEAD_WIDTH)


def turn(values, cos_tab, sin_tab):
    lane = lax.broadcasted_iota(jnp.int32, values.shape, 1)
    swapped = jnp.where(
        lane % HEAD_WIDTH < HEAD_WIDTH // 2,
        pltpu.roll(values, LANES - HEAD_WIDTH // 2, 1),
        pltpu.roll(values, HEAD_WIDTH // 2, 1),
    )
    return values * cos_tab + swapped * sin_tab


def twice(values, half):
    other = pltpu.roll(values, HEAD_WIDTH, 1)
    first = half_lanes(values.shape[0], 0)
    return jnp.where(first, values, other) if half == 0 else jnp.where(first, other, values)


def qkv_body(x_ref, w_own, w_other, la_q, la_k, la_v, exit_q, exit_kv, cos_ref, sin_ref, q_ref, k_ref, v_ref):
    cos_tab, sin_tab = cos_ref[...], sin_ref[...]
    half = w_own.shape[0]
    product = low_dot(x_ref[:, :half], w_own[...]) + low_dot(x_ref[:, half:], w_other[...])
    q_cols = q_ref.shape[1]
    query = product[:, :q_cols] + low_dot(la_q[...], exit_q[...])
    for i in range(0, q_cols, LANES):
        q_ref[:, i : i + LANES] = turn(query[:, i : i + LANES], cos_tab, sin_tab).astype(BF)
    key = product[:, q_cols : q_cols + LANES] + low_dot(la_k[...], exit_kv[0])
    key = turn(key, cos_tab, sin_tab)
    value = product[:, q_cols + LANES :] + low_dot(la_v[...], exit_kv[1])
    for half in range(2):
        k_ref[:, half * LANES : (half + 1) * LANES] = twice(key, half).astype(BF)
        v_ref[:, half * LANES : (half + 1) * LANES] = twice(value, half).astype(BF)


def qkv_call(x, weights, la_q, la_k, la_v, exit_q, exit_kv, cos_tab, sin_tab):
    rows, width = x.shape[0], 2 * weights[0].shape[0]
    q_cols = exit_q.shape[1]

    def tile(columns):
        return pl.BlockSpec((TILE, columns), lambda i: (i, 0))

    return pl.pallas_call(
        qkv_body,
        grid=(rows // TILE,),
        in_specs=[
            tile(width),
            pl.BlockSpec(weights[0].shape, lambda i: (0, 0)),
            pl.BlockSpec(weights[1].shape, lambda i: (0, 0)),
            tile(LANES),
            tile(LANES),
            tile(LANES),
            pl.BlockSpec(exit_q.shape, lambda i: (0, 0)),
            pl.BlockSpec(exit_kv.shape, lambda i: (0, 0, 0)),
            tile(LANES),
            tile(LANES),
        ],
        out_specs=[tile(q_cols), tile(2 * LANES), tile(2 * LANES)],
        out_shape=[
            jax.ShapeDtypeStruct((rows, q_cols), BF),
            jax.ShapeDtypeStruct((rows, 2 * LANES), BF),
            jax.ShapeDtypeStruct((rows, 2 * LANES), BF),
        ],
        name="qkv",
        cost_estimate=pl.CostEstimate(
            flops=2 * rows * width * weights[0].shape[1], bytes_accessed=12 << 20, transcendentals=0
        ),
    )(x, *weights, la_q, la_k, la_v, exit_q, exit_kv, cos_tab, sin_tab)


def allowed_pairs(i, t, doc_col, doc_row):
    start = pl.multiple_of(t * TILE, TILE)
    rows = i * TILE + lax.broadcasted_iota(jnp.int32, (TILE, TILE), 0)
    keys = start + lax.broadcasted_iota(jnp.int32, (TILE, TILE), 1)
    return (doc_col[...] == doc_row[:, pl.ds(start, TILE)]) & (keys <= rows)


def forward_body(first_ref, q_ref, k_ref, v_ref, doc_col, doc_row, o_ref, lse_ref, m_s, l_s, acc_s):
    i = pl.program_id(0)
    m_s[...] = jnp.full_like(m_s, MASKED)
    l_s[...] = jnp.zeros_like(l_s)
    acc_s[...] = jnp.zeros_like(acc_s)

    def step(t, carry):
        allowed = allowed_pairs(i, t, doc_col, doc_row)
        start = pl.multiple_of(t * TILE, TILE)
        keys, vals = k_ref[pl.ds(start, TILE), :], v_ref[pl.ds(start, TILE), :]
        for h in range(4):
            pair = q_ref[:, (h // 2) * LANES : (h // 2 + 1) * LANES]
            query = jnp.where(half_lanes(TILE, h % 2), pair, jnp.zeros_like(pair))
            logits = jnp.where(allowed, SCORE_MULT * reverse_product(query, keys), MASKED)
            old = m_s[h]
            top = jnp.maximum(old, jnp.max(logits, axis=1, keepdims=True))
            shrink = jnp.exp(old - top)
            shifted = jnp.exp(logits - top)
            m_s[h] = top
            l_s[h] = l_s[h] * shrink + jnp.sum(shifted, axis=1, keepdims=True)
            acc_s[h] = acc_s[h] * shrink + low_dot(shifted.astype(BF), vals)
        return carry

    lax.fori_loop(first_ref[i], i + 1, step, 0)
    lane = lax.broadcasted_iota(jnp.int32, (TILE, LANES), 1)
    total = jnp.zeros((TILE, LANES), F32)
    for p in range(2):
        both = [acc_s[2 * p + n] / l_s[2 * p + n] for n in range(2)]
        o_ref[:, p * LANES : (p + 1) * LANES] = jnp.where(
            half_lanes(TILE, 0), both[0], both[1]
        ).astype(BF)
    for h in range(4):
        total = jnp.where(lane == h, m_s[h] + jnp.log(l_s[h]), total)
    lse_ref[...] = total


def attention_call(j, first, query, keys, values, doc_col, doc_row):
    rows = query.shape[0]
    group = query.shape[1] // 2
    return pl.pallas_call(
        forward_body,
        grid_spec=pltpu.PrefetchScalarGridSpec(
            num_scalar_prefetch=1,
            grid=(rows // TILE,),
            in_specs=[
                pl.BlockSpec((TILE, group), lambda i, _: (i, j)),
                pl.BlockSpec((rows, LANES), lambda i, _: (0, j)),
                pl.BlockSpec((rows, LANES), lambda i, _: (0, j)),
                pl.BlockSpec((TILE, 1), lambda i, _: (i, 0)),
                pl.BlockSpec((1, rows), lambda i, _: (0, 0)),
            ],
            out_specs=[
                pl.BlockSpec((TILE, group), lambda i, _: (i, 0)),
                pl.BlockSpec((TILE, LANES), lambda i, _: (i, 0)),
            ],
            scratch_shapes=[
                pltpu.VMEM((4, TILE, 1), F32),
                pltpu.VMEM((4, TILE, 1), F32),
                pltpu.VMEM((4, TILE, LANES), F32),
            ],
        ),
        out_shape=[
            jax.ShapeDtypeStruct((rows, group), BF),
            jax.ShapeDtypeStruct((rows, LANES), F32),
        ],
        name="attention",
        cost_estimate=pl.CostEstimate(
            flops=4 * 4 * rows * rows * LANES,
            bytes_accessed=3 << 20,
            transcendentals=4 * rows * rows,
        ),
    )(first, query, keys, values, doc_col, doc_row)


def backward_body(
    first_ref, q_ref, k_ref, v_ref, do_ref, o_ref, lse_ref, doc_col, doc_row, cos_ref, sin_ref,
    cos_all, sin_all, dq_ref, dk_ref, dv_ref, dq_s, dk_s, dv_s,
):
    i = pl.program_id(0)

    @pl.when(i == 0)
    def _():
        dk_s[...] = jnp.zeros_like(dk_s)
        dv_s[...] = jnp.zeros_like(dv_s)

    dq_s[...] = jnp.zeros_like(dq_s)
    queries, grads, deltas = [], [], []
    for h in range(4):
        at = slice((h // 2) * LANES, (h // 2 + 1) * LANES)
        half = half_lanes(TILE, h % 2)
        pair, grad = q_ref[:, at], do_ref[:, at]
        queries.append(jnp.where(half, pair, jnp.zeros_like(pair)))
        grads.append(jnp.where(half, grad, jnp.zeros_like(grad)))
        product = grads[h].astype(F32) * o_ref[:, at].astype(F32)
        deltas.append(jnp.sum(product, axis=1, keepdims=True))

    def step(t, carry):
        allowed = allowed_pairs(i, t, doc_col, doc_row)
        start = pl.multiple_of(t * TILE, TILE)
        at = pl.ds(start, TILE)
        keys, vals = k_ref[at, :], v_ref[at, :]
        dk, dv = dk_s[at, :], dv_s[at, :]
        for h in range(4):
            logits = jnp.where(allowed, SCORE_MULT * reverse_product(queries[h], keys), MASKED)
            probs = jnp.exp(logits - lse_ref[:, h : h + 1])
            d_probs = reverse_product(grads[h], vals)
            d_logits = (probs * (d_probs - deltas[h])).astype(BF)
            dq_s[h] = dq_s[h] + low_dot(d_logits, keys)
            dk = dk + gradient_product(d_logits, queries[h])
            dv = dv + gradient_product(probs.astype(BF), grads[h])
        dk_s[at, :] = dk
        dv_s[at, :] = dv
        return carry

    lax.fori_loop(first_ref[i], i + 1, step, 0)
    for p in range(2):
        both = jnp.where(half_lanes(TILE, 0), dq_s[2 * p], dq_s[2 * p + 1])
        both = (SCORE_MULT * both).astype(BF).astype(F32)
        dq_ref[:, p * LANES : (p + 1) * LANES] = turn(both, cos_ref[...], -sin_ref[...]).astype(BF)

    @pl.when(i == pl.num_programs(0) - 1)
    def _():
        def finish(t, carry):
            at = pl.ds(pl.multiple_of(t * TILE, TILE), TILE)
            dk, dv = dk_s[at, :], dv_s[at, :]
            dk = (SCORE_MULT * (dk + pltpu.roll(dk, HEAD_WIDTH, 1))).astype(BF).astype(F32)
            dk_ref[at, :] = turn(dk, cos_all[at, :], -sin_all[at, :]).astype(BF)
            dv_ref[at, :] = (dv + pltpu.roll(dv, HEAD_WIDTH, 1)).astype(BF)
            return carry

        lax.fori_loop(0, pl.num_programs(0), finish, 0)


def attention_back_call(
    j, first, query, keys, values, d_out, out, lse, doc_col, doc_row, cos_tab, sin_tab
):
    rows = query.shape[0]
    group = query.shape[1] // 2
    whole = pl.BlockSpec((rows, LANES), lambda i, _: (0, j))
    tile = pl.BlockSpec((TILE, group), lambda i, _: (i, j))
    table = pl.BlockSpec((TILE, LANES), lambda i, _: (i, 0))
    table_all = pl.BlockSpec((rows, LANES), lambda i, _: (0, 0))
    own_tile = pl.BlockSpec((TILE, group), lambda i, _: (i, 0))
    return pl.pallas_call(
        backward_body,
        grid_spec=pltpu.PrefetchScalarGridSpec(
            num_scalar_prefetch=1,
            grid=(rows // TILE,),
            in_specs=[
                tile,
                whole,
                whole,
                tile,
                own_tile,
                table,
                pl.BlockSpec((TILE, 1), lambda i, _: (i, 0)),
                pl.BlockSpec((1, rows), lambda i, _: (0, 0)),
                table,
                table,
                table_all,
                table_all,
            ],
            out_specs=[own_tile, table_all, table_all],
            scratch_shapes=[
                pltpu.VMEM((4, TILE, LANES), F32),
                pltpu.VMEM((rows, LANES), F32),
                pltpu.VMEM((rows, LANES), F32),
            ],
        ),
        out_shape=[
            jax.ShapeDtypeStruct((rows, group), BF),
            jax.ShapeDtypeStruct((rows, LANES), BF),
            jax.ShapeDtypeStruct((rows, LANES), BF),
        ],
        name="attention_back",
        cost_estimate=pl.CostEstimate(
            flops=4 * 10 * rows * rows * LANES,
            bytes_accessed=5 << 20,
            transcendentals=4 * rows * rows,
        ),
    )(first, query, keys, values, d_out, out, lse, doc_col, doc_row, cos_tab, sin_tab, cos_tab, sin_tab)


def fast_attention(
    x, weights, la_q, la_k, la_v, exit_q, exit_k, exit_v, document_line
):
    rows = x.shape[0]
    half = HEAD_WIDTH // 2
    cos_tab, sin_tab = rope_tables(jnp.arange(rows, dtype=jnp.int32), HEAD_WIDTH)
    cos_tab = jnp.tile(cos_tab.reshape(rows, half), (1, 4))
    sin_tab = sin_tab.reshape(rows, half)
    sin_tab = jnp.tile(jnp.concatenate([-sin_tab, sin_tab], axis=1), (1, 2))
    first_docs = document_line[::TILE]
    first = jnp.sum((document_line[None, :] < first_docs[:, None]).astype(jnp.int32), axis=1)
    first = first // TILE
    doc_col, doc_row = document_line[:, None], document_line[None, :]
    query, keys, values = qkv_call(
        x, weights, la_q, la_k, la_v, exit_q, jnp.stack([exit_k, exit_v]), cos_tab, sin_tab
    )
    early = attention_call(0, first, query, keys, values, doc_col, doc_row)
    found = [early]

    def finish(*deps):
        query_late = after(query, early[0], *deps)
        found.append(attention_call(1, first, query_late, keys, values, doc_col, doc_row))
        return jnp.concatenate([early[0], found[1][0]], axis=1)

    def backward(d_heads, between, behind):
        back = []
        for j in range(2):
            if j:
                d_heads = after(d_heads, back[0][1], *between)
            args = (first, query, keys, values, d_heads, *found[j], doc_col, doc_row)
            back.append(attention_back_call(j, *args, cos_tab, sin_tab))
        back[1] = after(back[1], *behind)
        lane = jnp.arange(LANES, dtype=jnp.int32)[None, :] < HEAD_WIDTH
        d_query = jnp.concatenate([back[0][0], back[1][0]], axis=1)
        d_key = jnp.where(lane, back[0][1], back[1][1])
        d_value = jnp.where(lane, back[0][2], back[1][2])
        return d_query, d_key, d_value

    return early[0], finish, backward


def units_rows(at_own, own, other):
    return jnp.where(at_own, own[...], other[...])


def mlp_body(owners, add, sc, n2, w_own, w_other, la_gate, la_up, exit_gate, exit_up, d_mlp,
             low_own, low_other, high_own, high_other, d_la_d, entry, *rest):
    if add:
        sum_in, la_in, mixed_ref, gate_ref, up_ref, sum_ref, la_ref = rest
    else:
        mixed_ref, gate_ref, up_ref, sum_ref, la_ref = rest
    half = w_own.shape[0]
    size = TILE * len(owners)
    both = low_dot(n2[:, :half], w_own[...]) + low_dot(n2[:, half:], w_other[...])
    gate = both[:, :size] + low_dot(la_gate[...], exit_gate[...])
    up = both[:, size:] + low_dot(la_up[...], exit_up[...])
    parts = []
    for w in owners:
        at_own = sc[1] == w % 2
        parts.append(
            reverse_product(d_mlp[:, :half], units_rows(at_own, low_own, low_other))
            + reverse_product(d_mlp[:, half:], units_rows(at_own, high_own, high_other))
        )
    d_mixed = jnp.concatenate(parts, axis=1) + low_dot(d_la_d[...], entry[...])
    sigma = jax.nn.sigmoid(gate)
    swish = gate * sigma
    mixed_ref[...] = (swish * up).astype(BF)
    d_gate = (d_mixed * up * sigma * (1.0 + gate * (1.0 - sigma))).astype(BF)
    d_up = (d_mixed * swish).astype(BF)
    gate_ref[...] = d_gate
    up_ref[...] = d_up
    d_both = jnp.concatenate([d_gate, d_up], axis=1)
    sum_own, sum_other = reverse_product(d_both, w_own[...]), reverse_product(d_both, w_other[...])
    back_gate, back_up = reverse_product(d_gate, exit_gate[...]), reverse_product(d_up, exit_up[...])
    if add:
        sum_own, sum_other = sum_own + sum_in[:, :half], sum_other + sum_in[:, half:]
        back_gate, back_up = back_gate + la_in[:, :LANES], back_up + la_in[:, LANES:]
    sum_ref[:, :half] = sum_own
    sum_ref[:, half:] = sum_other
    la_ref[:, :LANES] = back_gate
    la_ref[:, LANES:] = back_up


def mlp_call(owners, block, x, n2, weights, la_gate, la_up, exit_gate, exit_up, d_mlp, low, high,
             d_la_d, entry, sums):
    rows = d_mlp.shape[0]
    half = weights[0].shape[0]
    size = TILE * len(owners)

    def tile(columns):
        return pl.BlockSpec((TILE, columns), lambda t, _: (t, 0))

    def whole(array):
        return pl.BlockSpec(array.shape, lambda t, _: (0, 0))

    units = pl.BlockSpec((TILE, half), lambda t, sc: (sc[0], 0))
    args = [n2, *weights, la_gate, la_up, exit_gate, exit_up, d_mlp, *low, *high, d_la_d, entry]
    in_specs = [tile(2 * half), whole(weights[0]), whole(weights[1]), tile(LANES), tile(LANES)]
    in_specs += [whole(exit_gate), whole(exit_up), tile(2 * half)] + [units] * 4
    in_specs += [tile(LANES), whole(entry)]
    aliases = {}
    if sums is not None:
        aliases = {1 + len(args): 3, 2 + len(args): 4}
        args += sums
        in_specs += [tile(2 * half), tile(2 * LANES)]
    return pl.pallas_call(
        lambda *refs: mlp_body(owners, sums is not None, *refs),
        grid_spec=pltpu.PrefetchScalarGridSpec(
            num_scalar_prefetch=1,
            grid=(rows // TILE,),
            in_specs=in_specs,
            out_specs=[tile(size)] * 3 + [tile(2 * half), tile(2 * LANES)],
        ),
        out_shape=[jax.ShapeDtypeStruct((rows, size), BF)] * 3
        + [
            jax.ShapeDtypeStruct((rows, 2 * half), F32),
            jax.ShapeDtypeStruct((rows, 2 * LANES), F32),
        ],
        input_output_aliases=aliases,
        name="units",
        cost_estimate=pl.CostEstimate(
            flops=20 * rows * half * size, bytes_accessed=32 << 20, transcendentals=rows * size
        ),
    )(jnp.stack([block, x]).astype(jnp.int32), *args)


def mlp_out_body(chunks, sc, *refs):
    mixed = refs[: len(chunks)]
    low_own, low_other, high_own, high_other, out_ref = refs[len(chunks) :]
    half = low_own.shape[1]
    low = high = None
    for (owners, ref) in zip(chunks, mixed):
        for n, w in enumerate(owners):
            at = pl.ds(pl.multiple_of(sc[w // 2] * TILE, TILE), TILE)
            at_own = sc[4] == w % 2
            part = ref[:, n * TILE : (n + 1) * TILE]
            more_low = low_dot(part, jnp.where(at_own, low_own[at, :], low_other[at, :]))
            more_high = low_dot(part, jnp.where(at_own, high_own[at, :], high_other[at, :]))
            low = more_low if low is None else low + more_low
            high = more_high if high is None else high + more_high
    out_ref[:, :half] = low
    out_ref[:, half:] = high


def mlp_out_call(chunks, z_slots, x, mixed, low, high):
    rows, half = mixed[0].shape[0], low[0].shape[1]
    places = jnp.stack([*z_slots, x]).astype(jnp.int32)
    return pl.pallas_call(
        lambda *refs: mlp_out_body(chunks, *refs),
        grid_spec=pltpu.PrefetchScalarGridSpec(
            num_scalar_prefetch=1,
            grid=(rows // TILE,),
            in_specs=[pl.BlockSpec((TILE, m.shape[1]), lambda t, _: (t, 0)) for m in mixed]
            + [pl.BlockSpec(low[0].shape, lambda t, _: (0, 0))] * 4,
            out_specs=pl.BlockSpec((TILE, 2 * half), lambda t, _: (t, 0)),
        ),
        out_shape=jax.ShapeDtypeStruct((rows, 2 * half), F32),
        name="units_out",
        cost_estimate=pl.CostEstimate(
            flops=4 * rows * half * 8 * TILE, bytes_accessed=20 << 20, transcendentals=0
        ),
    )(places, *mixed, *low, *high)


def attention_forward(query_heads, key_heads, value_heads, document_line):
    token_length = query_heads.shape[0]
    kv_dev = key_heads.shape[1] // HEAD_WIDTH
    per_kv = query_heads.shape[1] // key_heads.shape[1]
    block_rows = min(512, token_length)
    query_four = query_heads.reshape(token_length, kv_dev, per_kv, HEAD_WIDTH)
    key_three = key_heads.reshape(token_length, kv_dev, HEAD_WIDTH)
    value_three = value_heads.reshape(token_length, kv_dev, HEAD_WIDTH)
    key_pos = jnp.arange(token_length, dtype=jnp.int32)

    def scores_of(first_row):
        query_rows = lax.dynamic_slice_in_dim(query_four, first_row, block_rows, 0)
        row_docs = lax.dynamic_slice_in_dim(document_line, first_row, block_rows, 0)
        row_pos = first_row + jnp.arange(block_rows, dtype=jnp.int32)
        allowed = (row_docs[:, None] == document_line[None, :]) & (
            key_pos[None, :] <= row_pos[:, None]
        )
        raw_scores = jnp.einsum(
            "qkgd,skd->kgqs", query_rows, key_three, preferred_element_type=F32
        )
        return (jnp.where(allowed[None, None], SCORE_MULT * raw_scores, MASKED), query_rows)

    def forward_block(running_totals, block_index):
        logits, query_rows = scores_of(block_index * block_rows)
        row_max = jnp.max(logits, axis=-1, keepdims=True)
        shifted = jnp.exp(logits - row_max)
        row_sum = jnp.sum(shifted, axis=-1, keepdims=True)
        probs_low = (shifted / row_sum).astype(BF)
        mixed_rows = jnp.einsum(
            "kgqs,skd->qkgd", probs_low, value_three, preferred_element_type=F32
        )
        log_total = row_max[..., 0] + jnp.log(row_sum[..., 0])
        return (running_totals, (mixed_rows.reshape(block_rows, -1).astype(BF), log_total))

    block_ids = jnp.arange(token_length // block_rows, dtype=jnp.int32)
    _, (attn_blocks, log_totals) = lax.scan(forward_block, 0, block_ids)

    def backward(d_heads):
        d_heads_four = d_heads.reshape(token_length, kv_dev, per_kv, HEAD_WIDTH)

        def backward_block(running_totals, block_items):
            d_key_sum, d_value_sum = running_totals
            block_index, log_total = block_items
            first_row = block_index * block_rows
            logits, query_rows = scores_of(first_row)
            probs = jnp.exp(logits - log_total[..., None])
            d_rows = lax.dynamic_slice_in_dim(d_heads_four, first_row, block_rows, 0)
            d_probs = jnp.einsum(
                "qkgd,skd->kgqs", d_rows, value_three, preferred_element_type=F32
            )
            inner = jnp.sum(probs * d_probs, axis=-1, keepdims=True)
            d_logits = (probs * (d_probs - inner)).astype(BF)
            d_query_rows = SCORE_MULT * jnp.einsum(
                "kgqs,skd->qkgd", d_logits, key_three, preferred_element_type=F32
            )
            d_key_sum = d_key_sum + SCORE_MULT * jnp.einsum(
                "kgqs,qkgd->skd", d_logits, query_rows, preferred_element_type=F32
            )
            d_value_sum = d_value_sum + jnp.einsum(
                "kgqs,qkgd->skd", probs.astype(BF), d_rows, preferred_element_type=F32
            )
            return (
                (d_key_sum, d_value_sum),
                d_query_rows.astype(BF).reshape(block_rows, -1),
            )

        zero_keys = jnp.zeros((token_length, kv_dev, HEAD_WIDTH), F32)
        (d_key_sum, d_value_sum), d_query_blocks = lax.scan(
            backward_block, (zero_keys, zero_keys), (block_ids, log_totals)
        )
        return (
            d_query_blocks.reshape(token_length, -1),
            d_key_sum.astype(BF).reshape(token_length, -1),
            d_value_sum.astype(BF).reshape(token_length, -1),
        )

    return attn_blocks.reshape(token_length, -1), backward


def rope(values, cos_tab, sin_tab):
    rows, width = values.shape
    heads = values.astype(F32).reshape(rows, width // HEAD_WIDTH, HEAD_WIDTH)
    return rotate(heads, cos_tab, sin_tab).astype(BF).reshape(rows, width)


def plain_attention(
    x, weights, la_q, la_k, la_v, exit_q, exit_k, exit_v, document_line, *_
):
    rows = x.shape[0]
    q_cols, kv_cols = exit_q.shape[1], exit_k.shape[1]
    projected = low_dot(x[:, : weights[0].shape[0]], weights[0])
    cos_tab, sin_tab = rope_tables(jnp.arange(rows, dtype=jnp.int32), HEAD_WIDTH)
    query_rot = rope(projected[:, :q_cols] + low_dot(la_q, exit_q), cos_tab, sin_tab)
    key_rot = rope(
        projected[:, q_cols : q_cols + kv_cols] + low_dot(la_k, exit_k), cos_tab, sin_tab
    )
    value_low = (projected[:, q_cols + kv_cols :] + low_dot(la_v, exit_v)).astype(BF)
    attended, attention_back = attention_forward(query_rot, key_rot, value_low, document_line)

    def backward(d_heads, *_):
        d_query, d_key, d_value = attention_back(d_heads)
        return rope(d_query, cos_tab, -sin_tab), rope(d_key, cos_tab, -sin_tab), d_value

    return attended, lambda: attended, backward


def layer(mover, args):
    (
        tokens,
        token_document,
        document_adapter,
        attention_norm_gain,
        feedforward_norm_gain,
        query_weight,
        key_weight,
        value_weight,
        output_weight,
        gate_weight,
        up_weight,
        down_weight,
        attention_down_maps,
        query_exit_maps,
        key_value_exit_maps,
        output_entry_maps,
        output_exit_maps,
        feedforward_entry_maps,
        feedforward_exit_maps,
        down_entry_maps,
        down_exit_maps,
        cotangent,
    ) = args
    seq_size, wsh_size, s = mover.seq_size, mover.wsh_size, mover.s
    own_rows = tokens.shape[1]
    width = tokens.shape[2]
    adapters = attention_down_maps.shape[1]
    rank = query_exit_maps.shape[1]
    flat = adapters * rank
    doc_count = document_adapter.shape[1]
    q_cols = query_weight.shape[1] // seq_size
    kv_cols = key_weight.shape[1] // seq_size
    feature = width // seq_size
    row_block = width // wsh_size
    hidden = gate_weight.shape[1]
    hid_block = hidden // (wsh_size * seq_size)
    hid_own = hidden // seq_size

    def owners(docs):
        hot = (docs[:, None] == jnp.arange(doc_count, dtype=jnp.int32)[None, :]).astype(jnp.int32)
        return jnp.sum(hot * document_adapter[0][None, :], axis=1)

    def turned(maps):
        return maps.transpose(1, 2, 0).reshape(-1, maps.shape[0])

    def own_hidden(values, lower=0, upper=hid_own):
        parts, at = [], lower
        while at < upper:
            w = at // hid_block
            stop = min(upper, (w + 1) * hid_block)
            start = (w * seq_size + s) * hid_block + at - w * hid_block
            parts.append(cut(values, start, stop - at, 1))
            at = stop
        return parts

    qkv_local = jnp.concatenate(
        [
            cut(query_weight, s * q_cols, q_cols, 1),
            cut(key_weight, s * kv_cols, kv_cols, 1),
            cut(value_weight, s * kv_cols, kv_cols, 1),
        ],
        axis=1,
    )
    local_docs = token_document[0]
    own_owner = owners(local_docs)
    hidden_state = tokens[0].astype(F32)
    first_normed, scale_one = normed(hidden_state, attention_norm_gain)
    first_normed = first_normed.astype(BF)
    input_maps = turned(attention_down_maps)
    picked_first = reverse_product(first_normed, input_maps)
    picked_first = picked_first * adapter_mask(own_owner, 3 * rank, adapters)
    picked_first = fold(picked_first, 3 * rank, 0)
    last_lane = jnp.arange(LANES, dtype=jnp.int32)[None, :] == LANES - 1
    picked_first = jnp.where(last_lane, local_docs.astype(F32)[:, None], picked_first).astype(BF)

    half_width = width // 2
    down_local = cut(down_weight, s * hid_block, hid_block, 0)
    if mover.fast:
        chunks = [(0, 1), (2, 3), (4, 5), (6,), (7,)]
    else:
        chunks = [tuple(range(wsh_size))]
    chunk_bounds = [(c[0] * hid_block, (c[-1] + 1) * hid_block) for c in chunks]

    def gate_up_far(i, *deps):
        gate_late, up_late = after((gate_weight, up_weight), *deps)
        parts = own_hidden(gate_late, *chunk_bounds[i]) + own_hidden(up_late, *chunk_bounds[i])
        return mover.far(jnp.concatenate(parts, axis=1))

    output_gradient = cotangent[0].astype(F32)
    d_mlp_local = (RESIDUAL_MULT * output_gradient).astype(BF)
    first_cols = jnp.concatenate([mover.to_slots(first_normed, row_block), picked_first], axis=1)
    qkv_pair = mover.far(qkv_local)
    if mover.fast:
        d_mlp_other = lax.ppermute(d_mlp_local, "seq", Y_SWAP)
        first_other = after(lax.ppermute(first_cols, "seq", Y_SWAP), d_mlp_other)
        out_piece = mover.head_rows(output_weight)
        qkv_four = mover.near(qkv_pair)
        out_pair = mover.far(out_piece, qkv_pair)
        qkv_full = mover.across(qkv_four)
        first_all = mover.gather_rest(first_cols, first_other)
        out_four = mover.near(out_pair, qkv_four)
        low_pair = mover.far(down_local[:, :half_width], qkv_four)
        out_swapped = mover.across(out_four, qkv_full[1])
        out_full = mover.head_rows_done(out_swapped, output_weight.shape[0])
        d_mlp = mover.gather_rest(d_mlp_local, after(d_mlp_other, first_all))
        low_four = mover.near(low_pair, out_four)
        high_pair = mover.far(down_local[:, half_width:], low_pair, qkv_full[1])
    else:
        qkv_full = mover.across(qkv_pair)
        first_all = mover.gather_tokens(first_cols)
        d_mlp = mover.gather_tokens(d_mlp_local)
        out_full = mover.head_rows(output_weight)
        down_full = mover.across(down_local)[0]
    document_line = first_all[:, width + LANES - 1].astype(jnp.int32)
    owner = owners(document_line)
    mask_rank = adapter_mask(owner, rank, adapters)

    (
        query_exit_maps,
        key_value_exit_maps,
    ) = after((query_exit_maps, key_value_exit_maps), first_normed)
    query_exit = cut(query_exit_maps.reshape(flat, -1), s * q_cols, q_cols, 1)
    key_exit = cut(key_value_exit_maps[0].reshape(flat, -1), s * kv_cols, kv_cols, 1)
    value_exit = cut(key_value_exit_maps[1].reshape(flat, -1), s * kv_cols, kv_cols, 1)
    la_one = first_all[:, width:]
    la_q = spread(la_one, owner, rank, 0, adapters)
    la_k = spread(la_one, owner, rank, rank, adapters)
    la_v = spread(la_one, owner, rank, 2 * rank, adapters)
    token_length = first_all.shape[0]
    attend = fast_attention if mover.fast else plain_attention
    early, attend_rest, attention_back = attend(
        first_all, qkv_full, la_q, la_k, la_v, query_exit, key_exit, value_exit, document_line,
    )

    (
        feedforward_entry_maps,
        feedforward_exit_maps,
        down_entry_maps,
        down_exit_maps,
        output_entry_maps,
        output_exit_maps,
    ) = after(
        (
            feedforward_entry_maps,
            feedforward_exit_maps,
            down_entry_maps,
            down_exit_maps,
            output_entry_maps,
            output_exit_maps,
        ),
        early,
    )
    if mover.fast:
        low_rows = low_four.shape[0] // 2
        low_early = after(low_four[:low_rows], out_swapped[1], early)
        low_other = [
            lax.ppermute(low_early, "wsh", X_SWAP),
            lax.ppermute(low_four[low_rows:], "wsh", X_SWAP),
        ]
        down_low = (low_four, jnp.concatenate(low_other, axis=0))
        high_four = mover.near(high_pair, low_four, early)
        attended = attend_rest(out_full, high_pair, d_mlp)
        chunk_pairs = [gate_up_far(0, high_pair, early)]
        attended = after(attended, high_four, low_other[0])
        down_high, high_parts = mover.across_parts(high_four)
        chunk_fours = [mover.near(chunk_pairs[0], high_four)]
        chunk_weights, chunk_parts = mover.across_parts(chunk_fours[0])
        chunk_weights = [chunk_weights]
        chunk_pairs.append(gate_up_far(1, chunk_pairs[0]))
    else:
        attended = attend_rest()

    out_entry = cut(turned(output_entry_maps), s * q_cols, q_cols, 1)
    out_exit = output_exit_maps.reshape(flat, -1)
    la_out_part = fold(reverse_product(attended, out_entry) * mask_rank, rank, 0)
    attn_sum = mover.scatter_tokens(
        low_dot(attended, out_full), la_out_part, deps=chunk_pairs[:1] if mover.fast else ()
    )
    la_out_own = attn_sum[1].astype(BF)
    attention_path = attn_sum[0] + low_dot(
        spread(la_out_own, own_owner, rank, 0, adapters), out_exit
    )
    middle = hidden_state + RESIDUAL_MULT * attention_path
    if mover.fast:
        middle = after(middle, low_other[1], high_parts[0], chunk_fours[0])

    second_normed, scale_two = normed(middle, feedforward_norm_gain)
    second_normed = second_normed.astype(BF)
    entry_maps = turned(feedforward_entry_maps)
    picked_second = reverse_product(second_normed, entry_maps) * adapter_mask(
        own_owner, 2 * rank, adapters
    )
    picked_second = fold(picked_second, 2 * rank, rank) + la_out_own.astype(F32)
    second_cols = jnp.concatenate(
        [mover.to_slots(second_normed, row_block), picked_second.astype(BF)], axis=1
    )
    if mover.fast:
        second_other = lax.ppermute(second_cols, "seq", Y_SWAP)
        second_all = mover.gather_rest(
            second_cols, after(second_other, high_parts[1], chunk_parts[0], chunk_pairs[1])
        )
    else:
        second_all = mover.gather_tokens(second_cols)
    la_out = spread(second_all[:, width:], owner, rank, 0, adapters)
    la_gate = spread(second_all[:, width:], owner, rank, rank, adapters)
    la_up = spread(second_all[:, width:], owner, rank, 2 * rank, adapters)

    down_exit = down_exit_maps.reshape(flat, -1)
    d_la_d = (reverse_product(d_mlp, down_exit) * mask_rank).astype(BF)
    down_entry = jnp.concatenate(own_hidden(turned(down_entry_maps)), axis=1)
    all_exits = feedforward_exit_maps.reshape(2, flat, -1)
    exits = [jnp.concatenate(own_hidden(all_exits[i]), axis=1) for i in range(2)]
    units_found = []
    if mover.fast:
        sums = None
        for i, units in enumerate(chunks):
            if i + 1 < len(chunks):
                deps = [chunk_fours[i]] + ([] if sums is None else [sums[0]])
                chunk_fours.append(mover.near(chunk_pairs[i + 1], *deps))
                chunk_weights.append(mover.across(chunk_fours[i + 1]))
            if i + 2 < len(chunks):
                deps = [chunk_pairs[i + 1], down_high[1] if sums is None else sums[0]]
                chunk_pairs.append(gate_up_far(i + 2, *deps))
            lower, upper = chunk_bounds[i]
            units_in = after(second_all, *chunk_fours[i + 1 : i + 2], *chunk_pairs[i + 2 : i + 3])
            mixed, d_gate, d_up, *sums = mlp_call(
                units,
                mover.z_slot(units[0] // 2),
                mover.x,
                units_in,
                chunk_weights[i],
                la_gate,
                la_up,
                exits[0][:, lower:upper],
                exits[1][:, lower:upper],
                d_mlp,
                down_low,
                down_high,
                d_la_d,
                down_entry[:, lower:upper],
                sums,
            )
            units_found.append((mixed, d_gate, d_up))
        d_second, d_la_both = sums
        d_la_gate, d_la_up = d_la_both[:, :flat], d_la_both[:, flat:]
    else:
        weights = mover.across(gate_up_far(0))[0]
        both = low_dot(second_all[:, :width], weights)
        gate = both[:, :hid_own] + low_dot(la_gate, exits[0])
        up = both[:, hid_own:] + low_dot(la_up, exits[1])
        d_mixed = reverse_product(d_mlp, down_full) + low_dot(d_la_d, down_entry)
        sigma = jax.nn.sigmoid(gate)
        swish = gate * sigma
        mixed = (swish * up).astype(BF)
        d_gate = (d_mixed * up * sigma * (1.0 + gate * (1.0 - sigma))).astype(BF)
        d_up = (d_mixed * swish).astype(BF)
        d_second = reverse_product(jnp.concatenate([d_gate, d_up], axis=1), weights)
        d_la_gate = reverse_product(d_gate, exits[0])
        d_la_up = reverse_product(d_up, exits[1])
        units_found.append((mixed, d_gate, d_up))
    d_la_two_part = fold(d_la_gate * mask_rank, rank, 0) + fold(d_la_up * mask_rank, rank, rank)
    d_second_sum = mover.scatter_tokens(d_second, d_la_two_part, mark="second")
    units_found[-1] = after(units_found[-1], mover.marks.get("second_away"))
    mixed_parts = [found[0] for found in units_found]
    gate_grads = [gradient_product(la_gate, found[1]) for found in units_found]
    up_grads = [gradient_product(la_up, found[2]) for found in units_found]
    entry_grads = [gradient_product(d_la_d, found[0]) for found in units_found]
    d_la_two_own = d_second_sum[1].astype(BF)
    d_second_own = mover.from_slots(d_second_sum[0], row_block) + low_dot(
        spread(d_la_two_own, own_owner, 2 * rank, 0, adapters), entry_maps
    )
    grad_middle = output_gradient + normed_back(
        middle, scale_two, feedforward_norm_gain, d_second_own
    )
    d_attn_own = (RESIDUAL_MULT * grad_middle).astype(BF)
    gate_grad = jnp.concatenate(gate_grads, axis=1)
    up_grad = jnp.concatenate(up_grads, axis=1)
    down_in_grad = jnp.concatenate(entry_grads, axis=1)
    d_attn_cols = jnp.concatenate([d_attn_own, d_la_two_own], axis=1)
    if mover.fast:
        packed = jnp.concatenate([pack(v) for v in (gate_grad, up_grad, down_in_grad)], axis=0)
        hidden_half = mover.sum_start(packed)
        d_attn_other = lax.ppermute(d_attn_cols, "seq", Y_SWAP)
        d_attn_all = mover.gather_rest(d_attn_cols, after(d_attn_other, hidden_half))
    else:
        d_attn_all = mover.gather_tokens(d_attn_cols)
    d_attn = d_attn_all[:, :width]

    mixed_all = jnp.concatenate(mixed_parts, axis=1)
    la_down_part = fold(reverse_product(mixed_all, down_entry) * mask_rank, rank, 0)
    if mover.fast:
        mlp_part = mlp_out_call(
            chunks, [mover.z_slot(i) for i in range(4)], mover.x, mixed_parts, down_low, down_high
        )
    else:
        mlp_part = low_dot(mixed_all, down_full)
    mlp_sum = mover.scatter_tokens(mlp_part, la_down_part, deps=(d_attn_all,), mark="mlp")
    if mover.fast:
        hidden_grads = mover.sum_hidden(
            hidden_half, (mover.marks["mlp"],), "hidden", (d_attn_all,)
        )
    else:
        hidden_grads = mover.plain_hidden([gate_grad, up_grad, down_in_grad], hid_block)
    hidden_sent = mover.marks.get("hidden", (None, None))
    la_down_own = mlp_sum[1].astype(BF)
    feedforward_path = mlp_sum[0] + low_dot(
        spread(la_down_own, own_owner, rank, 0, adapters), down_exit
    )
    layer_out = (middle + RESIDUAL_MULT * feedforward_path).astype(BF)[None]
    la_down = spread(mover.gather_tokens(la_down_own), owner, rank, 0, adapters)

    def own_features(slots):
        per = wsh_size // seq_size
        parts = [
            cut(slots, mover.slot_of(s * per + i) * row_block, row_block, 1) for i in range(per)
        ]
        return jnp.concatenate(parts, axis=1)

    d_la_two = spread(d_attn_all[:, width:], owner, 2 * rank, 0, adapters)
    entry_grad = gradient_product(d_la_two, own_features(second_all))
    down_out_grad = gradient_product(la_down, cut(d_mlp, s * feature, feature, 1))
    d_la_o = (reverse_product(d_attn, out_exit) * mask_rank).astype(BF)
    out_in_grad = gradient_product(d_la_o, attended)
    out_out_grad = gradient_product(la_out, cut(d_attn, s * feature, feature, 1))

    d_attended = (reverse_product(d_attn, out_full) + low_dot(d_la_o, out_entry)).astype(BF)
    d_query, d_key, d_value = attention_back(
        d_attended, (mover.marks.get("mlp"),), hidden_sent[:1]
    )
    d_la_one_part = (
        fold(reverse_product(d_query, query_exit) * mask_rank, rank, 0)
        + fold(reverse_product(d_key, key_exit) * mask_rank, rank, rank)
        + fold(reverse_product(d_value, value_exit) * mask_rank, rank, 2 * rank)
    )
    d_la_one = mover.sum_small(d_la_one_part.astype(BF), hidden_sent[1:]).astype(BF)
    d_qkv = jnp.concatenate([d_query, d_key, d_value], axis=1)
    d_qkv = after(d_qkv, d_la_one_part)
    d_first_sum = jnp.concatenate(
        mover.scatter_tokens(
            *[reverse_product(d_qkv, half) for half in qkv_full],
            deps=(d_la_one,),
            late=hidden_grads,
            mark="first",
        ),
        axis=1,
    )
    d_la_one_own = cut(d_la_one, s * own_rows, own_rows, 0)
    d_first = mover.from_slots(d_first_sum, row_block) + low_dot(
        spread(d_la_one_own, own_owner, 3 * rank, 0, adapters), input_maps
    )
    hidden_gradient = grad_middle + normed_back(
        hidden_state, scale_one, attention_norm_gain, d_first
    )
    attention_in_grad = gradient_product(
        spread(d_la_one, owner, 3 * rank, 0, adapters), own_features(first_all)
    )
    query_out_grad = gradient_product(la_q, d_query)
    key_out_grad = gradient_product(la_k, d_key)
    value_out_grad = gradient_product(la_v, d_value)
    last_grads = mover.sum_features(
        [attention_in_grad, query_out_grad, down_out_grad, entry_grad, out_in_grad, out_out_grad],
        key_out_grad,
        value_out_grad,
        (mover.marks.get("first_away"),),
        (mover.marks.get("first"),),
    )

    def back(values, shape):
        return values.reshape(shape[1], shape[2], shape[0]).transpose(2, 0, 1)

    return (
        layer_out,
        hidden_gradient[None],
        back(last_grads[0], attention_down_maps.shape),
        last_grads[1].reshape(query_exit_maps.shape),
        last_grads[6].reshape(key_value_exit_maps.shape),
        back(last_grads[4], output_entry_maps.shape),
        last_grads[5].reshape(output_exit_maps.shape),
        back(last_grads[3], feedforward_entry_maps.shape),
        hidden_grads[0].reshape(feedforward_exit_maps.shape),
        back(hidden_grads[1], down_entry_maps.shape),
        last_grads[2].reshape(down_exit_maps.shape),
    )


def solution(mesh):
    seq_size, wsh_size = mesh.shape["seq"], mesh.shape["wsh"]

    def on_device(*args):
        return layer(Mover(seq_size, wsh_size), args)

    rows = P("wsh", None)
    stream = P("wsh", "seq", None)
    in_specs = (stream, P("wsh", "seq"), rows, P(), P()) + (rows,) * 7 + (P(),) * 9 + (stream,)
    out_specs = (stream, stream) + (P(),) * 9
    return jax.shard_map(
        on_device, mesh=mesh, in_specs=in_specs, out_specs=out_specs, check_vma=False
    )
```

```python
import jax
import jax.numpy as jnp
from jax import lax
from jax.experimental import pallas as pl
from jax.experimental.pallas import tpu as pltpu
from jax.sharding import PartitionSpec as P

QUERY_HEADS = 32
KEY_HEADS = 8
HEAD_WIDTH = 64
LANES = 128
PACK = 512
TILE = 256

EPSILON = 1e-05
RESIDUAL_MULT = 0.22
SCORE_MULT = 0.015625
ROPE_BASE = 10000000.0
MASKED = -1e30

BF = jnp.bfloat16
F32 = jnp.float32

CORE_SWAP = [(s, s ^ 1) for s in range(4)]
Y_SWAP = [(s, s ^ 2) for s in range(4)]
X_SWAP = [(w, w ^ 1) for w in range(8)]
NEAR_SWAP = [(w, w ^ 2) for w in range(8)]
FAR_SWAP = [(w, w ^ 4) for w in range(8)]


def z_shift(steps):
    return [(2 * z + x, 2 * ((z + steps) % 4) + x) for z in range(4) for x in range(2)]


def low_dot(left, right):
    return jnp.dot(left, right, preferred_element_type=F32)


def gradient_product(left, right):
    return lax.dot_general(left, right, (((0,), (0,)), ((), ())), preferred_element_type=F32)


def reverse_product(left, right):
    return lax.dot_general(left, right, (((1,), (1,)), ((), ())), preferred_element_type=F32)


def normed(values, gain):
    norm_scale = lax.rsqrt(jnp.mean(values * values, axis=-1, keepdims=True) + EPSILON)
    return (values * norm_scale * gain, norm_scale)


def normed_back(values, norm_scale, gain, grad_in):
    scaled = grad_in * gain
    cubed = norm_scale * norm_scale * norm_scale
    return norm_scale * scaled - values * cubed * jnp.mean(scaled * values, axis=-1, keepdims=True)


def rope_tables(positions, head_size):
    half_size = head_size // 2
    inv_freq = ROPE_BASE ** (-(jnp.arange(half_size).astype(F32) * 2.0) / head_size)
    angles = positions.astype(F32)[:, None] * inv_freq[None, :]
    return (jnp.cos(angles)[:, None, :], jnp.sin(angles)[:, None, :])


def rotate(values, cos_tab, sin_tab):
    half_size = values.shape[-1] // 2
    former = values[..., :half_size]
    latter = values[..., half_size:]
    return jnp.concatenate(
        [former * cos_tab - latter * sin_tab, latter * cos_tab + former * sin_tab], axis=-1
    )


def cut(values, start, size, axis):
    return lax.dynamic_slice_in_dim(values, start, size, axis)


def pick(values, index, axis):
    return lax.dynamic_index_in_dim(values, index, axis, keepdims=False)


def adapter_mask(owner, ranks, adapters):
    lane = jnp.arange(adapters * ranks, dtype=jnp.int32) // ranks
    return (owner[:, None] == lane[None, :]).astype(F32)


def fold(masked, ranks, offset):
    rows = jnp.arange(masked.shape[1], dtype=jnp.int32) % ranks
    lanes = jnp.arange(LANES, dtype=jnp.int32) - offset
    return low_dot(masked.astype(BF), (rows[:, None] == lanes[None, :]).astype(BF))


def spread(folded, owner, ranks, offset, adapters):
    rows = jnp.arange(LANES, dtype=jnp.int32) - offset
    lanes = jnp.arange(adapters * ranks, dtype=jnp.int32) % ranks
    wide = low_dot(folded.astype(BF), (rows[:, None] == lanes[None, :]).astype(BF))
    return (wide * adapter_mask(owner, ranks, adapters)).astype(BF)


def pack(values):
    parts = [values[:, i : i + PACK] for i in range(0, values.shape[1], PACK)]
    return jnp.concatenate(parts, axis=0)


def after(values, *deps):
    deps = [d for d in deps if d is not None]
    if not deps:
        return values
    return lax.optimization_barrier((values, tuple(deps)))[0]


class Mover:
    def __init__(self, seq_size, wsh_size):
        self.seq_size, self.wsh_size = seq_size, wsh_size
        self.fast = seq_size == 4 and wsh_size == 8
        self.s, self.w = lax.axis_index("seq"), lax.axis_index("wsh")
        self.y, self.c = self.s // 2, self.s % 2
        self.z, self.x = self.w // 2, self.w % 2
        self.marks = {}

    def far(self, chunk, *deps):
        chunk = after(chunk, *deps)
        if not self.fast:
            return chunk
        return jnp.concatenate([chunk, lax.ppermute(chunk, "wsh", FAR_SWAP)], axis=0)

    def near(self, pair, *deps):
        pair = after(pair, *deps)
        if not self.fast:
            return pair
        return jnp.concatenate([pair, lax.ppermute(pair, "wsh", NEAR_SWAP)], axis=0)

    def across(self, four, *deps):
        four = after(four, *deps)
        if not self.fast:
            return (lax.all_gather(four, "wsh", axis=0, tiled=True),)
        return four, lax.ppermute(four, "wsh", X_SWAP)

    def swap_bits(self, d):
        return d // 2 + 2 * (d % 2)

    def slot_owner(self, k):
        if not self.fast:
            return k
        return 2 * (self.z ^ self.swap_bits(k % 4)) + (self.x ^ (k // 4))

    def slot_of(self, w):
        if not self.fast:
            return w
        return self.z_slot(w // 2) + 4 * (self.x ^ (w % 2))

    def z_slot(self, z):
        return self.swap_bits(self.z ^ z)

    def to_slots(self, values, block):
        if not self.fast:
            return values
        parts = [cut(values, self.slot_owner(k) * block, block, 1) for k in range(self.wsh_size)]
        return jnp.concatenate(parts, axis=1)

    def from_slots(self, values, block):
        if not self.fast:
            return values
        parts = [cut(values, self.slot_of(w) * block, block, 1) for w in range(self.wsh_size)]
        return jnp.concatenate(parts, axis=1)

    def head_rows(self, weight):
        rows = weight.shape[0]
        per = self.wsh_size // self.seq_size
        if not self.fast:
            return cut(
                lax.all_gather(weight, "wsh", axis=0, tiled=True),
                self.s * per * rows,
                per * rows,
                0,
            )
        piece = rows // 4

        def part(z):
            return cut(weight, z * piece, piece, 0)

        def pairs(senders, step):
            return [
                (8 * s + 2 * (s ^ sender) + x, 8 * s + 2 * (s ^ sender ^ step) + x)
                for s in range(4)
                for sender in senders
                for x in range(2)
            ]

        z, axes = self.z, ("seq", "wsh")
        away = jnp.concatenate([part(z ^ 2), part(z ^ 3)], axis=0)
        got = lax.ppermute(away, axes, pairs((0,), 2))
        first = z == self.s
        mine = jnp.where(first, part(z), got[:piece])
        away = jnp.where(first, part(z ^ 1), got[piece:])
        got = lax.ppermute(away, axes, pairs((0, 2), 1))
        return jnp.where(first | (z == (self.s ^ 2)), mine, got)

    def head_rows_done(self, halves, rows):
        piece = rows // 4
        out = []
        for shard in range(2):
            half = jnp.where(self.x == shard, halves[0], halves[1])
            blocks = half.reshape(4, piece, half.shape[1])
            out += [pick(blocks, self.z_slot(j), 0) for j in range(4)]
        return jnp.concatenate(out, axis=0)

    def gather_tokens(self, values):
        if not self.fast:
            return lax.all_gather(values, "seq", axis=0, tiled=True)
        return self.gather_rest(values, lax.ppermute(values, "seq", Y_SWAP))

    def gather_rest(self, values, other):
        first = self.y == 0
        column = jnp.stack([jnp.where(first, values, other), jnp.where(first, other, values)])
        partner = lax.ppermute(column, "seq", CORE_SWAP)
        first = self.c == 0
        whole = jnp.stack(
            [jnp.where(first, column, partner), jnp.where(first, partner, column)], axis=1
        )
        return whole.reshape((4 * values.shape[0],) + values.shape[1:])

    def scatter_tokens(self, *partials, deps=(), late=(), mark=None):
        if not self.fast:
            return [
                lax.psum_scatter(v.astype(BF), "seq", scatter_dimension=0, tiled=True).astype(F32)
                for v in partials
            ]
        rows = partials[0].shape[0] // 4
        blocks = [v.reshape(2, 2, rows, v.shape[1]) for v in partials]
        out = jnp.concatenate([pick(v, 1 - self.c, 1).astype(BF) for v in blocks], axis=2)
        got = lax.ppermute(out, "seq", CORE_SWAP).astype(F32)
        mine = jnp.concatenate([pick(v, self.c, 1) for v in blocks], axis=2)
        away = (pick(mine, 1 - self.y, 0) + pick(got, 1 - self.y, 0)).astype(BF)
        other = lax.ppermute(after(away, *deps), "seq", Y_SWAP)
        self.marks[mark] = other
        if mark is not None:
            self.marks[mark + "_away"] = away
        other = after(other, *late).astype(F32)
        total = pick(mine, self.y, 0) + pick(got, self.y, 0) + other
        found, at = [], 0
        for v in partials:
            found.append(total[:, at : at + v.shape[1]])
            at += v.shape[1]
        return found

    def sum_small(self, partial, deps=()):
        if not self.fast:
            return lax.psum(partial, "seq")
        total = partial.astype(F32) + lax.ppermute(partial, "seq", CORE_SWAP).astype(F32)
        other = lax.ppermute(after(total.astype(BF), *deps), "seq", Y_SWAP)
        return total + other.astype(F32)

    def sum_plain(self, grad):
        total = lax.psum(grad.astype(BF), "wsh")
        return lax.all_gather(total.astype(BF), "seq", axis=0).astype(F32)

    def plain_hidden(self, grads, hid_block):
        found = []
        for grad in grads:
            rows = grad.shape[0]
            wide = self.sum_plain(grad).reshape(self.seq_size, rows, self.wsh_size, hid_block)
            found.append(wide.transpose(1, 2, 0, 3).reshape(rows, -1))
        return [jnp.stack(found[:2]), found[2]]

    def sum_hidden(self, half, deps, mark, early):
        parts = self.sum_end(half, deps, mark, early)
        s = self.s.astype(jnp.int32)[None]
        return [
            final_hidden(parts, s, 0, 2),
            final_hidden(parts, s, 8 * LANES, 1)[0],
        ]

    def sum_features(self, grads, key=None, value=None, mid=(), deps=(), late=(), mark=None):
        if not self.fast:
            grads = grads + ([key, value] if key is not None else [])
            found = []
            for grad in grads:
                found.append(self.sum_plain(grad).transpose(1, 0, 2).reshape(grad.shape[0], -1))
            return found[:-2] + [jnp.stack(found[-2:])] if key is not None else found
        packed = list(grads)
        if key is not None:
            rest = jnp.zeros((key.shape[0], PACK - 2 * LANES), F32)
            packed.append(jnp.concatenate([key, value, rest], axis=1))
        half = self.sum_start(jnp.concatenate(packed, axis=0), mid)
        parts = self.sum_end(half, deps, late=late)
        self.marks[mark] = parts[2]
        s = self.s.astype(jnp.int32)[None]
        found, at = [], 0
        for grad in grads:
            found.append(final_features(parts, s, at, grad.shape[0]))
            at += grad.shape[0]
        if key is not None:
            found.append(final_kv(parts, s, at))
        return found

    def sum_start(self, packed, mid=()):
        rows = packed.shape[0]
        halves = packed.reshape(2, rows // 2, PACK)
        got = lax.ppermute(pick(halves, 1 - self.x, 0).astype(BF), "wsh", X_SWAP)
        half = pick(halves, self.x, 0) + got.astype(F32)
        blocks = after(half, *mid).reshape(4, rows // 8, PACK)
        total = pick(blocks, self.z, 0)
        for r in range(1, 4):
            out = pick(blocks, (self.z + r) % 4, 0).astype(BF)
            total = total + lax.ppermute(out, "wsh", z_shift(r)).astype(F32)
        own = total.astype(BF)
        got = [own] + [lax.ppermute(own, "wsh", z_shift(r)) for r in range(1, 4)]
        ring = jnp.stack(got)
        return jnp.concatenate([pick(ring, (self.z - j) % 4, 0) for j in range(4)], axis=0)

    def sum_end(self, half, deps=(), mark=None, early=(), late=()):
        rows = 2 * half.shape[0]
        half = after(half, *early)
        other = lax.ppermute(half, "wsh", X_SWAP)
        first = self.x == 0
        part = jnp.concatenate([jnp.where(first, half, other), jnp.where(first, other, half)])
        core = lax.ppermute(part, "seq", CORE_SWAP)
        if mark is None:
            other = after(lax.ppermute(after(part, *deps), "seq", Y_SWAP), *late)
        else:
            top = lax.ppermute(after(part[: rows // 2], *deps), "seq", Y_SWAP)
            rest = lax.ppermute(after(part[rows // 2 :], top), "seq", Y_SWAP)
            self.marks[mark] = (top, rest)
            other = jnp.concatenate([top, rest], axis=0)
        return part, core, other, lax.ppermute(other, "seq", CORE_SWAP)


def final_body(s_ref, own, core, other, last, out_ref):
    columns = own.shape[-1]
    for k in range(4):
        place = s_ref[0] ^ k
        low = jnp.where(place % 2 == 0, own[...], core[...])
        high = jnp.where(place % 2 == 0, other[...], last[...])
        value = jnp.where(place < 2, low, high).astype(F32)
        at = slice(k * columns, (k + 1) * columns)
        if len(out_ref.shape) == 3:
            out_ref[0, :, at] = value
        else:
            out_ref[:, at] = value


def final_call(parts, s, grid, part_block, part_map, out_shape, out_block, out_map):
    return pl.pallas_call(
        final_body,
        grid_spec=pltpu.PrefetchScalarGridSpec(
            num_scalar_prefetch=1,
            grid=grid,
            in_specs=[pl.BlockSpec(part_block, part_map)] * 4,
            out_specs=pl.BlockSpec(out_block, out_map),
        ),
        out_shape=jax.ShapeDtypeStruct(out_shape, F32),
        name="finish",
    )(s, *parts)


def final_features(parts, s, row, rows):
    at = row // LANES
    return final_call(
        parts,
        s,
        (rows // LANES,),
        (LANES, PACK),
        lambda i, _: (at + i, 0),
        (rows, 4 * PACK),
        (LANES, 4 * PACK),
        lambda i, _: (i, 0),
    )


def final_hidden(parts, s, row, count):
    at = row // LANES
    return final_call(
        parts,
        s,
        (count, 8),
        (LANES, TILE),
        lambda n, w, _: (at + 4 * n + w // 2, w % 2),
        (count, LANES, 32 * TILE),
        (1, LANES, 4 * TILE),
        lambda n, w, _: (n, 0, w),
    )


def final_kv(parts, s, row):
    at = row // LANES
    return final_call(
        parts,
        s,
        (2,),
        (LANES, LANES),
        lambda n, _: (at, n),
        (2, LANES, 4 * LANES),
        (1, LANES, 4 * LANES),
        lambda n, _: (n, 0, 0),
    )


def half_lanes(rows, half):
    lane = lax.broadcasted_iota(jnp.int32, (rows, LANES), 1)
    return (lane < HEAD_WIDTH) if half == 0 else (lane >= HEAD_WIDTH)


def turn(values, cos_tab, sin_tab):
    lane = lax.broadcasted_iota(jnp.int32, values.shape, 1)
    swapped = jnp.where(
        lane % HEAD_WIDTH < HEAD_WIDTH // 2,
        pltpu.roll(values, LANES - HEAD_WIDTH // 2, 1),
        pltpu.roll(values, HEAD_WIDTH // 2, 1),
    )
    return values * cos_tab + swapped * sin_tab


def twice(values, half):
    other = pltpu.roll(values, HEAD_WIDTH, 1)
    first = half_lanes(values.shape[0], 0)
    return jnp.where(first, values, other) if half == 0 else jnp.where(first, other, values)


def qkv_body(x_ref, w_own, w_other, la_q, la_k, la_v, exit_q, exit_kv, cos_ref, sin_ref, q_ref, k_ref, v_ref):
    cos_tab, sin_tab = cos_ref[...], sin_ref[...]
    half = w_own.shape[0]
    product = low_dot(x_ref[:, :half], w_own[...]) + low_dot(x_ref[:, half:], w_other[...])
    q_cols = q_ref.shape[1]
    query = product[:, :q_cols] + low_dot(la_q[...], exit_q[...])
    for i in range(0, q_cols, LANES):
        q_ref[:, i : i + LANES] = turn(query[:, i : i + LANES], cos_tab, sin_tab).astype(BF)
    key = product[:, q_cols : q_cols + LANES] + low_dot(la_k[...], exit_kv[0])
    key = turn(key, cos_tab, sin_tab)
    value = product[:, q_cols + LANES :] + low_dot(la_v[...], exit_kv[1])
    for half in range(2):
        k_ref[:, half * LANES : (half + 1) * LANES] = twice(key, half).astype(BF)
        v_ref[:, half * LANES : (half + 1) * LANES] = twice(value, half).astype(BF)


def qkv_call(x, weights, la_q, la_k, la_v, exit_q, exit_kv, cos_tab, sin_tab):
    rows, width = x.shape[0], 2 * weights[0].shape[0]
    q_cols = exit_q.shape[1]

    def tile(columns):
        return pl.BlockSpec((TILE, columns), lambda i: (i, 0))

    return pl.pallas_call(
        qkv_body,
        grid=(rows // TILE,),
        in_specs=[
            tile(width),
            pl.BlockSpec(weights[0].shape, lambda i: (0, 0)),
            pl.BlockSpec(weights[1].shape, lambda i: (0, 0)),
            tile(LANES),
            tile(LANES),
            tile(LANES),
            pl.BlockSpec(exit_q.shape, lambda i: (0, 0)),
            pl.BlockSpec(exit_kv.shape, lambda i: (0, 0, 0)),
            tile(LANES),
            tile(LANES),
        ],
        out_specs=[tile(q_cols), tile(2 * LANES), tile(2 * LANES)],
        out_shape=[
            jax.ShapeDtypeStruct((rows, q_cols), BF),
            jax.ShapeDtypeStruct((rows, 2 * LANES), BF),
            jax.ShapeDtypeStruct((rows, 2 * LANES), BF),
        ],
        name="qkv",
        cost_estimate=pl.CostEstimate(
            flops=2 * rows * width * weights[0].shape[1], bytes_accessed=12 << 20, transcendentals=0
        ),
    )(x, *weights, la_q, la_k, la_v, exit_q, exit_kv, cos_tab, sin_tab)


def allowed_pairs(i, t, doc_col, doc_row):
    start = pl.multiple_of(t * TILE, TILE)
    rows = i * TILE + lax.broadcasted_iota(jnp.int32, (TILE, TILE), 0)
    keys = start + lax.broadcasted_iota(jnp.int32, (TILE, TILE), 1)
    return (doc_col[...] == doc_row[:, pl.ds(start, TILE)]) & (keys <= rows)


def forward_body(first_ref, q_ref, k_ref, v_ref, doc_col, doc_row, o_ref, lse_ref, m_s, l_s, acc_s):
    i = pl.program_id(0)
    m_s[...] = jnp.full_like(m_s, MASKED)
    l_s[...] = jnp.zeros_like(l_s)
    acc_s[...] = jnp.zeros_like(acc_s)

    def step(t, carry):
        allowed = allowed_pairs(i, t, doc_col, doc_row)
        start = pl.multiple_of(t * TILE, TILE)
        keys, vals = k_ref[pl.ds(start, TILE), :], v_ref[pl.ds(start, TILE), :]
        for h in range(4):
            pair = q_ref[:, (h // 2) * LANES : (h // 2 + 1) * LANES]
            query = jnp.where(half_lanes(TILE, h % 2), pair, jnp.zeros_like(pair))
            logits = jnp.where(allowed, SCORE_MULT * reverse_product(query, keys), MASKED)
            old = m_s[h]
            top = jnp.maximum(old, jnp.max(logits, axis=1, keepdims=True))
            shrink = jnp.exp(old - top)
            shifted = jnp.exp(logits - top)
            m_s[h] = top
            l_s[h] = l_s[h] * shrink + jnp.sum(shifted, axis=1, keepdims=True)
            acc_s[h] = acc_s[h] * shrink + low_dot(shifted.astype(BF), vals)
        return carry

    lax.fori_loop(first_ref[i], i + 1, step, 0)
    lane = lax.broadcasted_iota(jnp.int32, (TILE, LANES), 1)
    total = jnp.zeros((TILE, LANES), F32)
    for p in range(2):
        both = [acc_s[2 * p + n] / l_s[2 * p + n] for n in range(2)]
        o_ref[:, p * LANES : (p + 1) * LANES] = jnp.where(
            half_lanes(TILE, 0), both[0], both[1]
        ).astype(BF)
    for h in range(4):
        total = jnp.where(lane == h, m_s[h] + jnp.log(l_s[h]), total)
    lse_ref[...] = total


def attention_call(j, first, query, keys, values, doc_col, doc_row):
    rows = query.shape[0]
    group = query.shape[1] // 2
    return pl.pallas_call(
        forward_body,
        grid_spec=pltpu.PrefetchScalarGridSpec(
            num_scalar_prefetch=1,
            grid=(rows // TILE,),
            in_specs=[
                pl.BlockSpec((TILE, group), lambda i, _: (i, j)),
                pl.BlockSpec((rows, LANES), lambda i, _: (0, j)),
                pl.BlockSpec((rows, LANES), lambda i, _: (0, j)),
                pl.BlockSpec((TILE, 1), lambda i, _: (i, 0)),
                pl.BlockSpec((1, rows), lambda i, _: (0, 0)),
            ],
            out_specs=[
                pl.BlockSpec((TILE, group), lambda i, _: (i, 0)),
                pl.BlockSpec((TILE, LANES), lambda i, _: (i, 0)),
            ],
            scratch_shapes=[
                pltpu.VMEM((4, TILE, 1), F32),
                pltpu.VMEM((4, TILE, 1), F32),
                pltpu.VMEM((4, TILE, LANES), F32),
            ],
        ),
        out_shape=[
            jax.ShapeDtypeStruct((rows, group), BF),
            jax.ShapeDtypeStruct((rows, LANES), F32),
        ],
        name="attention",
        cost_estimate=pl.CostEstimate(
            flops=4 * 4 * rows * rows * LANES,
            bytes_accessed=3 << 20,
            transcendentals=4 * rows * rows,
        ),
    )(first, query, keys, values, doc_col, doc_row)


def backward_body(
    first_ref, q_ref, k_ref, v_ref, do_ref, o_ref, lse_ref, doc_col, doc_row, cos_ref, sin_ref,
    cos_all, sin_all, dq_ref, dk_ref, dv_ref, dq_s, dk_s, dv_s,
):
    i = pl.program_id(0)

    @pl.when(i == 0)
    def _():
        dk_s[...] = jnp.zeros_like(dk_s)
        dv_s[...] = jnp.zeros_like(dv_s)

    dq_s[...] = jnp.zeros_like(dq_s)
    queries, grads, deltas = [], [], []
    for h in range(4):
        at = slice((h // 2) * LANES, (h // 2 + 1) * LANES)
        half = half_lanes(TILE, h % 2)
        pair, grad = q_ref[:, at], do_ref[:, at]
        queries.append(jnp.where(half, pair, jnp.zeros_like(pair)))
        grads.append(jnp.where(half, grad, jnp.zeros_like(grad)))
        product = grads[h].astype(F32) * o_ref[:, at].astype(F32)
        deltas.append(jnp.sum(product, axis=1, keepdims=True))

    def step(t, carry):
        allowed = allowed_pairs(i, t, doc_col, doc_row)
        start = pl.multiple_of(t * TILE, TILE)
        at = pl.ds(start, TILE)
        keys, vals = k_ref[at, :], v_ref[at, :]
        dk, dv = dk_s[at, :], dv_s[at, :]
        for h in range(4):
            logits = jnp.where(allowed, SCORE_MULT * reverse_product(queries[h], keys), MASKED)
            probs = jnp.exp(logits - lse_ref[:, h : h + 1])
            d_probs = reverse_product(grads[h], vals)
            d_logits = (probs * (d_probs - deltas[h])).astype(BF)
            dq_s[h] = dq_s[h] + low_dot(d_logits, keys)
            dk = dk + gradient_product(d_logits, queries[h])
            dv = dv + gradient_product(probs.astype(BF), grads[h])
        dk_s[at, :] = dk
        dv_s[at, :] = dv
        return carry

    lax.fori_loop(first_ref[i], i + 1, step, 0)
    for p in range(2):
        both = jnp.where(half_lanes(TILE, 0), dq_s[2 * p], dq_s[2 * p + 1])
        both = (SCORE_MULT * both).astype(BF).astype(F32)
        dq_ref[:, p * LANES : (p + 1) * LANES] = turn(both, cos_ref[...], -sin_ref[...]).astype(BF)

    @pl.when(i == pl.num_programs(0) - 1)
    def _():
        def finish(t, carry):
            at = pl.ds(pl.multiple_of(t * TILE, TILE), TILE)
            dk, dv = dk_s[at, :], dv_s[at, :]
            dk = (SCORE_MULT * (dk + pltpu.roll(dk, HEAD_WIDTH, 1))).astype(BF).astype(F32)
            dk_ref[at, :] = turn(dk, cos_all[at, :], -sin_all[at, :]).astype(BF)
            dv_ref[at, :] = (dv + pltpu.roll(dv, HEAD_WIDTH, 1)).astype(BF)
            return carry

        lax.fori_loop(0, pl.num_programs(0), finish, 0)


def attention_back_call(
    j, first, query, keys, values, d_out, out, lse, doc_col, doc_row, cos_tab, sin_tab
):
    rows = query.shape[0]
    group = query.shape[1] // 2
    whole = pl.BlockSpec((rows, LANES), lambda i, _: (0, j))
    tile = pl.BlockSpec((TILE, group), lambda i, _: (i, j))
    table = pl.BlockSpec((TILE, LANES), lambda i, _: (i, 0))
    table_all = pl.BlockSpec((rows, LANES), lambda i, _: (0, 0))
    own_tile = pl.BlockSpec((TILE, group), lambda i, _: (i, 0))
    return pl.pallas_call(
        backward_body,
        grid_spec=pltpu.PrefetchScalarGridSpec(
            num_scalar_prefetch=1,
            grid=(rows // TILE,),
            in_specs=[
                tile,
                whole,
                whole,
                tile,
                own_tile,
                table,
                pl.BlockSpec((TILE, 1), lambda i, _: (i, 0)),
                pl.BlockSpec((1, rows), lambda i, _: (0, 0)),
                table,
                table,
                table_all,
                table_all,
            ],
            out_specs=[own_tile, table_all, table_all],
            scratch_shapes=[
                pltpu.VMEM((4, TILE, LANES), F32),
                pltpu.VMEM((rows, LANES), F32),
                pltpu.VMEM((rows, LANES), F32),
            ],
        ),
        out_shape=[
            jax.ShapeDtypeStruct((rows, group), BF),
            jax.ShapeDtypeStruct((rows, LANES), BF),
            jax.ShapeDtypeStruct((rows, LANES), BF),
        ],
        name="attention_back",
        cost_estimate=pl.CostEstimate(
            flops=4 * 10 * rows * rows * LANES,
            bytes_accessed=5 << 20,
            transcendentals=4 * rows * rows,
        ),
    )(first, query, keys, values, d_out, out, lse, doc_col, doc_row, cos_tab, sin_tab, cos_tab, sin_tab)


def fast_attention(
    x, weights, la_q, la_k, la_v, exit_q, exit_k, exit_v, document_line
):
    rows = x.shape[0]
    half = HEAD_WIDTH // 2
    cos_tab, sin_tab = rope_tables(jnp.arange(rows, dtype=jnp.int32), HEAD_WIDTH)
    cos_tab = jnp.tile(cos_tab.reshape(rows, half), (1, 4))
    sin_tab = sin_tab.reshape(rows, half)
    sin_tab = jnp.tile(jnp.concatenate([-sin_tab, sin_tab], axis=1), (1, 2))
    first_docs = document_line[::TILE]
    first = jnp.sum((document_line[None, :] < first_docs[:, None]).astype(jnp.int32), axis=1)
    first = first // TILE
    doc_col, doc_row = document_line[:, None], document_line[None, :]
    query, keys, values = qkv_call(
        x, weights, la_q, la_k, la_v, exit_q, jnp.stack([exit_k, exit_v]), cos_tab, sin_tab
    )
    early = attention_call(0, first, query, keys, values, doc_col, doc_row)
    found = [early]

    def finish(*deps):
        query_late = after(query, early[0], *deps)
        found.append(attention_call(1, first, query_late, keys, values, doc_col, doc_row))
        return jnp.concatenate([early[0], found[1][0]], axis=1)

    def backward(d_heads, between, behind):
        back = []
        for j in range(2):
            if j:
                d_heads = after(d_heads, back[0][1], *between)
            args = (first, query, keys, values, d_heads, *found[j], doc_col, doc_row)
            back.append(attention_back_call(j, *args, cos_tab, sin_tab))
        back[1] = after(back[1], *behind)
        lane = jnp.arange(LANES, dtype=jnp.int32)[None, :] < HEAD_WIDTH
        d_query = jnp.concatenate([back[0][0], back[1][0]], axis=1)
        d_key = jnp.where(lane, back[0][1], back[1][1])
        d_value = jnp.where(lane, back[0][2], back[1][2])
        return d_query, d_key, d_value

    return early[0], finish, backward


def units_rows(at_own, own, other):
    return jnp.where(at_own, own[...], other[...])


def mlp_body(owners, add, sc, n2, w_own, w_other, la_gate, la_up, exit_gate, exit_up, d_mlp,
             low_own, low_other, high_own, high_other, d_la_d, entry, *rest):
    if add:
        sum_in, la_in, mixed_ref, gate_ref, up_ref, sum_ref, la_ref = rest
    else:
        mixed_ref, gate_ref, up_ref, sum_ref, la_ref = rest
    half = w_own.shape[0]
    size = TILE * len(owners)
    both = low_dot(n2[:, :half], w_own[...]) + low_dot(n2[:, half:], w_other[...])
    gate = both[:, :size] + low_dot(la_gate[...], exit_gate[...])
    up = both[:, size:] + low_dot(la_up[...], exit_up[...])
    parts = []
    for w in owners:
        at_own = sc[1] == w % 2
        parts.append(
            reverse_product(d_mlp[:, :half], units_rows(at_own, low_own, low_other))
            + reverse_product(d_mlp[:, half:], units_rows(at_own, high_own, high_other))
        )
    d_mixed = jnp.concatenate(parts, axis=1) + low_dot(d_la_d[...], entry[...])
    sigma = jax.nn.sigmoid(gate)
    swish = gate * sigma
    mixed_ref[...] = (swish * up).astype(BF)
    d_gate = (d_mixed * up * sigma * (1.0 + gate * (1.0 - sigma))).astype(BF)
    d_up = (d_mixed * swish).astype(BF)
    gate_ref[...] = d_gate
    up_ref[...] = d_up
    d_both = jnp.concatenate([d_gate, d_up], axis=1)
    sum_own, sum_other = reverse_product(d_both, w_own[...]), reverse_product(d_both, w_other[...])
    back_gate, back_up = reverse_product(d_gate, exit_gate[...]), reverse_product(d_up, exit_up[...])
    if add:
        sum_own, sum_other = sum_own + sum_in[:, :half], sum_other + sum_in[:, half:]
        back_gate, back_up = back_gate + la_in[:, :LANES], back_up + la_in[:, LANES:]
    sum_ref[:, :half] = sum_own
    sum_ref[:, half:] = sum_other
    la_ref[:, :LANES] = back_gate
    la_ref[:, LANES:] = back_up


def mlp_call(owners, block, x, n2, weights, la_gate, la_up, exit_gate, exit_up, d_mlp, low, high,
             d_la_d, entry, sums):
    rows = d_mlp.shape[0]
    half = weights[0].shape[0]
    size = TILE * len(owners)

    def tile(columns):
        return pl.BlockSpec((TILE, columns), lambda t, _: (t, 0))

    def whole(array):
        return pl.BlockSpec(array.shape, lambda t, _: (0, 0))

    units = pl.BlockSpec((TILE, half), lambda t, sc: (sc[0], 0))
    args = [n2, *weights, la_gate, la_up, exit_gate, exit_up, d_mlp, *low, *high, d_la_d, entry]
    in_specs = [tile(2 * half), whole(weights[0]), whole(weights[1]), tile(LANES), tile(LANES)]
    in_specs += [whole(exit_gate), whole(exit_up), tile(2 * half)] + [units] * 4
    in_specs += [tile(LANES), whole(entry)]
    aliases = {}
    if sums is not None:
        aliases = {1 + len(args): 3, 2 + len(args): 4}
        args += sums
        in_specs += [tile(2 * half), tile(2 * LANES)]
    return pl.pallas_call(
        lambda *refs: mlp_body(owners, sums is not None, *refs),
        grid_spec=pltpu.PrefetchScalarGridSpec(
            num_scalar_prefetch=1,
            grid=(rows // TILE,),
            in_specs=in_specs,
            out_specs=[tile(size)] * 3 + [tile(2 * half), tile(2 * LANES)],
        ),
        out_shape=[jax.ShapeDtypeStruct((rows, size), BF)] * 3
        + [
            jax.ShapeDtypeStruct((rows, 2 * half), F32),
            jax.ShapeDtypeStruct((rows, 2 * LANES), F32),
        ],
        input_output_aliases=aliases,
        name="units",
        cost_estimate=pl.CostEstimate(
            flops=20 * rows * half * size, bytes_accessed=32 << 20, transcendentals=rows * size
        ),
    )(jnp.stack([block, x]).astype(jnp.int32), *args)


def mlp_out_body(chunks, sc, *refs):
    mixed = refs[: len(chunks)]
    low_own, low_other, high_own, high_other, out_ref = refs[len(chunks) :]
    half = low_own.shape[1]
    low = high = None
    for (owners, ref) in zip(chunks, mixed):
        for n, w in enumerate(owners):
            at = pl.ds(pl.multiple_of(sc[w // 2] * TILE, TILE), TILE)
            at_own = sc[4] == w % 2
            part = ref[:, n * TILE : (n + 1) * TILE]
            more_low = low_dot(part, jnp.where(at_own, low_own[at, :], low_other[at, :]))
            more_high = low_dot(part, jnp.where(at_own, high_own[at, :], high_other[at, :]))
            low = more_low if low is None else low + more_low
            high = more_high if high is None else high + more_high
    out_ref[:, :half] = low
    out_ref[:, half:] = high


def mlp_out_call(chunks, z_slots, x, mixed, low, high):
    rows, half = mixed[0].shape[0], low[0].shape[1]
    places = jnp.stack([*z_slots, x]).astype(jnp.int32)
    return pl.pallas_call(
        lambda *refs: mlp_out_body(chunks, *refs),
        grid_spec=pltpu.PrefetchScalarGridSpec(
            num_scalar_prefetch=1,
            grid=(rows // TILE,),
            in_specs=[pl.BlockSpec((TILE, m.shape[1]), lambda t, _: (t, 0)) for m in mixed]
            + [pl.BlockSpec(low[0].shape, lambda t, _: (0, 0))] * 4,
            out_specs=pl.BlockSpec((TILE, 2 * half), lambda t, _: (t, 0)),
        ),
        out_shape=jax.ShapeDtypeStruct((rows, 2 * half), F32),
        name="units_out",
        cost_estimate=pl.CostEstimate(
            flops=4 * rows * half * 8 * TILE, bytes_accessed=20 << 20, transcendentals=0
        ),
    )(places, *mixed, *low, *high)


def attention_forward(query_heads, key_heads, value_heads, document_line):
    token_length = query_heads.shape[0]
    kv_dev = key_heads.shape[1] // HEAD_WIDTH
    per_kv = query_heads.shape[1] // key_heads.shape[1]
    block_rows = min(512, token_length)
    query_four = query_heads.reshape(token_length, kv_dev, per_kv, HEAD_WIDTH)
    key_three = key_heads.reshape(token_length, kv_dev, HEAD_WIDTH)
    value_three = value_heads.reshape(token_length, kv_dev, HEAD_WIDTH)
    key_pos = jnp.arange(token_length, dtype=jnp.int32)

    def scores_of(first_row):
        query_rows = lax.dynamic_slice_in_dim(query_four, first_row, block_rows, 0)
        row_docs = lax.dynamic_slice_in_dim(document_line, first_row, block_rows, 0)
        row_pos = first_row + jnp.arange(block_rows, dtype=jnp.int32)
        allowed = (row_docs[:, None] == document_line[None, :]) & (
            key_pos[None, :] <= row_pos[:, None]
        )
        raw_scores = jnp.einsum(
            "qkgd,skd->kgqs", query_rows, key_three, preferred_element_type=F32
        )
        return (jnp.where(allowed[None, None], SCORE_MULT * raw_scores, MASKED), query_rows)

    def forward_block(running_totals, block_index):
        logits, query_rows = scores_of(block_index * block_rows)
        row_max = jnp.max(logits, axis=-1, keepdims=True)
        shifted = jnp.exp(logits - row_max)
        row_sum = jnp.sum(shifted, axis=-1, keepdims=True)
        probs_low = (shifted / row_sum).astype(BF)
        mixed_rows = jnp.einsum(
            "kgqs,skd->qkgd", probs_low, value_three, preferred_element_type=F32
        )
        log_total = row_max[..., 0] + jnp.log(row_sum[..., 0])
        return (running_totals, (mixed_rows.reshape(block_rows, -1).astype(BF), log_total))

    block_ids = jnp.arange(token_length // block_rows, dtype=jnp.int32)
    _, (attn_blocks, log_totals) = lax.scan(forward_block, 0, block_ids)

    def backward(d_heads):
        d_heads_four = d_heads.reshape(token_length, kv_dev, per_kv, HEAD_WIDTH)

        def backward_block(running_totals, block_items):
            d_key_sum, d_value_sum = running_totals
            block_index, log_total = block_items
            first_row = block_index * block_rows
            logits, query_rows = scores_of(first_row)
            probs = jnp.exp(logits - log_total[..., None])
            d_rows = lax.dynamic_slice_in_dim(d_heads_four, first_row, block_rows, 0)
            d_probs = jnp.einsum(
                "qkgd,skd->kgqs", d_rows, value_three, preferred_element_type=F32
            )
            inner = jnp.sum(probs * d_probs, axis=-1, keepdims=True)
            d_logits = (probs * (d_probs - inner)).astype(BF)
            d_query_rows = SCORE_MULT * jnp.einsum(
                "kgqs,skd->qkgd", d_logits, key_three, preferred_element_type=F32
            )
            d_key_sum = d_key_sum + SCORE_MULT * jnp.einsum(
                "kgqs,qkgd->skd", d_logits, query_rows, preferred_element_type=F32
            )
            d_value_sum = d_value_sum + jnp.einsum(
                "kgqs,qkgd->skd", probs.astype(BF), d_rows, preferred_element_type=F32
            )
            return (
                (d_key_sum, d_value_sum),
                d_query_rows.astype(BF).reshape(block_rows, -1),
            )

        zero_keys = jnp.zeros((token_length, kv_dev, HEAD_WIDTH), F32)
        (d_key_sum, d_value_sum), d_query_blocks = lax.scan(
            backward_block, (zero_keys, zero_keys), (block_ids, log_totals)
        )
        return (
            d_query_blocks.reshape(token_length, -1),
            d_key_sum.astype(BF).reshape(token_length, -1),
            d_value_sum.astype(BF).reshape(token_length, -1),
        )

    return attn_blocks.reshape(token_length, -1), backward


def rope(values, cos_tab, sin_tab):
    rows, width = values.shape
    heads = values.astype(F32).reshape(rows, width // HEAD_WIDTH, HEAD_WIDTH)
    return rotate(heads, cos_tab, sin_tab).astype(BF).reshape(rows, width)


def plain_attention(
    x, weights, la_q, la_k, la_v, exit_q, exit_k, exit_v, document_line, *_
):
    rows = x.shape[0]
    q_cols, kv_cols = exit_q.shape[1], exit_k.shape[1]
    projected = low_dot(x[:, : weights[0].shape[0]], weights[0])
    cos_tab, sin_tab = rope_tables(jnp.arange(rows, dtype=jnp.int32), HEAD_WIDTH)
    query_rot = rope(projected[:, :q_cols] + low_dot(la_q, exit_q), cos_tab, sin_tab)
    key_rot = rope(
        projected[:, q_cols : q_cols + kv_cols] + low_dot(la_k, exit_k), cos_tab, sin_tab
    )
    value_low = (projected[:, q_cols + kv_cols :] + low_dot(la_v, exit_v)).astype(BF)
    attended, attention_back = attention_forward(query_rot, key_rot, value_low, document_line)

    def backward(d_heads, *_):
        d_query, d_key, d_value = attention_back(d_heads)
        return rope(d_query, cos_tab, -sin_tab), rope(d_key, cos_tab, -sin_tab), d_value

    return attended, lambda: attended, backward


def layer(mover, args):
    (
        tokens,
        token_document,
        document_adapter,
        attention_norm_gain,
        feedforward_norm_gain,
        query_weight,
        key_weight,
        value_weight,
        output_weight,
        gate_weight,
        up_weight,
        down_weight,
        attention_down_maps,
        query_exit_maps,
        key_value_exit_maps,
        output_entry_maps,
        output_exit_maps,
        feedforward_entry_maps,
        feedforward_exit_maps,
        down_entry_maps,
        down_exit_maps,
        cotangent,
    ) = args
    seq_size, wsh_size, s = mover.seq_size, mover.wsh_size, mover.s
    own_rows = tokens.shape[1]
    width = tokens.shape[2]
    adapters = attention_down_maps.shape[1]
    rank = query_exit_maps.shape[1]
    flat = adapters * rank
    doc_count = document_adapter.shape[1]
    q_cols = query_weight.shape[1] // seq_size
    kv_cols = key_weight.shape[1] // seq_size
    feature = width // seq_size
    row_block = width // wsh_size
    hidden = gate_weight.shape[1]
    hid_block = hidden // (wsh_size * seq_size)
    hid_own = hidden // seq_size

    def owners(docs):
        hot = (docs[:, None] == jnp.arange(doc_count, dtype=jnp.int32)[None, :]).astype(jnp.int32)
        return jnp.sum(hot * document_adapter[0][None, :], axis=1)

    def turned(maps):
        return maps.transpose(1, 2, 0).reshape(-1, maps.shape[0])

    def own_hidden(values, lower=0, upper=hid_own):
        parts, at = [], lower
        while at < upper:
            w = at // hid_block
            stop = min(upper, (w + 1) * hid_block)
            start = (w * seq_size + s) * hid_block + at - w * hid_block
            parts.append(cut(values, start, stop - at, 1))
            at = stop
        return parts

    qkv_local = jnp.concatenate(
        [
            cut(query_weight, s * q_cols, q_cols, 1),
            cut(key_weight, s * kv_cols, kv_cols, 1),
            cut(value_weight, s * kv_cols, kv_cols, 1),
        ],
        axis=1,
    )
    local_docs = token_document[0]
    own_owner = owners(local_docs)
    hidden_state = tokens[0].astype(F32)
    first_normed, scale_one = normed(hidden_state, attention_norm_gain)
    first_normed = first_normed.astype(BF)
    input_maps = turned(attention_down_maps)
    picked_first = reverse_product(first_normed, input_maps)
    picked_first = picked_first * adapter_mask(own_owner, 3 * rank, adapters)
    picked_first = fold(picked_first, 3 * rank, 0)
    last_lane = jnp.arange(LANES, dtype=jnp.int32)[None, :] == LANES - 1
    picked_first = jnp.where(last_lane, local_docs.astype(F32)[:, None], picked_first).astype(BF)

    half_width = width // 2
    down_local = cut(down_weight, s * hid_block, hid_block, 0)
    if mover.fast:
        chunks = [(0, 1), (2, 3), (4, 5), (6,), (7,)]
    else:
        chunks = [tuple(range(wsh_size))]
    chunk_bounds = [(c[0] * hid_block, (c[-1] + 1) * hid_block) for c in chunks]

    def gate_up_far(i, *deps):
        gate_late, up_late = after((gate_weight, up_weight), *deps)
        parts = own_hidden(gate_late, *chunk_bounds[i]) + own_hidden(up_late, *chunk_bounds[i])
        return mover.far(jnp.concatenate(parts, axis=1))

    output_gradient = cotangent[0].astype(F32)
    d_mlp_local = (RESIDUAL_MULT * output_gradient).astype(BF)
    first_cols = jnp.concatenate([mover.to_slots(first_normed, row_block), picked_first], axis=1)
    qkv_pair = mover.far(qkv_local)
    if mover.fast:
        d_mlp_other = lax.ppermute(d_mlp_local, "seq", Y_SWAP)
        first_other = after(lax.ppermute(first_cols, "seq", Y_SWAP), d_mlp_other)
        out_piece = mover.head_rows(output_weight)
        qkv_four = mover.near(qkv_pair)
        out_pair = mover.far(out_piece, qkv_pair)
        qkv_full = mover.across(qkv_four)
        first_all = mover.gather_rest(first_cols, first_other)
        out_four = mover.near(out_pair, qkv_four)
        low_pair = mover.far(down_local[:, :half_width], qkv_four)
        out_swapped = mover.across(out_four, qkv_full[1])
        out_full = mover.head_rows_done(out_swapped, output_weight.shape[0])
        d_mlp = mover.gather_rest(d_mlp_local, after(d_mlp_other, first_all))
        low_four = mover.near(low_pair, out_four)
        high_pair = mover.far(down_local[:, half_width:], low_pair, qkv_full[1])
        first_all = after(first_all, d_mlp)
    else:
        qkv_full = mover.across(qkv_pair)
        first_all = mover.gather_tokens(first_cols)
        d_mlp = mover.gather_tokens(d_mlp_local)
        out_full = mover.head_rows(output_weight)
        down_full = mover.across(down_local)[0]
    document_line = first_all[:, width + LANES - 1].astype(jnp.int32)
    owner = owners(document_line)
    mask_rank = adapter_mask(owner, rank, adapters)

    (
        query_exit_maps,
        key_value_exit_maps,
    ) = after((query_exit_maps, key_value_exit_maps), first_normed)
    query_exit = cut(query_exit_maps.reshape(flat, -1), s * q_cols, q_cols, 1)
    key_exit = cut(key_value_exit_maps[0].reshape(flat, -1), s * kv_cols, kv_cols, 1)
    value_exit = cut(key_value_exit_maps[1].reshape(flat, -1), s * kv_cols, kv_cols, 1)
    la_one = first_all[:, width:]
    la_q = spread(la_one, owner, rank, 0, adapters)
    la_k = spread(la_one, owner, rank, rank, adapters)
    la_v = spread(la_one, owner, rank, 2 * rank, adapters)
    token_length = first_all.shape[0]
    attend = fast_attention if mover.fast else plain_attention
    early, attend_rest, attention_back = attend(
        first_all, qkv_full, la_q, la_k, la_v, query_exit, key_exit, value_exit, document_line,
    )

    (
        feedforward_entry_maps,
        feedforward_exit_maps,
        down_entry_maps,
        down_exit_maps,
        output_entry_maps,
        output_exit_maps,
    ) = after(
        (
            feedforward_entry_maps,
            feedforward_exit_maps,
            down_entry_maps,
            down_exit_maps,
            output_entry_maps,
            output_exit_maps,
        ),
        early,
    )
    if mover.fast:
        low_rows = low_four.shape[0] // 2
        low_early = after(low_four[:low_rows], out_swapped[1], early)
        low_other = [
            lax.ppermute(low_early, "wsh", X_SWAP),
            lax.ppermute(low_four[low_rows:], "wsh", X_SWAP),
        ]
        down_low = (low_four, jnp.concatenate(low_other, axis=0))
        high_four = mover.near(high_pair, low_four, early)
        attended = attend_rest(out_full, high_pair)
        chunk_pairs = [gate_up_far(0, high_four)]
        attended = after(attended, high_four, low_other[0])
        down_high = mover.across(high_four)
        chunk_fours = [mover.near(chunk_pairs[0], high_four)]
        chunk_pairs.append(gate_up_far(1, chunk_pairs[0]))
    else:
        attended = attend_rest()

    out_entry = cut(turned(output_entry_maps), s * q_cols, q_cols, 1)
    out_exit = output_exit_maps.reshape(flat, -1)
    la_out_part = fold(reverse_product(attended, out_entry) * mask_rank, rank, 0)
    attn_sum = mover.scatter_tokens(low_dot(attended, out_full), la_out_part)
    la_out_own = attn_sum[1].astype(BF)
    attention_path = attn_sum[0] + low_dot(
        spread(la_out_own, own_owner, rank, 0, adapters), out_exit
    )
    middle = hidden_state + RESIDUAL_MULT * attention_path
    if mover.fast:
        middle = after(middle, low_other[1], chunk_pairs[0])

    second_normed, scale_two = normed(middle, feedforward_norm_gain)
    second_normed = second_normed.astype(BF)
    entry_maps = turned(feedforward_entry_maps)
    picked_second = reverse_product(second_normed, entry_maps) * adapter_mask(
        own_owner, 2 * rank, adapters
    )
    picked_second = fold(picked_second, 2 * rank, rank) + la_out_own.astype(F32)
    second_cols = jnp.concatenate(
        [mover.to_slots(second_normed, row_block), picked_second.astype(BF)], axis=1
    )
    if mover.fast:
        second_other = lax.ppermute(second_cols, "seq", Y_SWAP)
        second_all = mover.gather_rest(
            second_cols, after(second_other, down_high[1], chunk_fours[0], chunk_pairs[1])
        )
    else:
        second_all = mover.gather_tokens(second_cols)
    la_out = spread(second_all[:, width:], owner, rank, 0, adapters)
    la_gate = spread(second_all[:, width:], owner, rank, rank, adapters)
    la_up = spread(second_all[:, width:], owner, rank, 2 * rank, adapters)

    down_exit = down_exit_maps.reshape(flat, -1)
    d_la_d = (reverse_product(d_mlp, down_exit) * mask_rank).astype(BF)
    down_entry = jnp.concatenate(own_hidden(turned(down_entry_maps)), axis=1)
    all_exits = feedforward_exit_maps.reshape(2, flat, -1)
    exits = [jnp.concatenate(own_hidden(all_exits[i]), axis=1) for i in range(2)]
    units_found = []
    if mover.fast:
        chunk_weights = [mover.across(chunk_fours[0])]
        sums = None
        for i, units in enumerate(chunks):
            if i + 1 < len(chunks):
                deps = [chunk_fours[i]] + ([] if sums is None else [sums[0]])
                chunk_fours.append(mover.near(chunk_pairs[i + 1], *deps))
                chunk_weights.append(mover.across(chunk_fours[i + 1]))
            if i + 2 < len(chunks):
                deps = [chunk_pairs[i + 1], down_high[1] if sums is None else sums[0]]
                chunk_pairs.append(gate_up_far(i + 2, *deps))
            lower, upper = chunk_bounds[i]
            units_in = after(second_all, *chunk_fours[i + 1 : i + 2], *chunk_pairs[i + 2 : i + 3])
            mixed, d_gate, d_up, *sums = mlp_call(
                units,
                mover.z_slot(units[0] // 2),
                mover.x,
                units_in,
                chunk_weights[i],
                la_gate,
                la_up,
                exits[0][:, lower:upper],
                exits[1][:, lower:upper],
                d_mlp,
                down_low,
                down_high,
                d_la_d,
                down_entry[:, lower:upper],
                sums,
            )
            units_found.append((mixed, d_gate, d_up))
        d_second, d_la_both = sums
        d_la_gate, d_la_up = d_la_both[:, :flat], d_la_both[:, flat:]
    else:
        weights = mover.across(gate_up_far(0))[0]
        both = low_dot(second_all[:, :width], weights)
        gate = both[:, :hid_own] + low_dot(la_gate, exits[0])
        up = both[:, hid_own:] + low_dot(la_up, exits[1])
        d_mixed = reverse_product(d_mlp, down_full) + low_dot(d_la_d, down_entry)
        sigma = jax.nn.sigmoid(gate)
        swish = gate * sigma
        mixed = (swish * up).astype(BF)
        d_gate = (d_mixed * up * sigma * (1.0 + gate * (1.0 - sigma))).astype(BF)
        d_up = (d_mixed * swish).astype(BF)
        d_second = reverse_product(jnp.concatenate([d_gate, d_up], axis=1), weights)
        d_la_gate = reverse_product(d_gate, exits[0])
        d_la_up = reverse_product(d_up, exits[1])
        units_found.append((mixed, d_gate, d_up))
    d_la_two_part = fold(d_la_gate * mask_rank, rank, 0) + fold(d_la_up * mask_rank, rank, rank)
    d_second_sum = mover.scatter_tokens(d_second, d_la_two_part, mark="second")
    units_found[-1] = after(units_found[-1], mover.marks.get("second_away"))
    mixed_parts = [found[0] for found in units_found]
    gate_grads = [gradient_product(la_gate, found[1]) for found in units_found]
    up_grads = [gradient_product(la_up, found[2]) for found in units_found]
    entry_grads = [gradient_product(d_la_d, found[0]) for found in units_found]
    d_la_two_own = d_second_sum[1].astype(BF)
    d_second_own = mover.from_slots(d_second_sum[0], row_block) + low_dot(
        spread(d_la_two_own, own_owner, 2 * rank, 0, adapters), entry_maps
    )
    grad_middle = output_gradient + normed_back(
        middle, scale_two, feedforward_norm_gain, d_second_own
    )
    d_attn_own = (RESIDUAL_MULT * grad_middle).astype(BF)
    gate_grad = jnp.concatenate(gate_grads, axis=1)
    up_grad = jnp.concatenate(up_grads, axis=1)
    down_in_grad = jnp.concatenate(entry_grads, axis=1)
    d_attn_cols = jnp.concatenate([d_attn_own, d_la_two_own], axis=1)
    if mover.fast:
        packed = jnp.concatenate([pack(v) for v in (gate_grad, up_grad, down_in_grad)], axis=0)
        hidden_half = mover.sum_start(packed)
        d_attn_other = lax.ppermute(d_attn_cols, "seq", Y_SWAP)
        d_attn_all = mover.gather_rest(d_attn_cols, after(d_attn_other, hidden_half))
    else:
        d_attn_all = mover.gather_tokens(d_attn_cols)
    d_attn = d_attn_all[:, :width]

    mixed_all = jnp.concatenate(mixed_parts, axis=1)
    la_down_part = fold(reverse_product(mixed_all, down_entry) * mask_rank, rank, 0)
    if mover.fast:
        mlp_part = mlp_out_call(
            chunks, [mover.z_slot(i) for i in range(4)], mover.x, mixed_parts, down_low, down_high
        )
    else:
        mlp_part = low_dot(mixed_all, down_full)
    mlp_sum = mover.scatter_tokens(mlp_part, la_down_part, deps=(d_attn_all,), mark="mlp")
    if mover.fast:
        hidden_grads = mover.sum_hidden(
            hidden_half, (mover.marks["mlp"],), "hidden", (d_attn_all,)
        )
    else:
        hidden_grads = mover.plain_hidden([gate_grad, up_grad, down_in_grad], hid_block)
    hidden_sent = mover.marks.get("hidden", (None, None))
    la_down_own = mlp_sum[1].astype(BF)
    feedforward_path = mlp_sum[0] + low_dot(
        spread(la_down_own, own_owner, rank, 0, adapters), down_exit
    )
    layer_out = (middle + RESIDUAL_MULT * feedforward_path).astype(BF)[None]
    la_down = spread(mover.gather_tokens(la_down_own), owner, rank, 0, adapters)

    def own_features(slots):
        per = wsh_size // seq_size
        parts = [
            cut(slots, mover.slot_of(s * per + i) * row_block, row_block, 1) for i in range(per)
        ]
        return jnp.concatenate(parts, axis=1)

    d_la_two = spread(d_attn_all[:, width:], owner, 2 * rank, 0, adapters)
    entry_grad = gradient_product(d_la_two, own_features(second_all))
    down_out_grad = gradient_product(la_down, cut(d_mlp, s * feature, feature, 1))
    d_la_o = (reverse_product(d_attn, out_exit) * mask_rank).astype(BF)
    out_in_grad = gradient_product(d_la_o, attended)
    out_out_grad = gradient_product(la_out, cut(d_attn, s * feature, feature, 1))

    d_attended = (reverse_product(d_attn, out_full) + low_dot(d_la_o, out_entry)).astype(BF)
    d_query, d_key, d_value = attention_back(
        d_attended, (mover.marks.get("mlp"),), hidden_sent[:1]
    )
    d_la_one_part = (
        fold(reverse_product(d_query, query_exit) * mask_rank, rank, 0)
        + fold(reverse_product(d_key, key_exit) * mask_rank, rank, rank)
        + fold(reverse_product(d_value, value_exit) * mask_rank, rank, 2 * rank)
    )
    d_la_one = mover.sum_small(d_la_one_part.astype(BF), hidden_sent[1:]).astype(BF)
    d_qkv = jnp.concatenate([d_query, d_key, d_value], axis=1)
    d_qkv = after(d_qkv, d_la_one_part)
    d_first_sum = jnp.concatenate(
        mover.scatter_tokens(
            *[reverse_product(d_qkv, half) for half in qkv_full],
            deps=(d_la_one,),
            late=hidden_grads,
            mark="first",
        ),
        axis=1,
    )
    d_la_one_own = cut(d_la_one, s * own_rows, own_rows, 0)
    d_first = mover.from_slots(d_first_sum, row_block) + low_dot(
        spread(d_la_one_own, own_owner, 3 * rank, 0, adapters), input_maps
    )
    hidden_gradient = grad_middle + normed_back(
        hidden_state, scale_one, attention_norm_gain, d_first
    )
    attention_in_grad = gradient_product(
        spread(d_la_one, owner, 3 * rank, 0, adapters), own_features(first_all)
    )
    query_out_grad = gradient_product(la_q, d_query)
    key_out_grad = gradient_product(la_k, d_key)
    value_out_grad = gradient_product(la_v, d_value)
    first_sent = mover.marks.get("first")
    early_grads = mover.sum_features(
        [query_out_grad, down_out_grad, entry_grad, out_in_grad, out_out_grad],
        key_out_grad,
        value_out_grad,
        deps=(first_sent,),
        mark="features",
    )
    (last_grad,) = mover.sum_features(
        [attention_in_grad],
        mid=(mover.marks.get("first_away"),),
        deps=(mover.marks.get("features"),),
        late=early_grads,
    )

    def back(values, shape):
        return values.reshape(shape[1], shape[2], shape[0]).transpose(2, 0, 1)

    return (
        layer_out,
        hidden_gradient[None],
        back(last_grad, attention_down_maps.shape),
        early_grads[0].reshape(query_exit_maps.shape),
        early_grads[5].reshape(key_value_exit_maps.shape),
        back(early_grads[3], output_entry_maps.shape),
        early_grads[4].reshape(output_exit_maps.shape),
        back(early_grads[2], feedforward_entry_maps.shape),
        hidden_grads[0].reshape(feedforward_exit_maps.shape),
        back(hidden_grads[1], down_entry_maps.shape),
        early_grads[1].reshape(down_exit_maps.shape),
    )


def solution(mesh):
    seq_size, wsh_size = mesh.shape["seq"], mesh.shape["wsh"]

    def on_device(*args):
        return layer(Mover(seq_size, wsh_size), args)

    rows = P("wsh", None)
    stream = P("wsh", "seq", None)
    in_specs = (stream, P("wsh", "seq"), rows, P(), P()) + (rows,) * 7 + (P(),) * 9 + (stream,)
    out_specs = (stream, stream) + (P(),) * 9
    return jax.shard_map(
        on_device, mesh=mesh, in_specs=in_specs, out_specs=out_specs, check_vma=False
    )
```

```python
import jax
import jax.numpy as jnp
from jax import lax
from jax.experimental import pallas as pl
from jax.experimental.pallas import tpu as pltpu
from jax.sharding import PartitionSpec as P

QUERY_HEADS = 32
KEY_HEADS = 8
HEAD_WIDTH = 64
LANES = 128
PACK = 512
TILE = 256

EPSILON = 1e-05
RESIDUAL_MULT = 0.22
SCORE_MULT = 0.015625
ROPE_BASE = 10000000.0
MASKED = -1e30

BF = jnp.bfloat16
F32 = jnp.float32

CORE_SWAP = [(s, s ^ 1) for s in range(4)]
Y_SWAP = [(s, s ^ 2) for s in range(4)]
X_SWAP = [(w, w ^ 1) for w in range(8)]
NEAR_SWAP = [(w, w ^ 2) for w in range(8)]
FAR_SWAP = [(w, w ^ 4) for w in range(8)]


def z_shift(steps):
    return [(2 * z + x, 2 * ((z + steps) % 4) + x) for z in range(4) for x in range(2)]


def low_dot(left, right):
    return jnp.dot(left, right, preferred_element_type=F32)


def gradient_product(left, right):
    return lax.dot_general(left, right, (((0,), (0,)), ((), ())), preferred_element_type=F32)


def reverse_product(left, right):
    return lax.dot_general(left, right, (((1,), (1,)), ((), ())), preferred_element_type=F32)


def normed(values, gain):
    norm_scale = lax.rsqrt(jnp.mean(values * values, axis=-1, keepdims=True) + EPSILON)
    return (values * norm_scale * gain, norm_scale)


def normed_back(values, norm_scale, gain, grad_in):
    scaled = grad_in * gain
    cubed = norm_scale * norm_scale * norm_scale
    return norm_scale * scaled - values * cubed * jnp.mean(scaled * values, axis=-1, keepdims=True)


def rope_tables(positions, head_size):
    half_size = head_size // 2
    inv_freq = ROPE_BASE ** (-(jnp.arange(half_size).astype(F32) * 2.0) / head_size)
    angles = positions.astype(F32)[:, None] * inv_freq[None, :]
    return (jnp.cos(angles)[:, None, :], jnp.sin(angles)[:, None, :])


def rotate(values, cos_tab, sin_tab):
    half_size = values.shape[-1] // 2
    former = values[..., :half_size]
    latter = values[..., half_size:]
    return jnp.concatenate(
        [former * cos_tab - latter * sin_tab, latter * cos_tab + former * sin_tab], axis=-1
    )


def cut(values, start, size, axis):
    return lax.dynamic_slice_in_dim(values, start, size, axis)


def pick(values, index, axis):
    return lax.dynamic_index_in_dim(values, index, axis, keepdims=False)


def adapter_mask(owner, ranks, adapters):
    lane = jnp.arange(adapters * ranks, dtype=jnp.int32) // ranks
    return (owner[:, None] == lane[None, :]).astype(F32)


def fold(masked, ranks, offset):
    rows = jnp.arange(masked.shape[1], dtype=jnp.int32) % ranks
    lanes = jnp.arange(LANES, dtype=jnp.int32) - offset
    return low_dot(masked.astype(BF), (rows[:, None] == lanes[None, :]).astype(BF))


def spread(folded, owner, ranks, offset, adapters):
    rows = jnp.arange(LANES, dtype=jnp.int32) - offset
    lanes = jnp.arange(adapters * ranks, dtype=jnp.int32) % ranks
    wide = low_dot(folded.astype(BF), (rows[:, None] == lanes[None, :]).astype(BF))
    return (wide * adapter_mask(owner, ranks, adapters)).astype(BF)


def pack(values):
    parts = [values[:, i : i + PACK] for i in range(0, values.shape[1], PACK)]
    return jnp.concatenate(parts, axis=0)


def after(values, *deps):
    deps = [d for d in deps if d is not None]
    if not deps:
        return values
    return lax.optimization_barrier((values, tuple(deps)))[0]


class Mover:
    def __init__(self, seq_size, wsh_size):
        self.seq_size, self.wsh_size = seq_size, wsh_size
        self.fast = seq_size == 4 and wsh_size == 8
        self.s, self.w = lax.axis_index("seq"), lax.axis_index("wsh")
        self.y, self.c = self.s // 2, self.s % 2
        self.z, self.x = self.w // 2, self.w % 2
        self.marks = {}

    def far(self, chunk, *deps):
        chunk = after(chunk, *deps)
        if not self.fast:
            return chunk
        return jnp.concatenate([chunk, lax.ppermute(chunk, "wsh", FAR_SWAP)], axis=0)

    def near(self, pair, *deps):
        pair = after(pair, *deps)
        if not self.fast:
            return pair
        return jnp.concatenate([pair, lax.ppermute(pair, "wsh", NEAR_SWAP)], axis=0)

    def across(self, four, *deps):
        four = after(four, *deps)
        if not self.fast:
            return (lax.all_gather(four, "wsh", axis=0, tiled=True),)
        return four, lax.ppermute(four, "wsh", X_SWAP)

    def swap_bits(self, d):
        return d // 2 + 2 * (d % 2)

    def slot_owner(self, k):
        if not self.fast:
            return k
        return 2 * (self.z ^ self.swap_bits(k % 4)) + (self.x ^ (k // 4))

    def slot_of(self, w):
        if not self.fast:
            return w
        return self.z_slot(w // 2) + 4 * (self.x ^ (w % 2))

    def z_slot(self, z):
        return self.swap_bits(self.z ^ z)

    def to_slots(self, values, block):
        if not self.fast:
            return values
        parts = [cut(values, self.slot_owner(k) * block, block, 1) for k in range(self.wsh_size)]
        return jnp.concatenate(parts, axis=1)

    def from_slots(self, values, block):
        if not self.fast:
            return values
        parts = [cut(values, self.slot_of(w) * block, block, 1) for w in range(self.wsh_size)]
        return jnp.concatenate(parts, axis=1)

    def head_rows(self, weight):
        rows = weight.shape[0]
        per = self.wsh_size // self.seq_size
        if not self.fast:
            return cut(
                lax.all_gather(weight, "wsh", axis=0, tiled=True),
                self.s * per * rows,
                per * rows,
                0,
            )
        piece = rows // 4

        def part(z):
            return cut(weight, z * piece, piece, 0)

        def pairs(senders, step):
            return [
                (8 * s + 2 * (s ^ sender) + x, 8 * s + 2 * (s ^ sender ^ step) + x)
                for s in range(4)
                for sender in senders
                for x in range(2)
            ]

        z, axes = self.z, ("seq", "wsh")
        away = jnp.concatenate([part(z ^ 2), part(z ^ 3)], axis=0)
        got = lax.ppermute(away, axes, pairs((0,), 2))
        first = z == self.s
        mine = jnp.where(first, part(z), got[:piece])
        away = jnp.where(first, part(z ^ 1), got[piece:])
        got = lax.ppermute(away, axes, pairs((0, 2), 1))
        return jnp.where(first | (z == (self.s ^ 2)), mine, got)

    def head_rows_done(self, halves, rows):
        piece = rows // 4
        out = []
        for shard in range(2):
            half = jnp.where(self.x == shard, halves[0], halves[1])
            blocks = half.reshape(4, piece, half.shape[1])
            out += [pick(blocks, self.z_slot(j), 0) for j in range(4)]
        return jnp.concatenate(out, axis=0)

    def gather_tokens(self, values):
        if not self.fast:
            return lax.all_gather(values, "seq", axis=0, tiled=True)
        return self.gather_rest(values, lax.ppermute(values, "seq", Y_SWAP))

    def gather_rest(self, values, other):
        first = self.y == 0
        column = jnp.stack([jnp.where(first, values, other), jnp.where(first, other, values)])
        partner = lax.ppermute(column, "seq", CORE_SWAP)
        first = self.c == 0
        whole = jnp.stack(
            [jnp.where(first, column, partner), jnp.where(first, partner, column)], axis=1
        )
        return whole.reshape((4 * values.shape[0],) + values.shape[1:])

    def scatter_tokens(self, *partials, deps=(), late=(), mark=None):
        if not self.fast:
            return [
                lax.psum_scatter(v.astype(BF), "seq", scatter_dimension=0, tiled=True).astype(F32)
                for v in partials
            ]
        rows = partials[0].shape[0] // 4
        blocks = [v.reshape(2, 2, rows, v.shape[1]) for v in partials]
        out = jnp.concatenate([pick(v, 1 - self.c, 1).astype(BF) for v in blocks], axis=2)
        got = lax.ppermute(out, "seq", CORE_SWAP).astype(F32)
        mine = jnp.concatenate([pick(v, self.c, 1) for v in blocks], axis=2)
        away = (pick(mine, 1 - self.y, 0) + pick(got, 1 - self.y, 0)).astype(BF)
        other = lax.ppermute(after(away, *deps), "seq", Y_SWAP)
        self.marks[mark] = other
        if mark is not None:
            self.marks[mark + "_away"] = away
        other = after(other, *late).astype(F32)
        total = pick(mine, self.y, 0) + pick(got, self.y, 0) + other
        found, at = [], 0
        for v in partials:
            found.append(total[:, at : at + v.shape[1]])
            at += v.shape[1]
        return found

    def sum_small(self, partial, deps=()):
        if not self.fast:
            return lax.psum(partial, "seq")
        total = partial.astype(F32) + lax.ppermute(partial, "seq", CORE_SWAP).astype(F32)
        other = lax.ppermute(after(total.astype(BF), *deps), "seq", Y_SWAP)
        return total + other.astype(F32)

    def sum_plain(self, grad):
        total = lax.psum(grad.astype(BF), "wsh")
        return lax.all_gather(total.astype(BF), "seq", axis=0).astype(F32)

    def plain_hidden(self, grads, hid_block):
        found = []
        for grad in grads:
            rows = grad.shape[0]
            wide = self.sum_plain(grad).reshape(self.seq_size, rows, self.wsh_size, hid_block)
            found.append(wide.transpose(1, 2, 0, 3).reshape(rows, -1))
        return [jnp.stack(found[:2]), found[2]]

    def sum_hidden(self, half, deps, mark, early):
        parts = self.sum_end(half, deps, mark, early)
        s = self.s.astype(jnp.int32)[None]
        return [
            final_hidden(parts, s, 0, 2),
            final_hidden(parts, s, 8 * LANES, 1)[0],
        ]

    def sum_features(self, grads, key=None, value=None, mid=(), back=(), deps=(), late=(), mark=None):
        if not self.fast:
            grads = grads + ([key, value] if key is not None else [])
            found = []
            for grad in grads:
                found.append(self.sum_plain(grad).transpose(1, 0, 2).reshape(grad.shape[0], -1))
            return found[:-2] + [jnp.stack(found[-2:])] if key is not None else found
        packed = list(grads)
        if key is not None:
            rest = jnp.zeros((key.shape[0], PACK - 2 * LANES), F32)
            packed.append(jnp.concatenate([key, value, rest], axis=1))
        half = self.sum_start(jnp.concatenate(packed, axis=0), mid, back)
        parts = self.sum_end(half, deps, late=late)
        self.marks[mark] = parts[2]
        s = self.s.astype(jnp.int32)[None]
        found, at = [], 0
        for grad in grads:
            found.append(final_features(parts, s, at, grad.shape[0]))
            at += grad.shape[0]
        if key is not None:
            found.append(final_kv(parts, s, at))
        return found

    def sum_start(self, packed, mid=(), back=()):
        rows = packed.shape[0]
        halves = packed.reshape(2, rows // 2, PACK)
        got = lax.ppermute(pick(halves, 1 - self.x, 0).astype(BF), "wsh", X_SWAP)
        half = pick(halves, self.x, 0) + got.astype(F32)
        blocks = after(half, *mid).reshape(4, rows // 8, PACK)
        total = pick(blocks, self.z, 0)
        for r in range(1, 4):
            out = pick(blocks, (self.z + r) % 4, 0).astype(BF)
            total = total + lax.ppermute(out, "wsh", z_shift(r)).astype(F32)
        own = after(total.astype(BF), *back)
        got = [own] + [lax.ppermute(own, "wsh", z_shift(r)) for r in range(1, 4)]
        ring = jnp.stack(got)
        return jnp.concatenate([pick(ring, (self.z - j) % 4, 0) for j in range(4)], axis=0)

    def sum_end(self, half, deps=(), mark=None, early=(), late=()):
        rows = 2 * half.shape[0]
        half = after(half, *early)
        other = lax.ppermute(half, "wsh", X_SWAP)
        first = self.x == 0
        part = jnp.concatenate([jnp.where(first, half, other), jnp.where(first, other, half)])
        core = lax.ppermute(part, "seq", CORE_SWAP)
        if mark is None:
            other = after(lax.ppermute(after(part, *deps), "seq", Y_SWAP), *late)
        else:
            top = lax.ppermute(after(part[: rows // 2], *deps), "seq", Y_SWAP)
            rest = lax.ppermute(after(part[rows // 2 :], top), "seq", Y_SWAP)
            self.marks[mark] = (top, rest)
            other = jnp.concatenate([top, rest], axis=0)
        return part, core, other, lax.ppermute(other, "seq", CORE_SWAP)


def final_body(s_ref, own, core, other, last, out_ref):
    columns = own.shape[-1]
    for k in range(4):
        place = s_ref[0] ^ k
        low = jnp.where(place % 2 == 0, own[...], core[...])
        high = jnp.where(place % 2 == 0, other[...], last[...])
        value = jnp.where(place < 2, low, high).astype(F32)
        at = slice(k * columns, (k + 1) * columns)
        if len(out_ref.shape) == 3:
            out_ref[0, :, at] = value
        else:
            out_ref[:, at] = value


def final_call(parts, s, grid, part_block, part_map, out_shape, out_block, out_map):
    return pl.pallas_call(
        final_body,
        grid_spec=pltpu.PrefetchScalarGridSpec(
            num_scalar_prefetch=1,
            grid=grid,
            in_specs=[pl.BlockSpec(part_block, part_map)] * 4,
            out_specs=pl.BlockSpec(out_block, out_map),
        ),
        out_shape=jax.ShapeDtypeStruct(out_shape, F32),
        name="finish",
    )(s, *parts)


def final_features(parts, s, row, rows):
    at = row // LANES
    return final_call(
        parts,
        s,
        (rows // LANES,),
        (LANES, PACK),
        lambda i, _: (at + i, 0),
        (rows, 4 * PACK),
        (LANES, 4 * PACK),
        lambda i, _: (i, 0),
    )


def final_hidden(parts, s, row, count):
    at = row // LANES
    return final_call(
        parts,
        s,
        (count, 8),
        (LANES, TILE),
        lambda n, w, _: (at + 4 * n + w // 2, w % 2),
        (count, LANES, 32 * TILE),
        (1, LANES, 4 * TILE),
        lambda n, w, _: (n, 0, w),
    )


def final_kv(parts, s, row):
    at = row // LANES
    return final_call(
        parts,
        s,
        (2,),
        (LANES, LANES),
        lambda n, _: (at, n),
        (2, LANES, 4 * LANES),
        (1, LANES, 4 * LANES),
        lambda n, _: (n, 0, 0),
    )


def half_lanes(rows, half):
    lane = lax.broadcasted_iota(jnp.int32, (rows, LANES), 1)
    return (lane < HEAD_WIDTH) if half == 0 else (lane >= HEAD_WIDTH)


def turn(values, cos_tab, sin_tab):
    lane = lax.broadcasted_iota(jnp.int32, values.shape, 1)
    swapped = jnp.where(
        lane % HEAD_WIDTH < HEAD_WIDTH // 2,
        pltpu.roll(values, LANES - HEAD_WIDTH // 2, 1),
        pltpu.roll(values, HEAD_WIDTH // 2, 1),
    )
    return values * cos_tab + swapped * sin_tab


def twice(values, half):
    other = pltpu.roll(values, HEAD_WIDTH, 1)
    first = half_lanes(values.shape[0], 0)
    return jnp.where(first, values, other) if half == 0 else jnp.where(first, other, values)


def qkv_body(x_ref, w_own, w_other, la_q, la_k, la_v, exit_q, exit_kv, cos_ref, sin_ref, q_ref, k_ref, v_ref):
    cos_tab, sin_tab = cos_ref[...], sin_ref[...]
    half = w_own.shape[0]
    product = low_dot(x_ref[:, :half], w_own[...]) + low_dot(x_ref[:, half:], w_other[...])
    q_cols = q_ref.shape[1]
    query = product[:, :q_cols] + low_dot(la_q[...], exit_q[...])
    for i in range(0, q_cols, LANES):
        q_ref[:, i : i + LANES] = turn(query[:, i : i + LANES], cos_tab, sin_tab).astype(BF)
    key = product[:, q_cols : q_cols + LANES] + low_dot(la_k[...], exit_kv[0])
    key = turn(key, cos_tab, sin_tab)
    value = product[:, q_cols + LANES :] + low_dot(la_v[...], exit_kv[1])
    for half in range(2):
        k_ref[:, half * LANES : (half + 1) * LANES] = twice(key, half).astype(BF)
        v_ref[:, half * LANES : (half + 1) * LANES] = twice(value, half).astype(BF)


def qkv_call(x, weights, la_q, la_k, la_v, exit_q, exit_kv, cos_tab, sin_tab):
    rows, width = x.shape[0], 2 * weights[0].shape[0]
    q_cols = exit_q.shape[1]

    def tile(columns):
        return pl.BlockSpec((TILE, columns), lambda i: (i, 0))

    return pl.pallas_call(
        qkv_body,
        grid=(rows // TILE,),
        in_specs=[
            tile(width),
            pl.BlockSpec(weights[0].shape, lambda i: (0, 0)),
            pl.BlockSpec(weights[1].shape, lambda i: (0, 0)),
            tile(LANES),
            tile(LANES),
            tile(LANES),
            pl.BlockSpec(exit_q.shape, lambda i: (0, 0)),
            pl.BlockSpec(exit_kv.shape, lambda i: (0, 0, 0)),
            tile(LANES),
            tile(LANES),
        ],
        out_specs=[tile(q_cols), tile(2 * LANES), tile(2 * LANES)],
        out_shape=[
            jax.ShapeDtypeStruct((rows, q_cols), BF),
            jax.ShapeDtypeStruct((rows, 2 * LANES), BF),
            jax.ShapeDtypeStruct((rows, 2 * LANES), BF),
        ],
        name="qkv",
        cost_estimate=pl.CostEstimate(
            flops=2 * rows * width * weights[0].shape[1], bytes_accessed=12 << 20, transcendentals=0
        ),
    )(x, *weights, la_q, la_k, la_v, exit_q, exit_kv, cos_tab, sin_tab)


def allowed_pairs(i, t, doc_col, doc_row):
    start = pl.multiple_of(t * TILE, TILE)
    rows = i * TILE + lax.broadcasted_iota(jnp.int32, (TILE, TILE), 0)
    keys = start + lax.broadcasted_iota(jnp.int32, (TILE, TILE), 1)
    return (doc_col[...] == doc_row[:, pl.ds(start, TILE)]) & (keys <= rows)


def forward_body(first_ref, q_ref, k_ref, v_ref, doc_col, doc_row, o_ref, lse_ref, m_s, l_s, acc_s):
    i = pl.program_id(0)
    m_s[...] = jnp.full_like(m_s, MASKED)
    l_s[...] = jnp.zeros_like(l_s)
    acc_s[...] = jnp.zeros_like(acc_s)

    def step(t, carry):
        allowed = allowed_pairs(i, t, doc_col, doc_row)
        start = pl.multiple_of(t * TILE, TILE)
        keys, vals = k_ref[pl.ds(start, TILE), :], v_ref[pl.ds(start, TILE), :]
        for h in range(4):
            pair = q_ref[:, (h // 2) * LANES : (h // 2 + 1) * LANES]
            query = jnp.where(half_lanes(TILE, h % 2), pair, jnp.zeros_like(pair))
            logits = jnp.where(allowed, SCORE_MULT * reverse_product(query, keys), MASKED)
            old = m_s[h]
            top = jnp.maximum(old, jnp.max(logits, axis=1, keepdims=True))
            shrink = jnp.exp(old - top)
            shifted = jnp.exp(logits - top)
            m_s[h] = top
            l_s[h] = l_s[h] * shrink + jnp.sum(shifted, axis=1, keepdims=True)
            acc_s[h] = acc_s[h] * shrink + low_dot(shifted.astype(BF), vals)
        return carry

    lax.fori_loop(first_ref[i], i + 1, step, 0)
    lane = lax.broadcasted_iota(jnp.int32, (TILE, LANES), 1)
    total = jnp.zeros((TILE, LANES), F32)
    for p in range(2):
        both = [acc_s[2 * p + n] / l_s[2 * p + n] for n in range(2)]
        o_ref[:, p * LANES : (p + 1) * LANES] = jnp.where(
            half_lanes(TILE, 0), both[0], both[1]
        ).astype(BF)
    for h in range(4):
        total = jnp.where(lane == h, m_s[h] + jnp.log(l_s[h]), total)
    lse_ref[...] = total


def attention_call(j, first, query, keys, values, doc_col, doc_row):
    rows = query.shape[0]
    group = query.shape[1] // 2
    return pl.pallas_call(
        forward_body,
        grid_spec=pltpu.PrefetchScalarGridSpec(
            num_scalar_prefetch=1,
            grid=(rows // TILE,),
            in_specs=[
                pl.BlockSpec((TILE, group), lambda i, _: (i, j)),
                pl.BlockSpec((rows, LANES), lambda i, _: (0, j)),
                pl.BlockSpec((rows, LANES), lambda i, _: (0, j)),
                pl.BlockSpec((TILE, 1), lambda i, _: (i, 0)),
                pl.BlockSpec((1, rows), lambda i, _: (0, 0)),
            ],
            out_specs=[
                pl.BlockSpec((TILE, group), lambda i, _: (i, 0)),
                pl.BlockSpec((TILE, LANES), lambda i, _: (i, 0)),
            ],
            scratch_shapes=[
                pltpu.VMEM((4, TILE, 1), F32),
                pltpu.VMEM((4, TILE, 1), F32),
                pltpu.VMEM((4, TILE, LANES), F32),
            ],
        ),
        out_shape=[
            jax.ShapeDtypeStruct((rows, group), BF),
            jax.ShapeDtypeStruct((rows, LANES), F32),
        ],
        name="attention",
        cost_estimate=pl.CostEstimate(
            flops=4 * 4 * rows * rows * LANES,
            bytes_accessed=3 << 20,
            transcendentals=4 * rows * rows,
        ),
    )(first, query, keys, values, doc_col, doc_row)


def backward_body(
    first_ref, q_ref, k_ref, v_ref, do_ref, o_ref, lse_ref, doc_col, doc_row, cos_ref, sin_ref,
    cos_all, sin_all, dq_ref, dk_ref, dv_ref, dq_s, dk_s, dv_s,
):
    i = pl.program_id(0)

    @pl.when(i == 0)
    def _():
        dk_s[...] = jnp.zeros_like(dk_s)
        dv_s[...] = jnp.zeros_like(dv_s)

    dq_s[...] = jnp.zeros_like(dq_s)
    queries, grads, deltas = [], [], []
    for h in range(4):
        at = slice((h // 2) * LANES, (h // 2 + 1) * LANES)
        half = half_lanes(TILE, h % 2)
        pair, grad = q_ref[:, at], do_ref[:, at]
        queries.append(jnp.where(half, pair, jnp.zeros_like(pair)))
        grads.append(jnp.where(half, grad, jnp.zeros_like(grad)))
        product = grads[h].astype(F32) * o_ref[:, at].astype(F32)
        deltas.append(jnp.sum(product, axis=1, keepdims=True))

    def step(t, carry):
        allowed = allowed_pairs(i, t, doc_col, doc_row)
        start = pl.multiple_of(t * TILE, TILE)
        at = pl.ds(start, TILE)
        keys, vals = k_ref[at, :], v_ref[at, :]
        dk, dv = dk_s[at, :], dv_s[at, :]
        for h in range(4):
            logits = jnp.where(allowed, SCORE_MULT * reverse_product(queries[h], keys), MASKED)
            probs = jnp.exp(logits - lse_ref[:, h : h + 1])
            d_probs = reverse_product(grads[h], vals)
            d_logits = (probs * (d_probs - deltas[h])).astype(BF)
            dq_s[h] = dq_s[h] + low_dot(d_logits, keys)
            dk = dk + gradient_product(d_logits, queries[h])
            dv = dv + gradient_product(probs.astype(BF), grads[h])
        dk_s[at, :] = dk
        dv_s[at, :] = dv
        return carry

    lax.fori_loop(first_ref[i], i + 1, step, 0)
    for p in range(2):
        both = jnp.where(half_lanes(TILE, 0), dq_s[2 * p], dq_s[2 * p + 1])
        both = (SCORE_MULT * both).astype(BF).astype(F32)
        dq_ref[:, p * LANES : (p + 1) * LANES] = turn(both, cos_ref[...], -sin_ref[...]).astype(BF)

    @pl.when(i == pl.num_programs(0) - 1)
    def _():
        def finish(t, carry):
            at = pl.ds(pl.multiple_of(t * TILE, TILE), TILE)
            dk, dv = dk_s[at, :], dv_s[at, :]
            dk = (SCORE_MULT * (dk + pltpu.roll(dk, HEAD_WIDTH, 1))).astype(BF).astype(F32)
            dk_ref[at, :] = turn(dk, cos_all[at, :], -sin_all[at, :]).astype(BF)
            dv_ref[at, :] = (dv + pltpu.roll(dv, HEAD_WIDTH, 1)).astype(BF)
            return carry

        lax.fori_loop(0, pl.num_programs(0), finish, 0)


def attention_back_call(
    j, first, query, keys, values, d_out, out, lse, doc_col, doc_row, cos_tab, sin_tab
):
    rows = query.shape[0]
    group = query.shape[1] // 2
    whole = pl.BlockSpec((rows, LANES), lambda i, _: (0, j))
    tile = pl.BlockSpec((TILE, group), lambda i, _: (i, j))
    table = pl.BlockSpec((TILE, LANES), lambda i, _: (i, 0))
    table_all = pl.BlockSpec((rows, LANES), lambda i, _: (0, 0))
    own_tile = pl.BlockSpec((TILE, group), lambda i, _: (i, 0))
    return pl.pallas_call(
        backward_body,
        grid_spec=pltpu.PrefetchScalarGridSpec(
            num_scalar_prefetch=1,
            grid=(rows // TILE,),
            in_specs=[
                tile,
                whole,
                whole,
                tile,
                own_tile,
                table,
                pl.BlockSpec((TILE, 1), lambda i, _: (i, 0)),
                pl.BlockSpec((1, rows), lambda i, _: (0, 0)),
                table,
                table,
                table_all,
                table_all,
            ],
            out_specs=[own_tile, table_all, table_all],
            scratch_shapes=[
                pltpu.VMEM((4, TILE, LANES), F32),
                pltpu.VMEM((rows, LANES), F32),
                pltpu.VMEM((rows, LANES), F32),
            ],
        ),
        out_shape=[
            jax.ShapeDtypeStruct((rows, group), BF),
            jax.ShapeDtypeStruct((rows, LANES), BF),
            jax.ShapeDtypeStruct((rows, LANES), BF),
        ],
        name="attention_back",
        cost_estimate=pl.CostEstimate(
            flops=4 * 10 * rows * rows * LANES,
            bytes_accessed=5 << 20,
            transcendentals=4 * rows * rows,
        ),
    )(first, query, keys, values, d_out, out, lse, doc_col, doc_row, cos_tab, sin_tab, cos_tab, sin_tab)


def fast_attention(
    x, weights, la_q, la_k, la_v, exit_q, exit_k, exit_v, document_line
):
    rows = x.shape[0]
    half = HEAD_WIDTH // 2
    cos_tab, sin_tab = rope_tables(jnp.arange(rows, dtype=jnp.int32), HEAD_WIDTH)
    cos_tab = jnp.tile(cos_tab.reshape(rows, half), (1, 4))
    sin_tab = sin_tab.reshape(rows, half)
    sin_tab = jnp.tile(jnp.concatenate([-sin_tab, sin_tab], axis=1), (1, 2))
    first_docs = document_line[::TILE]
    first = jnp.sum((document_line[None, :] < first_docs[:, None]).astype(jnp.int32), axis=1)
    first = first // TILE
    doc_col, doc_row = document_line[:, None], document_line[None, :]
    query, keys, values = qkv_call(
        x, weights, la_q, la_k, la_v, exit_q, jnp.stack([exit_k, exit_v]), cos_tab, sin_tab
    )
    early = attention_call(0, first, query, keys, values, doc_col, doc_row)
    found = [early]

    def finish(*deps):
        query_late = after(query, early[0], *deps)
        found.append(attention_call(1, first, query_late, keys, values, doc_col, doc_row))
        return jnp.concatenate([early[0], found[1][0]], axis=1)

    def backward(d_heads, between, behind):
        back = []
        for j in range(2):
            if j:
                d_heads = after(d_heads, back[0][1], *between)
            args = (first, query, keys, values, d_heads, *found[j], doc_col, doc_row)
            back.append(attention_back_call(j, *args, cos_tab, sin_tab))
        back[1] = after(back[1], *behind)
        lane = jnp.arange(LANES, dtype=jnp.int32)[None, :] < HEAD_WIDTH
        d_query = jnp.concatenate([back[0][0], back[1][0]], axis=1)
        d_key = jnp.where(lane, back[0][1], back[1][1])
        d_value = jnp.where(lane, back[0][2], back[1][2])
        return d_query, d_key, d_value

    return early[0], finish, backward


def units_rows(at_own, own, other):
    return jnp.where(at_own, own[...], other[...])


def mlp_body(owners, add, sc, n2, w_own, w_other, la_gate, la_up, exit_gate, exit_up, d_mlp,
             low_own, low_other, high_own, high_other, d_la_d, entry, *rest):
    if add:
        sum_in, la_in, mixed_ref, gate_ref, up_ref, sum_ref, la_ref = rest
    else:
        mixed_ref, gate_ref, up_ref, sum_ref, la_ref = rest
    half = w_own.shape[0]
    size = TILE * len(owners)
    both = low_dot(n2[:, :half], w_own[...]) + low_dot(n2[:, half:], w_other[...])
    gate = both[:, :size] + low_dot(la_gate[...], exit_gate[...])
    up = both[:, size:] + low_dot(la_up[...], exit_up[...])
    parts = []
    for w in owners:
        at_own = sc[1] == w % 2
        parts.append(
            reverse_product(d_mlp[:, :half], units_rows(at_own, low_own, low_other))
            + reverse_product(d_mlp[:, half:], units_rows(at_own, high_own, high_other))
        )
    d_mixed = jnp.concatenate(parts, axis=1) + low_dot(d_la_d[...], entry[...])
    sigma = jax.nn.sigmoid(gate)
    swish = gate * sigma
    mixed_ref[...] = (swish * up).astype(BF)
    d_gate = (d_mixed * up * sigma * (1.0 + gate * (1.0 - sigma))).astype(BF)
    d_up = (d_mixed * swish).astype(BF)
    gate_ref[...] = d_gate
    up_ref[...] = d_up
    d_both = jnp.concatenate([d_gate, d_up], axis=1)
    sum_own, sum_other = reverse_product(d_both, w_own[...]), reverse_product(d_both, w_other[...])
    back_gate, back_up = reverse_product(d_gate, exit_gate[...]), reverse_product(d_up, exit_up[...])
    if add:
        sum_own, sum_other = sum_own + sum_in[:, :half], sum_other + sum_in[:, half:]
        back_gate, back_up = back_gate + la_in[:, :LANES], back_up + la_in[:, LANES:]
    sum_ref[:, :half] = sum_own
    sum_ref[:, half:] = sum_other
    la_ref[:, :LANES] = back_gate
    la_ref[:, LANES:] = back_up


def mlp_call(owners, block, x, n2, weights, la_gate, la_up, exit_gate, exit_up, d_mlp, low, high,
             d_la_d, entry, sums):
    rows = d_mlp.shape[0]
    half = weights[0].shape[0]
    size = TILE * len(owners)

    def tile(columns):
        return pl.BlockSpec((TILE, columns), lambda t, _: (t, 0))

    def whole(array):
        return pl.BlockSpec(array.shape, lambda t, _: (0, 0))

    units = pl.BlockSpec((TILE, half), lambda t, sc: (sc[0], 0))
    args = [n2, *weights, la_gate, la_up, exit_gate, exit_up, d_mlp, *low, *high, d_la_d, entry]
    in_specs = [tile(2 * half), whole(weights[0]), whole(weights[1]), tile(LANES), tile(LANES)]
    in_specs += [whole(exit_gate), whole(exit_up), tile(2 * half)] + [units] * 4
    in_specs += [tile(LANES), whole(entry)]
    aliases = {}
    if sums is not None:
        aliases = {1 + len(args): 3, 2 + len(args): 4}
        args += sums
        in_specs += [tile(2 * half), tile(2 * LANES)]
    return pl.pallas_call(
        lambda *refs: mlp_body(owners, sums is not None, *refs),
        grid_spec=pltpu.PrefetchScalarGridSpec(
            num_scalar_prefetch=1,
            grid=(rows // TILE,),
            in_specs=in_specs,
            out_specs=[tile(size)] * 3 + [tile(2 * half), tile(2 * LANES)],
        ),
        out_shape=[jax.ShapeDtypeStruct((rows, size), BF)] * 3
        + [
            jax.ShapeDtypeStruct((rows, 2 * half), F32),
            jax.ShapeDtypeStruct((rows, 2 * LANES), F32),
        ],
        input_output_aliases=aliases,
        name="units",
        cost_estimate=pl.CostEstimate(
            flops=20 * rows * half * size, bytes_accessed=32 << 20, transcendentals=rows * size
        ),
    )(jnp.stack([block, x]).astype(jnp.int32), *args)


def mlp_out_body(chunks, sc, *refs):
    mixed = refs[: len(chunks)]
    low_own, low_other, high_own, high_other, out_ref = refs[len(chunks) :]
    half = low_own.shape[1]
    low = high = None
    for (owners, ref) in zip(chunks, mixed):
        for n, w in enumerate(owners):
            at = pl.ds(pl.multiple_of(sc[w // 2] * TILE, TILE), TILE)
            at_own = sc[4] == w % 2
            part = ref[:, n * TILE : (n + 1) * TILE]
            more_low = low_dot(part, jnp.where(at_own, low_own[at, :], low_other[at, :]))
            more_high = low_dot(part, jnp.where(at_own, high_own[at, :], high_other[at, :]))
            low = more_low if low is None else low + more_low
            high = more_high if high is None else high + more_high
    out_ref[:, :half] = low
    out_ref[:, half:] = high


def mlp_out_call(chunks, z_slots, x, mixed, low, high):
    rows, half = mixed[0].shape[0], low[0].shape[1]
    places = jnp.stack([*z_slots, x]).astype(jnp.int32)
    return pl.pallas_call(
        lambda *refs: mlp_out_body(chunks, *refs),
        grid_spec=pltpu.PrefetchScalarGridSpec(
            num_scalar_prefetch=1,
            grid=(rows // TILE,),
            in_specs=[pl.BlockSpec((TILE, m.shape[1]), lambda t, _: (t, 0)) for m in mixed]
            + [pl.BlockSpec(low[0].shape, lambda t, _: (0, 0))] * 4,
            out_specs=pl.BlockSpec((TILE, 2 * half), lambda t, _: (t, 0)),
        ),
        out_shape=jax.ShapeDtypeStruct((rows, 2 * half), F32),
        name="units_out",
        cost_estimate=pl.CostEstimate(
            flops=4 * rows * half * 8 * TILE, bytes_accessed=20 << 20, transcendentals=0
        ),
    )(places, *mixed, *low, *high)


def attention_forward(query_heads, key_heads, value_heads, document_line):
    token_length = query_heads.shape[0]
    kv_dev = key_heads.shape[1] // HEAD_WIDTH
    per_kv = query_heads.shape[1] // key_heads.shape[1]
    block_rows = min(512, token_length)
    query_four = query_heads.reshape(token_length, kv_dev, per_kv, HEAD_WIDTH)
    key_three = key_heads.reshape(token_length, kv_dev, HEAD_WIDTH)
    value_three = value_heads.reshape(token_length, kv_dev, HEAD_WIDTH)
    key_pos = jnp.arange(token_length, dtype=jnp.int32)

    def scores_of(first_row):
        query_rows = lax.dynamic_slice_in_dim(query_four, first_row, block_rows, 0)
        row_docs = lax.dynamic_slice_in_dim(document_line, first_row, block_rows, 0)
        row_pos = first_row + jnp.arange(block_rows, dtype=jnp.int32)
        allowed = (row_docs[:, None] == document_line[None, :]) & (
            key_pos[None, :] <= row_pos[:, None]
        )
        raw_scores = jnp.einsum(
            "qkgd,skd->kgqs", query_rows, key_three, preferred_element_type=F32
        )
        return (jnp.where(allowed[None, None], SCORE_MULT * raw_scores, MASKED), query_rows)

    def forward_block(running_totals, block_index):
        logits, query_rows = scores_of(block_index * block_rows)
        row_max = jnp.max(logits, axis=-1, keepdims=True)
        shifted = jnp.exp(logits - row_max)
        row_sum = jnp.sum(shifted, axis=-1, keepdims=True)
        probs_low = (shifted / row_sum).astype(BF)
        mixed_rows = jnp.einsum(
            "kgqs,skd->qkgd", probs_low, value_three, preferred_element_type=F32
        )
        log_total = row_max[..., 0] + jnp.log(row_sum[..., 0])
        return (running_totals, (mixed_rows.reshape(block_rows, -1).astype(BF), log_total))

    block_ids = jnp.arange(token_length // block_rows, dtype=jnp.int32)
    _, (attn_blocks, log_totals) = lax.scan(forward_block, 0, block_ids)

    def backward(d_heads):
        d_heads_four = d_heads.reshape(token_length, kv_dev, per_kv, HEAD_WIDTH)

        def backward_block(running_totals, block_items):
            d_key_sum, d_value_sum = running_totals
            block_index, log_total = block_items
            first_row = block_index * block_rows
            logits, query_rows = scores_of(first_row)
            probs = jnp.exp(logits - log_total[..., None])
            d_rows = lax.dynamic_slice_in_dim(d_heads_four, first_row, block_rows, 0)
            d_probs = jnp.einsum(
                "qkgd,skd->kgqs", d_rows, value_three, preferred_element_type=F32
            )
            inner = jnp.sum(probs * d_probs, axis=-1, keepdims=True)
            d_logits = (probs * (d_probs - inner)).astype(BF)
            d_query_rows = SCORE_MULT * jnp.einsum(
                "kgqs,skd->qkgd", d_logits, key_three, preferred_element_type=F32
            )
            d_key_sum = d_key_sum + SCORE_MULT * jnp.einsum(
                "kgqs,qkgd->skd", d_logits, query_rows, preferred_element_type=F32
            )
            d_value_sum = d_value_sum + jnp.einsum(
                "kgqs,qkgd->skd", probs.astype(BF), d_rows, preferred_element_type=F32
            )
            return (
                (d_key_sum, d_value_sum),
                d_query_rows.astype(BF).reshape(block_rows, -1),
            )

        zero_keys = jnp.zeros((token_length, kv_dev, HEAD_WIDTH), F32)
        (d_key_sum, d_value_sum), d_query_blocks = lax.scan(
            backward_block, (zero_keys, zero_keys), (block_ids, log_totals)
        )
        return (
            d_query_blocks.reshape(token_length, -1),
            d_key_sum.astype(BF).reshape(token_length, -1),
            d_value_sum.astype(BF).reshape(token_length, -1),
        )

    return attn_blocks.reshape(token_length, -1), backward


def rope(values, cos_tab, sin_tab):
    rows, width = values.shape
    heads = values.astype(F32).reshape(rows, width // HEAD_WIDTH, HEAD_WIDTH)
    return rotate(heads, cos_tab, sin_tab).astype(BF).reshape(rows, width)


def plain_attention(
    x, weights, la_q, la_k, la_v, exit_q, exit_k, exit_v, document_line, *_
):
    rows = x.shape[0]
    q_cols, kv_cols = exit_q.shape[1], exit_k.shape[1]
    projected = low_dot(x[:, : weights[0].shape[0]], weights[0])
    cos_tab, sin_tab = rope_tables(jnp.arange(rows, dtype=jnp.int32), HEAD_WIDTH)
    query_rot = rope(projected[:, :q_cols] + low_dot(la_q, exit_q), cos_tab, sin_tab)
    key_rot = rope(
        projected[:, q_cols : q_cols + kv_cols] + low_dot(la_k, exit_k), cos_tab, sin_tab
    )
    value_low = (projected[:, q_cols + kv_cols :] + low_dot(la_v, exit_v)).astype(BF)
    attended, attention_back = attention_forward(query_rot, key_rot, value_low, document_line)

    def backward(d_heads, *_):
        d_query, d_key, d_value = attention_back(d_heads)
        return rope(d_query, cos_tab, -sin_tab), rope(d_key, cos_tab, -sin_tab), d_value

    return attended, lambda: attended, backward


def layer(mover, args):
    (
        tokens,
        token_document,
        document_adapter,
        attention_norm_gain,
        feedforward_norm_gain,
        query_weight,
        key_weight,
        value_weight,
        output_weight,
        gate_weight,
        up_weight,
        down_weight,
        attention_down_maps,
        query_exit_maps,
        key_value_exit_maps,
        output_entry_maps,
        output_exit_maps,
        feedforward_entry_maps,
        feedforward_exit_maps,
        down_entry_maps,
        down_exit_maps,
        cotangent,
    ) = args
    seq_size, wsh_size, s = mover.seq_size, mover.wsh_size, mover.s
    own_rows = tokens.shape[1]
    width = tokens.shape[2]
    adapters = attention_down_maps.shape[1]
    rank = query_exit_maps.shape[1]
    flat = adapters * rank
    doc_count = document_adapter.shape[1]
    q_cols = query_weight.shape[1] // seq_size
    kv_cols = key_weight.shape[1] // seq_size
    feature = width // seq_size
    row_block = width // wsh_size
    hidden = gate_weight.shape[1]
    hid_block = hidden // (wsh_size * seq_size)
    hid_own = hidden // seq_size

    def owners(docs):
        hot = (docs[:, None] == jnp.arange(doc_count, dtype=jnp.int32)[None, :]).astype(jnp.int32)
        return jnp.sum(hot * document_adapter[0][None, :], axis=1)

    def turned(maps):
        return maps.transpose(1, 2, 0).reshape(-1, maps.shape[0])

    def own_hidden(values, lower=0, upper=hid_own):
        parts, at = [], lower
        while at < upper:
            w = at // hid_block
            stop = min(upper, (w + 1) * hid_block)
            start = (w * seq_size + s) * hid_block + at - w * hid_block
            parts.append(cut(values, start, stop - at, 1))
            at = stop
        return parts

    qkv_local = jnp.concatenate(
        [
            cut(query_weight, s * q_cols, q_cols, 1),
            cut(key_weight, s * kv_cols, kv_cols, 1),
            cut(value_weight, s * kv_cols, kv_cols, 1),
        ],
        axis=1,
    )
    local_docs = token_document[0]
    own_owner = owners(local_docs)
    hidden_state = tokens[0].astype(F32)
    first_normed, scale_one = normed(hidden_state, attention_norm_gain)
    first_normed = first_normed.astype(BF)
    input_maps = turned(attention_down_maps)
    picked_first = reverse_product(first_normed, input_maps)
    picked_first = picked_first * adapter_mask(own_owner, 3 * rank, adapters)
    picked_first = fold(picked_first, 3 * rank, 0)
    last_lane = jnp.arange(LANES, dtype=jnp.int32)[None, :] == LANES - 1
    picked_first = jnp.where(last_lane, local_docs.astype(F32)[:, None], picked_first).astype(BF)

    half_width = width // 2
    down_local = cut(down_weight, s * hid_block, hid_block, 0)
    if mover.fast:
        chunks = [(0, 1), (2, 3), (4, 5), (6,), (7,)]
    else:
        chunks = [tuple(range(wsh_size))]
    chunk_bounds = [(c[0] * hid_block, (c[-1] + 1) * hid_block) for c in chunks]

    def gate_up_far(i, *deps):
        gate_late, up_late = after((gate_weight, up_weight), *deps)
        parts = own_hidden(gate_late, *chunk_bounds[i]) + own_hidden(up_late, *chunk_bounds[i])
        return mover.far(jnp.concatenate(parts, axis=1))

    output_gradient = cotangent[0].astype(F32)
    d_mlp_local = (RESIDUAL_MULT * output_gradient).astype(BF)
    first_cols = jnp.concatenate([mover.to_slots(first_normed, row_block), picked_first], axis=1)
    qkv_pair = mover.far(qkv_local)
    if mover.fast:
        d_mlp_other = lax.ppermute(d_mlp_local, "seq", Y_SWAP)
        first_other = after(lax.ppermute(first_cols, "seq", Y_SWAP), d_mlp_other)
        out_piece = mover.head_rows(output_weight)
        qkv_four = mover.near(qkv_pair)
        out_pair = mover.far(out_piece, qkv_pair)
        qkv_full = mover.across(qkv_four)
        first_all = mover.gather_rest(first_cols, first_other)
        out_four = mover.near(out_pair, qkv_four)
        low_pair = mover.far(down_local[:, :half_width], qkv_four)
        out_swapped = mover.across(out_four, qkv_full[1])
        out_full = mover.head_rows_done(out_swapped, output_weight.shape[0])
        d_mlp = mover.gather_rest(d_mlp_local, after(d_mlp_other, first_all))
        low_near = lax.ppermute(after(low_pair, out_four), "wsh", NEAR_SWAP)
        high_local = after(down_local[:, half_width:], low_pair, qkv_full[1])
        high_far = lax.ppermute(high_local, "wsh", FAR_SWAP)
    else:
        qkv_full = mover.across(qkv_pair)
        first_all = mover.gather_tokens(first_cols)
        d_mlp = mover.gather_tokens(d_mlp_local)
        out_full = mover.head_rows(output_weight)
        down_full = mover.across(down_local)[0]
    document_line = first_all[:, width + LANES - 1].astype(jnp.int32)
    owner = owners(document_line)
    mask_rank = adapter_mask(owner, rank, adapters)

    (
        query_exit_maps,
        key_value_exit_maps,
    ) = after((query_exit_maps, key_value_exit_maps), first_normed)
    query_exit = cut(query_exit_maps.reshape(flat, -1), s * q_cols, q_cols, 1)
    key_exit = cut(key_value_exit_maps[0].reshape(flat, -1), s * kv_cols, kv_cols, 1)
    value_exit = cut(key_value_exit_maps[1].reshape(flat, -1), s * kv_cols, kv_cols, 1)
    la_one = first_all[:, width:]
    la_q = spread(la_one, owner, rank, 0, adapters)
    la_k = spread(la_one, owner, rank, rank, adapters)
    la_v = spread(la_one, owner, rank, 2 * rank, adapters)
    token_length = first_all.shape[0]
    attend = fast_attention if mover.fast else plain_attention
    early, attend_rest, attention_back = attend(
        first_all, qkv_full, la_q, la_k, la_v, query_exit, key_exit, value_exit, document_line,
    )

    (
        feedforward_entry_maps,
        feedforward_exit_maps,
        down_entry_maps,
        down_exit_maps,
        output_entry_maps,
        output_exit_maps,
    ) = after(
        (
            feedforward_entry_maps,
            feedforward_exit_maps,
            down_entry_maps,
            down_exit_maps,
            output_entry_maps,
            output_exit_maps,
        ),
        early,
    )
    if mover.fast:
        low_four = jnp.concatenate([low_pair, after(low_near, early)], axis=0)
        high_pair = jnp.concatenate([high_local, after(high_far, early)], axis=0)
        low_rows = low_four.shape[0] // 2
        low_early = after(low_four[:low_rows], out_swapped[1], early)
        low_other = [
            lax.ppermute(low_early, "wsh", X_SWAP),
            lax.ppermute(after(low_four[low_rows:], early), "wsh", X_SWAP),
        ]
        down_low = (low_four, jnp.concatenate(low_other, axis=0))
        high_near = lax.ppermute(after(high_pair, low_four, early), "wsh", NEAR_SWAP)
        attended = attend_rest(out_full, high_pair, d_mlp)
        high_four = jnp.concatenate([high_pair, after(high_near, attended)], axis=0)
        chunk_pairs = [gate_up_far(0, high_four)]
        attended = after(attended, high_four, low_other[0])
        down_high = mover.across(high_four)
        chunk_fours = [mover.near(chunk_pairs[0], high_four)]
        chunk_pairs.append(gate_up_far(1, chunk_pairs[0]))
    else:
        attended = attend_rest()

    out_entry = cut(turned(output_entry_maps), s * q_cols, q_cols, 1)
    out_exit = output_exit_maps.reshape(flat, -1)
    la_out_part = fold(reverse_product(attended, out_entry) * mask_rank, rank, 0)
    attn_sum = mover.scatter_tokens(low_dot(attended, out_full), la_out_part)
    la_out_own = attn_sum[1].astype(BF)
    attention_path = attn_sum[0] + low_dot(
        spread(la_out_own, own_owner, rank, 0, adapters), out_exit
    )
    middle = hidden_state + RESIDUAL_MULT * attention_path
    if mover.fast:
        middle = after(middle, low_other[1], chunk_pairs[0])

    second_normed, scale_two = normed(middle, feedforward_norm_gain)
    second_normed = second_normed.astype(BF)
    entry_maps = turned(feedforward_entry_maps)
    picked_second = reverse_product(second_normed, entry_maps) * adapter_mask(
        own_owner, 2 * rank, adapters
    )
    picked_second = fold(picked_second, 2 * rank, rank) + la_out_own.astype(F32)
    second_cols = jnp.concatenate(
        [mover.to_slots(second_normed, row_block), picked_second.astype(BF)], axis=1
    )
    if mover.fast:
        second_other = lax.ppermute(second_cols, "seq", Y_SWAP)
        second_all = mover.gather_rest(
            second_cols, after(second_other, down_high[1], chunk_fours[0], chunk_pairs[1])
        )
    else:
        second_all = mover.gather_tokens(second_cols)
    la_out = spread(second_all[:, width:], owner, rank, 0, adapters)
    la_gate = spread(second_all[:, width:], owner, rank, rank, adapters)
    la_up = spread(second_all[:, width:], owner, rank, 2 * rank, adapters)

    down_exit = down_exit_maps.reshape(flat, -1)
    d_la_d = (reverse_product(d_mlp, down_exit) * mask_rank).astype(BF)
    down_entry = jnp.concatenate(own_hidden(turned(down_entry_maps)), axis=1)
    all_exits = feedforward_exit_maps.reshape(2, flat, -1)
    exits = [jnp.concatenate(own_hidden(all_exits[i]), axis=1) for i in range(2)]
    units_found = []
    if mover.fast:
        chunk_weights = [mover.across(chunk_fours[0])]
        sums = None
        for i, units in enumerate(chunks):
            if i + 1 < len(chunks):
                deps = [chunk_fours[i]] + ([] if sums is None else [sums[0]])
                chunk_fours.append(mover.near(chunk_pairs[i + 1], *deps))
                chunk_weights.append(mover.across(chunk_fours[i + 1]))
            if i + 2 < len(chunks):
                deps = [chunk_pairs[i + 1], down_high[1] if sums is None else sums[0]]
                chunk_pairs.append(gate_up_far(i + 2, *deps))
            lower, upper = chunk_bounds[i]
            units_in = after(second_all, *chunk_fours[i + 1 : i + 2], *chunk_pairs[i + 2 : i + 3])
            mixed, d_gate, d_up, *sums = mlp_call(
                units,
                mover.z_slot(units[0] // 2),
                mover.x,
                units_in,
                chunk_weights[i],
                la_gate,
                la_up,
                exits[0][:, lower:upper],
                exits[1][:, lower:upper],
                d_mlp,
                down_low,
                down_high,
                d_la_d,
                down_entry[:, lower:upper],
                sums,
            )
            units_found.append((mixed, d_gate, d_up))
        d_second, d_la_both = sums
        d_la_gate, d_la_up = d_la_both[:, :flat], d_la_both[:, flat:]
    else:
        weights = mover.across(gate_up_far(0))[0]
        both = low_dot(second_all[:, :width], weights)
        gate = both[:, :hid_own] + low_dot(la_gate, exits[0])
        up = both[:, hid_own:] + low_dot(la_up, exits[1])
        d_mixed = reverse_product(d_mlp, down_full) + low_dot(d_la_d, down_entry)
        sigma = jax.nn.sigmoid(gate)
        swish = gate * sigma
        mixed = (swish * up).astype(BF)
        d_gate = (d_mixed * up * sigma * (1.0 + gate * (1.0 - sigma))).astype(BF)
        d_up = (d_mixed * swish).astype(BF)
        d_second = reverse_product(jnp.concatenate([d_gate, d_up], axis=1), weights)
        d_la_gate = reverse_product(d_gate, exits[0])
        d_la_up = reverse_product(d_up, exits[1])
        units_found.append((mixed, d_gate, d_up))
    d_la_two_part = fold(d_la_gate * mask_rank, rank, 0) + fold(d_la_up * mask_rank, rank, rank)
    d_second_sum = mover.scatter_tokens(d_second, d_la_two_part, mark="second")
    units_found[-1] = after(units_found[-1], mover.marks.get("second_away"))
    mixed_parts = [found[0] for found in units_found]
    gate_grads = [gradient_product(la_gate, found[1]) for found in units_found]
    up_grads = [gradient_product(la_up, found[2]) for found in units_found]
    entry_grads = [gradient_product(d_la_d, found[0]) for found in units_found]
    d_la_two_own = d_second_sum[1].astype(BF)
    d_second_own = mover.from_slots(d_second_sum[0], row_block) + low_dot(
        spread(d_la_two_own, own_owner, 2 * rank, 0, adapters), entry_maps
    )
    grad_middle = output_gradient + normed_back(
        middle, scale_two, feedforward_norm_gain, d_second_own
    )
    d_attn_own = (RESIDUAL_MULT * grad_middle).astype(BF)
    gate_grad = jnp.concatenate(gate_grads, axis=1)
    up_grad = jnp.concatenate(up_grads, axis=1)
    down_in_grad = jnp.concatenate(entry_grads, axis=1)
    d_attn_cols = jnp.concatenate([d_attn_own, d_la_two_own], axis=1)
    if mover.fast:
        packed = jnp.concatenate([pack(v) for v in (gate_grad, up_grad, down_in_grad)], axis=0)
        hidden_half = mover.sum_start(packed, (mover.marks["second"],))
        d_attn_other = lax.ppermute(d_attn_cols, "seq", Y_SWAP)
        d_attn_all = mover.gather_rest(d_attn_cols, after(d_attn_other, hidden_half))
    else:
        d_attn_all = mover.gather_tokens(d_attn_cols)
    d_attn = d_attn_all[:, :width]

    mixed_all = jnp.concatenate(mixed_parts, axis=1)
    la_down_part = fold(reverse_product(mixed_all, down_entry) * mask_rank, rank, 0)
    if mover.fast:
        mlp_part = mlp_out_call(
            chunks, [mover.z_slot(i) for i in range(4)], mover.x, mixed_parts, down_low, down_high
        )
    else:
        mlp_part = low_dot(mixed_all, down_full)
    mlp_sum = mover.scatter_tokens(mlp_part, la_down_part, deps=(d_attn_all,), mark="mlp")
    if mover.fast:
        hidden_grads = mover.sum_hidden(
            hidden_half, (mover.marks["mlp"],), "hidden", (d_attn_all,)
        )
    else:
        hidden_grads = mover.plain_hidden([gate_grad, up_grad, down_in_grad], hid_block)
    hidden_sent = mover.marks.get("hidden", (None, None))
    la_down_own = mlp_sum[1].astype(BF)
    feedforward_path = mlp_sum[0] + low_dot(
        spread(la_down_own, own_owner, rank, 0, adapters), down_exit
    )
    layer_out = (middle + RESIDUAL_MULT * feedforward_path).astype(BF)[None]
    la_down = spread(mover.gather_tokens(la_down_own), owner, rank, 0, adapters)

    def own_features(slots):
        per = wsh_size // seq_size
        parts = [
            cut(slots, mover.slot_of(s * per + i) * row_block, row_block, 1) for i in range(per)
        ]
        return jnp.concatenate(parts, axis=1)

    d_la_two = spread(d_attn_all[:, width:], owner, 2 * rank, 0, adapters)
    entry_grad = gradient_product(d_la_two, own_features(second_all))
    down_out_grad = gradient_product(la_down, cut(d_mlp, s * feature, feature, 1))
    d_la_o = (reverse_product(d_attn, out_exit) * mask_rank).astype(BF)
    out_in_grad = gradient_product(d_la_o, attended)
    out_out_grad = gradient_product(la_out, cut(d_attn, s * feature, feature, 1))

    d_attended = (reverse_product(d_attn, out_full) + low_dot(d_la_o, out_entry)).astype(BF)
    d_query, d_key, d_value = attention_back(
        d_attended, (mover.marks.get("mlp"),), hidden_sent[:1]
    )
    d_la_one_part = (
        fold(reverse_product(d_query, query_exit) * mask_rank, rank, 0)
        + fold(reverse_product(d_key, key_exit) * mask_rank, rank, rank)
        + fold(reverse_product(d_value, value_exit) * mask_rank, rank, 2 * rank)
    )
    d_la_one = mover.sum_small(d_la_one_part.astype(BF), hidden_sent[1:]).astype(BF)
    d_qkv = jnp.concatenate([d_query, d_key, d_value], axis=1)
    d_qkv = after(d_qkv, d_la_one_part)
    d_first_sum = jnp.concatenate(
        mover.scatter_tokens(
            *[reverse_product(d_qkv, half) for half in qkv_full],
            deps=(d_la_one,),
            late=hidden_grads,
            mark="first",
        ),
        axis=1,
    )
    d_la_one_own = cut(d_la_one, s * own_rows, own_rows, 0)
    d_first = mover.from_slots(d_first_sum, row_block) + low_dot(
        spread(d_la_one_own, own_owner, 3 * rank, 0, adapters), input_maps
    )
    hidden_gradient = grad_middle + normed_back(
        hidden_state, scale_one, attention_norm_gain, d_first
    )
    attention_in_grad = gradient_product(
        spread(d_la_one, owner, 3 * rank, 0, adapters), own_features(first_all)
    )
    query_out_grad = gradient_product(la_q, d_query)
    key_out_grad = gradient_product(la_k, d_key)
    value_out_grad = gradient_product(la_v, d_value)
    first_sent = mover.marks.get("first")
    early_grads = mover.sum_features(
        [query_out_grad, down_out_grad, entry_grad, out_in_grad, out_out_grad],
        key_out_grad,
        value_out_grad,
        deps=(first_sent,),
        mark="features",
    )
    (last_grad,) = mover.sum_features(
        [attention_in_grad],
        mid=(mover.marks.get("first_away"),),
        back=(first_sent,),
        deps=(mover.marks.get("features"),),
        late=early_grads,
    )

    def back(values, shape):
        return values.reshape(shape[1], shape[2], shape[0]).transpose(2, 0, 1)

    return (
        layer_out,
        hidden_gradient[None],
        back(last_grad, attention_down_maps.shape),
        early_grads[0].reshape(query_exit_maps.shape),
        early_grads[5].reshape(key_value_exit_maps.shape),
        back(early_grads[3], output_entry_maps.shape),
        early_grads[4].reshape(output_exit_maps.shape),
        back(early_grads[2], feedforward_entry_maps.shape),
        hidden_grads[0].reshape(feedforward_exit_maps.shape),
        back(hidden_grads[1], down_entry_maps.shape),
        early_grads[1].reshape(down_exit_maps.shape),
    )


def solution(mesh):
    seq_size, wsh_size = mesh.shape["seq"], mesh.shape["wsh"]

    def on_device(*args):
        return layer(Mover(seq_size, wsh_size), args)

    rows = P("wsh", None)
    stream = P("wsh", "seq", None)
    in_specs = (stream, P("wsh", "seq"), rows, P(), P()) + (rows,) * 7 + (P(),) * 9 + (stream,)
    out_specs = (stream, stream) + (P(),) * 9
    return jax.shard_map(
        on_device, mesh=mesh, in_specs=in_specs, out_specs=out_specs, check_vma=False
    )
```

```python
import jax
import jax.numpy as jnp
from jax import lax
from jax.experimental import pallas as pl
from jax.experimental.pallas import tpu as pltpu
from jax.sharding import PartitionSpec as P

QUERY_HEADS = 32
KEY_HEADS = 8
HEAD_WIDTH = 64
LANES = 128
PACK = 512
TILE = 256

EPSILON = 1e-05
RESIDUAL_MULT = 0.22
SCORE_MULT = 0.015625
ROPE_BASE = 10000000.0
MASKED = -1e30

BF = jnp.bfloat16
F32 = jnp.float32

CORE_SWAP = [(s, s ^ 1) for s in range(4)]
Y_SWAP = [(s, s ^ 2) for s in range(4)]
X_SWAP = [(w, w ^ 1) for w in range(8)]
NEAR_SWAP = [(w, w ^ 2) for w in range(8)]
FAR_SWAP = [(w, w ^ 4) for w in range(8)]


def z_shift(steps):
    return [(2 * z + x, 2 * ((z + steps) % 4) + x) for z in range(4) for x in range(2)]


def low_dot(left, right):
    return jnp.dot(left, right, preferred_element_type=F32)


def gradient_product(left, right):
    return lax.dot_general(left, right, (((0,), (0,)), ((), ())), preferred_element_type=F32)


def reverse_product(left, right):
    return lax.dot_general(left, right, (((1,), (1,)), ((), ())), preferred_element_type=F32)


def normed(values, gain):
    norm_scale = lax.rsqrt(jnp.mean(values * values, axis=-1, keepdims=True) + EPSILON)
    return (values * norm_scale * gain, norm_scale)


def normed_back(values, norm_scale, gain, grad_in):
    scaled = grad_in * gain
    cubed = norm_scale * norm_scale * norm_scale
    return norm_scale * scaled - values * cubed * jnp.mean(scaled * values, axis=-1, keepdims=True)


def rope_tables(positions, head_size):
    half_size = head_size // 2
    inv_freq = ROPE_BASE ** (-(jnp.arange(half_size).astype(F32) * 2.0) / head_size)
    angles = positions.astype(F32)[:, None] * inv_freq[None, :]
    return (jnp.cos(angles)[:, None, :], jnp.sin(angles)[:, None, :])


def rotate(values, cos_tab, sin_tab):
    half_size = values.shape[-1] // 2
    former = values[..., :half_size]
    latter = values[..., half_size:]
    return jnp.concatenate(
        [former * cos_tab - latter * sin_tab, latter * cos_tab + former * sin_tab], axis=-1
    )


def cut(values, start, size, axis):
    return lax.dynamic_slice_in_dim(values, start, size, axis)


def pick(values, index, axis):
    return lax.dynamic_index_in_dim(values, index, axis, keepdims=False)


def adapter_mask(owner, ranks, adapters):
    lane = jnp.arange(adapters * ranks, dtype=jnp.int32) // ranks
    return (owner[:, None] == lane[None, :]).astype(F32)


def fold(masked, ranks, offset):
    rows = jnp.arange(masked.shape[1], dtype=jnp.int32) % ranks
    lanes = jnp.arange(LANES, dtype=jnp.int32) - offset
    return low_dot(masked.astype(BF), (rows[:, None] == lanes[None, :]).astype(BF))


def spread(folded, owner, ranks, offset, adapters):
    rows = jnp.arange(LANES, dtype=jnp.int32) - offset
    lanes = jnp.arange(adapters * ranks, dtype=jnp.int32) % ranks
    wide = low_dot(folded.astype(BF), (rows[:, None] == lanes[None, :]).astype(BF))
    return (wide * adapter_mask(owner, ranks, adapters)).astype(BF)


def pack(values):
    parts = [values[:, i : i + PACK] for i in range(0, values.shape[1], PACK)]
    return jnp.concatenate(parts, axis=0)


def after(values, *deps):
    deps = [d for d in deps if d is not None]
    if not deps:
        return values
    return lax.optimization_barrier((values, tuple(deps)))[0]


class Mover:
    def __init__(self, seq_size, wsh_size):
        self.seq_size, self.wsh_size = seq_size, wsh_size
        self.fast = seq_size == 4 and wsh_size == 8
        self.s, self.w = lax.axis_index("seq"), lax.axis_index("wsh")
        self.y, self.c = self.s // 2, self.s % 2
        self.z, self.x = self.w // 2, self.w % 2
        self.marks = {}

    def far(self, chunk, *deps):
        chunk = after(chunk, *deps)
        if not self.fast:
            return chunk
        return jnp.concatenate([chunk, lax.ppermute(chunk, "wsh", FAR_SWAP)], axis=0)

    def near(self, pair, *deps):
        pair = after(pair, *deps)
        if not self.fast:
            return pair
        return jnp.concatenate([pair, lax.ppermute(pair, "wsh", NEAR_SWAP)], axis=0)

    def across(self, four, *deps):
        four = after(four, *deps)
        if not self.fast:
            return (lax.all_gather(four, "wsh", axis=0, tiled=True),)
        return four, lax.ppermute(four, "wsh", X_SWAP)

    def swap_bits(self, d):
        return d // 2 + 2 * (d % 2)

    def slot_owner(self, k):
        if not self.fast:
            return k
        return 2 * (self.z ^ self.swap_bits(k % 4)) + (self.x ^ (k // 4))

    def slot_of(self, w):
        if not self.fast:
            return w
        return self.z_slot(w // 2) + 4 * (self.x ^ (w % 2))

    def z_slot(self, z):
        return self.swap_bits(self.z ^ z)

    def to_slots(self, values, block):
        if not self.fast:
            return values
        parts = [cut(values, self.slot_owner(k) * block, block, 1) for k in range(self.wsh_size)]
        return jnp.concatenate(parts, axis=1)

    def from_slots(self, values, block):
        if not self.fast:
            return values
        parts = [cut(values, self.slot_of(w) * block, block, 1) for w in range(self.wsh_size)]
        return jnp.concatenate(parts, axis=1)

    def head_rows(self, weight):
        rows = weight.shape[0]
        per = self.wsh_size // self.seq_size
        if not self.fast:
            return cut(
                lax.all_gather(weight, "wsh", axis=0, tiled=True),
                self.s * per * rows,
                per * rows,
                0,
            )
        piece = rows // 4

        def part(z):
            return cut(weight, z * piece, piece, 0)

        def pairs(senders, step):
            return [
                (8 * s + 2 * (s ^ sender) + x, 8 * s + 2 * (s ^ sender ^ step) + x)
                for s in range(4)
                for sender in senders
                for x in range(2)
            ]

        z, axes = self.z, ("seq", "wsh")
        away = jnp.concatenate([part(z ^ 2), part(z ^ 3)], axis=0)
        got = lax.ppermute(away, axes, pairs((0,), 2))
        first = z == self.s
        mine = jnp.where(first, part(z), got[:piece])
        away = jnp.where(first, part(z ^ 1), got[piece:])
        got = lax.ppermute(away, axes, pairs((0, 2), 1))
        return jnp.where(first | (z == (self.s ^ 2)), mine, got)

    def head_rows_done(self, halves, rows):
        piece = rows // 4
        out = []
        for shard in range(2):
            half = jnp.where(self.x == shard, halves[0], halves[1])
            blocks = half.reshape(4, piece, half.shape[1])
            out += [pick(blocks, self.z_slot(j), 0) for j in range(4)]
        return jnp.concatenate(out, axis=0)

    def gather_tokens(self, values):
        if not self.fast:
            return lax.all_gather(values, "seq", axis=0, tiled=True)
        return self.gather_rest(values, lax.ppermute(values, "seq", Y_SWAP))

    def gather_rest(self, values, other):
        first = self.y == 0
        column = jnp.stack([jnp.where(first, values, other), jnp.where(first, other, values)])
        partner = lax.ppermute(column, "seq", CORE_SWAP)
        first = self.c == 0
        whole = jnp.stack(
            [jnp.where(first, column, partner), jnp.where(first, partner, column)], axis=1
        )
        return whole.reshape((4 * values.shape[0],) + values.shape[1:])

    def scatter_tokens(self, *partials, deps=(), late=(), mark=None):
        if not self.fast:
            return [
                lax.psum_scatter(v.astype(BF), "seq", scatter_dimension=0, tiled=True).astype(F32)
                for v in partials
            ]
        rows = partials[0].shape[0] // 4
        blocks = [v.reshape(2, 2, rows, v.shape[1]) for v in partials]
        out = jnp.concatenate([pick(v, 1 - self.c, 1).astype(BF) for v in blocks], axis=2)
        got = lax.ppermute(out, "seq", CORE_SWAP).astype(F32)
        mine = jnp.concatenate([pick(v, self.c, 1) for v in blocks], axis=2)
        away = (pick(mine, 1 - self.y, 0) + pick(got, 1 - self.y, 0)).astype(BF)
        other = lax.ppermute(after(away, *deps), "seq", Y_SWAP)
        self.marks[mark] = other
        if mark is not None:
            self.marks[mark + "_away"] = away
        other = after(other, *late).astype(F32)
        total = pick(mine, self.y, 0) + pick(got, self.y, 0) + other
        found, at = [], 0
        for v in partials:
            found.append(total[:, at : at + v.shape[1]])
            at += v.shape[1]
        return found

    def sum_small(self, partial, deps=()):
        if not self.fast:
            return lax.psum(partial, "seq")
        total = partial.astype(F32) + lax.ppermute(partial, "seq", CORE_SWAP).astype(F32)
        other = lax.ppermute(after(total.astype(BF), *deps), "seq", Y_SWAP)
        return total + other.astype(F32)

    def sum_plain(self, grad):
        total = lax.psum(grad.astype(BF), "wsh")
        return lax.all_gather(total.astype(BF), "seq", axis=0).astype(F32)

    def plain_hidden(self, grads, hid_block):
        found = []
        for grad in grads:
            rows = grad.shape[0]
            wide = self.sum_plain(grad).reshape(self.seq_size, rows, self.wsh_size, hid_block)
            found.append(wide.transpose(1, 2, 0, 3).reshape(rows, -1))
        return [jnp.stack(found[:2]), found[2]]

    def sum_hidden(self, half, deps, mark, early):
        parts = self.sum_end(half, deps, mark, early)
        s = self.s.astype(jnp.int32)[None]
        return [
            final_hidden(parts, s, 0, 2),
            final_hidden(parts, s, 8 * LANES, 1)[0],
        ]

    def sum_features(self, grads, key=None, value=None, mid=(), back=(), deps=(), late=(), mark=None):
        if not self.fast:
            grads = grads + ([key, value] if key is not None else [])
            found = []
            for grad in grads:
                found.append(self.sum_plain(grad).transpose(1, 0, 2).reshape(grad.shape[0], -1))
            return found[:-2] + [jnp.stack(found[-2:])] if key is not None else found
        packed = list(grads)
        if key is not None:
            rest = jnp.zeros((key.shape[0], PACK - 2 * LANES), F32)
            packed.append(jnp.concatenate([key, value, rest], axis=1))
        half = self.sum_start(jnp.concatenate(packed, axis=0), mid, back)
        parts = self.sum_end(half, deps, late=late)
        self.marks[mark] = parts[2]
        s = self.s.astype(jnp.int32)[None]
        found, at = [], 0
        for grad in grads:
            found.append(final_features(parts, s, at, grad.shape[0]))
            at += grad.shape[0]
        if key is not None:
            found.append(final_kv(parts, s, at))
        return found

    def sum_start(self, packed, mid=(), back=()):
        rows = packed.shape[0]
        halves = packed.reshape(2, rows // 2, PACK)
        got = lax.ppermute(pick(halves, 1 - self.x, 0).astype(BF), "wsh", X_SWAP)
        half = pick(halves, self.x, 0) + got.astype(F32)
        blocks = after(half, *mid).reshape(4, rows // 8, PACK)
        total = pick(blocks, self.z, 0)
        for r in range(1, 4):
            out = pick(blocks, (self.z + r) % 4, 0).astype(BF)
            total = total + lax.ppermute(out, "wsh", z_shift(r)).astype(F32)
        own = after(total.astype(BF), *back)
        got = [own] + [lax.ppermute(own, "wsh", z_shift(r)) for r in range(1, 4)]
        ring = jnp.stack(got)
        return jnp.concatenate([pick(ring, (self.z - j) % 4, 0) for j in range(4)], axis=0)

    def sum_end(self, half, deps=(), mark=None, early=(), late=()):
        rows = 2 * half.shape[0]
        half = after(half, *early)
        other = lax.ppermute(half, "wsh", X_SWAP)
        first = self.x == 0
        part = jnp.concatenate([jnp.where(first, half, other), jnp.where(first, other, half)])
        core = lax.ppermute(part, "seq", CORE_SWAP)
        if mark is None:
            other = after(lax.ppermute(after(part, *deps), "seq", Y_SWAP), *late)
        else:
            top = lax.ppermute(after(part[: rows // 2], *deps), "seq", Y_SWAP)
            rest = lax.ppermute(after(part[rows // 2 :], top), "seq", Y_SWAP)
            self.marks[mark] = (top, rest)
            other = jnp.concatenate([top, rest], axis=0)
        return part, core, other, lax.ppermute(other, "seq", CORE_SWAP)


def final_body(s_ref, own, core, other, last, out_ref):
    columns = own.shape[-1]
    for k in range(4):
        place = s_ref[0] ^ k
        low = jnp.where(place % 2 == 0, own[...], core[...])
        high = jnp.where(place % 2 == 0, other[...], last[...])
        value = jnp.where(place < 2, low, high).astype(F32)
        at = slice(k * columns, (k + 1) * columns)
        if len(out_ref.shape) == 3:
            out_ref[0, :, at] = value
        else:
            out_ref[:, at] = value


def final_call(parts, s, grid, part_block, part_map, out_shape, out_block, out_map):
    return pl.pallas_call(
        final_body,
        grid_spec=pltpu.PrefetchScalarGridSpec(
            num_scalar_prefetch=1,
            grid=grid,
            in_specs=[pl.BlockSpec(part_block, part_map)] * 4,
            out_specs=pl.BlockSpec(out_block, out_map),
        ),
        out_shape=jax.ShapeDtypeStruct(out_shape, F32),
        name="finish",
    )(s, *parts)


def final_features(parts, s, row, rows):
    at = row // LANES
    return final_call(
        parts,
        s,
        (rows // LANES,),
        (LANES, PACK),
        lambda i, _: (at + i, 0),
        (rows, 4 * PACK),
        (LANES, 4 * PACK),
        lambda i, _: (i, 0),
    )


def final_hidden(parts, s, row, count):
    at = row // LANES
    return final_call(
        parts,
        s,
        (count, 8),
        (LANES, TILE),
        lambda n, w, _: (at + 4 * n + w // 2, w % 2),
        (count, LANES, 32 * TILE),
        (1, LANES, 4 * TILE),
        lambda n, w, _: (n, 0, w),
    )


def final_kv(parts, s, row):
    at = row // LANES
    return final_call(
        parts,
        s,
        (2,),
        (LANES, LANES),
        lambda n, _: (at, n),
        (2, LANES, 4 * LANES),
        (1, LANES, 4 * LANES),
        lambda n, _: (n, 0, 0),
    )


def half_lanes(rows, half):
    lane = lax.broadcasted_iota(jnp.int32, (rows, LANES), 1)
    return (lane < HEAD_WIDTH) if half == 0 else (lane >= HEAD_WIDTH)


def turn(values, cos_tab, sin_tab):
    lane = lax.broadcasted_iota(jnp.int32, values.shape, 1)
    swapped = jnp.where(
        lane % HEAD_WIDTH < HEAD_WIDTH // 2,
        pltpu.roll(values, LANES - HEAD_WIDTH // 2, 1),
        pltpu.roll(values, HEAD_WIDTH // 2, 1),
    )
    return values * cos_tab + swapped * sin_tab


def twice(values, half):
    other = pltpu.roll(values, HEAD_WIDTH, 1)
    first = half_lanes(values.shape[0], 0)
    return jnp.where(first, values, other) if half == 0 else jnp.where(first, other, values)


def qkv_body(x_ref, w_own, w_other, la_q, la_k, la_v, exit_q, exit_kv, cos_ref, sin_ref, q_ref, k_ref, v_ref):
    cos_tab, sin_tab = cos_ref[...], sin_ref[...]
    half = w_own.shape[0]
    product = low_dot(x_ref[:, :half], w_own[...]) + low_dot(x_ref[:, half:], w_other[...])
    q_cols = q_ref.shape[1]
    query = product[:, :q_cols] + low_dot(la_q[...], exit_q[...])
    for i in range(0, q_cols, LANES):
        q_ref[:, i : i + LANES] = turn(query[:, i : i + LANES], cos_tab, sin_tab).astype(BF)
    key = product[:, q_cols : q_cols + LANES] + low_dot(la_k[...], exit_kv[0])
    key = turn(key, cos_tab, sin_tab)
    value = product[:, q_cols + LANES :] + low_dot(la_v[...], exit_kv[1])
    for half in range(2):
        k_ref[:, half * LANES : (half + 1) * LANES] = twice(key, half).astype(BF)
        v_ref[:, half * LANES : (half + 1) * LANES] = twice(value, half).astype(BF)


def qkv_call(x, weights, la_q, la_k, la_v, exit_q, exit_kv, cos_tab, sin_tab):
    rows, width = x.shape[0], 2 * weights[0].shape[0]
    q_cols = exit_q.shape[1]

    def tile(columns):
        return pl.BlockSpec((TILE, columns), lambda i: (i, 0))

    return pl.pallas_call(
        qkv_body,
        grid=(rows // TILE,),
        in_specs=[
            tile(width),
            pl.BlockSpec(weights[0].shape, lambda i: (0, 0)),
            pl.BlockSpec(weights[1].shape, lambda i: (0, 0)),
            tile(LANES),
            tile(LANES),
            tile(LANES),
            pl.BlockSpec(exit_q.shape, lambda i: (0, 0)),
            pl.BlockSpec(exit_kv.shape, lambda i: (0, 0, 0)),
            tile(LANES),
            tile(LANES),
        ],
        out_specs=[tile(q_cols), tile(2 * LANES), tile(2 * LANES)],
        out_shape=[
            jax.ShapeDtypeStruct((rows, q_cols), BF),
            jax.ShapeDtypeStruct((rows, 2 * LANES), BF),
            jax.ShapeDtypeStruct((rows, 2 * LANES), BF),
        ],
        name="qkv",
        cost_estimate=pl.CostEstimate(
            flops=2 * rows * width * weights[0].shape[1], bytes_accessed=12 << 20, transcendentals=0
        ),
    )(x, *weights, la_q, la_k, la_v, exit_q, exit_kv, cos_tab, sin_tab)


def allowed_pairs(i, t, doc_col, doc_row):
    start = pl.multiple_of(t * TILE, TILE)
    rows = i * TILE + lax.broadcasted_iota(jnp.int32, (TILE, TILE), 0)
    keys = start + lax.broadcasted_iota(jnp.int32, (TILE, TILE), 1)
    return (doc_col[...] == doc_row[:, pl.ds(start, TILE)]) & (keys <= rows)


def forward_body(first_ref, q_ref, k_ref, v_ref, doc_col, doc_row, o_ref, lse_ref, m_s, l_s, acc_s):
    i = pl.program_id(0)
    m_s[...] = jnp.full_like(m_s, MASKED)
    l_s[...] = jnp.zeros_like(l_s)
    acc_s[...] = jnp.zeros_like(acc_s)

    def step(t, carry):
        allowed = allowed_pairs(i, t, doc_col, doc_row)
        start = pl.multiple_of(t * TILE, TILE)
        keys, vals = k_ref[pl.ds(start, TILE), :], v_ref[pl.ds(start, TILE), :]
        for h in range(4):
            pair = q_ref[:, (h // 2) * LANES : (h // 2 + 1) * LANES]
            query = jnp.where(half_lanes(TILE, h % 2), pair, jnp.zeros_like(pair))
            logits = jnp.where(allowed, SCORE_MULT * reverse_product(query, keys), MASKED)
            old = m_s[h]
            top = jnp.maximum(old, jnp.max(logits, axis=1, keepdims=True))
            shrink = jnp.exp(old - top)
            shifted = jnp.exp(logits - top)
            m_s[h] = top
            l_s[h] = l_s[h] * shrink + jnp.sum(shifted, axis=1, keepdims=True)
            acc_s[h] = acc_s[h] * shrink + low_dot(shifted.astype(BF), vals)
        return carry

    lax.fori_loop(first_ref[i], i + 1, step, 0)
    lane = lax.broadcasted_iota(jnp.int32, (TILE, LANES), 1)
    total = jnp.zeros((TILE, LANES), F32)
    for p in range(2):
        both = [acc_s[2 * p + n] / l_s[2 * p + n] for n in range(2)]
        o_ref[:, p * LANES : (p + 1) * LANES] = jnp.where(
            half_lanes(TILE, 0), both[0], both[1]
        ).astype(BF)
    for h in range(4):
        total = jnp.where(lane == h, m_s[h] + jnp.log(l_s[h]), total)
    lse_ref[...] = total


def attention_call(j, first, query, keys, values, doc_col, doc_row):
    rows = query.shape[0]
    group = query.shape[1] // 2
    return pl.pallas_call(
        forward_body,
        grid_spec=pltpu.PrefetchScalarGridSpec(
            num_scalar_prefetch=1,
            grid=(rows // TILE,),
            in_specs=[
                pl.BlockSpec((TILE, group), lambda i, _: (i, j)),
                pl.BlockSpec((rows, LANES), lambda i, _: (0, j)),
                pl.BlockSpec((rows, LANES), lambda i, _: (0, j)),
                pl.BlockSpec((TILE, 1), lambda i, _: (i, 0)),
                pl.BlockSpec((1, rows), lambda i, _: (0, 0)),
            ],
            out_specs=[
                pl.BlockSpec((TILE, group), lambda i, _: (i, 0)),
                pl.BlockSpec((TILE, LANES), lambda i, _: (i, 0)),
            ],
            scratch_shapes=[
                pltpu.VMEM((4, TILE, 1), F32),
                pltpu.VMEM((4, TILE, 1), F32),
                pltpu.VMEM((4, TILE, LANES), F32),
            ],
        ),
        out_shape=[
            jax.ShapeDtypeStruct((rows, group), BF),
            jax.ShapeDtypeStruct((rows, LANES), F32),
        ],
        name="attention",
        cost_estimate=pl.CostEstimate(
            flops=4 * 4 * rows * rows * LANES,
            bytes_accessed=3 << 20,
            transcendentals=4 * rows * rows,
        ),
    )(first, query, keys, values, doc_col, doc_row)


def backward_body(
    first_ref, q_ref, k_ref, v_ref, do_ref, o_ref, lse_ref, doc_col, doc_row, cos_ref, sin_ref,
    cos_all, sin_all, dq_ref, dk_ref, dv_ref, dq_s, dk_s, dv_s,
):
    i = pl.program_id(0)

    @pl.when(i == 0)
    def _():
        dk_s[...] = jnp.zeros_like(dk_s)
        dv_s[...] = jnp.zeros_like(dv_s)

    dq_s[...] = jnp.zeros_like(dq_s)
    queries, grads, deltas = [], [], []
    for h in range(4):
        at = slice((h // 2) * LANES, (h // 2 + 1) * LANES)
        half = half_lanes(TILE, h % 2)
        pair, grad = q_ref[:, at], do_ref[:, at]
        queries.append(jnp.where(half, pair, jnp.zeros_like(pair)))
        grads.append(jnp.where(half, grad, jnp.zeros_like(grad)))
        product = grads[h].astype(F32) * o_ref[:, at].astype(F32)
        deltas.append(jnp.sum(product, axis=1, keepdims=True))

    def step(t, carry):
        allowed = allowed_pairs(i, t, doc_col, doc_row)
        start = pl.multiple_of(t * TILE, TILE)
        at = pl.ds(start, TILE)
        keys, vals = k_ref[at, :], v_ref[at, :]
        dk, dv = dk_s[at, :], dv_s[at, :]
        for h in range(4):
            logits = jnp.where(allowed, SCORE_MULT * reverse_product(queries[h], keys), MASKED)
            probs = jnp.exp(logits - lse_ref[:, h : h + 1])
            d_probs = reverse_product(grads[h], vals)
            d_logits = (probs * (d_probs - deltas[h])).astype(BF)
            dq_s[h] = dq_s[h] + low_dot(d_logits, keys)
            dk = dk + gradient_product(d_logits, queries[h])
            dv = dv + gradient_product(probs.astype(BF), grads[h])
        dk_s[at, :] = dk
        dv_s[at, :] = dv
        return carry

    lax.fori_loop(first_ref[i], i + 1, step, 0)
    for p in range(2):
        both = jnp.where(half_lanes(TILE, 0), dq_s[2 * p], dq_s[2 * p + 1])
        both = (SCORE_MULT * both).astype(BF).astype(F32)
        dq_ref[:, p * LANES : (p + 1) * LANES] = turn(both, cos_ref[...], -sin_ref[...]).astype(BF)

    @pl.when(i == pl.num_programs(0) - 1)
    def _():
        def finish(t, carry):
            at = pl.ds(pl.multiple_of(t * TILE, TILE), TILE)
            dk, dv = dk_s[at, :], dv_s[at, :]
            dk = (SCORE_MULT * (dk + pltpu.roll(dk, HEAD_WIDTH, 1))).astype(BF).astype(F32)
            dk_ref[at, :] = turn(dk, cos_all[at, :], -sin_all[at, :]).astype(BF)
            dv_ref[at, :] = (dv + pltpu.roll(dv, HEAD_WIDTH, 1)).astype(BF)
            return carry

        lax.fori_loop(0, pl.num_programs(0), finish, 0)


def attention_back_call(
    j, first, query, keys, values, d_out, out, lse, doc_col, doc_row, cos_tab, sin_tab
):
    rows = query.shape[0]
    group = query.shape[1] // 2
    whole = pl.BlockSpec((rows, LANES), lambda i, _: (0, j))
    tile = pl.BlockSpec((TILE, group), lambda i, _: (i, j))
    table = pl.BlockSpec((TILE, LANES), lambda i, _: (i, 0))
    table_all = pl.BlockSpec((rows, LANES), lambda i, _: (0, 0))
    own_tile = pl.BlockSpec((TILE, group), lambda i, _: (i, 0))
    return pl.pallas_call(
        backward_body,
        grid_spec=pltpu.PrefetchScalarGridSpec(
            num_scalar_prefetch=1,
            grid=(rows // TILE,),
            in_specs=[
                tile,
                whole,
                whole,
                tile,
                own_tile,
                table,
                pl.BlockSpec((TILE, 1), lambda i, _: (i, 0)),
                pl.BlockSpec((1, rows), lambda i, _: (0, 0)),
                table,
                table,
                table_all,
                table_all,
            ],
            out_specs=[own_tile, table_all, table_all],
            scratch_shapes=[
                pltpu.VMEM((4, TILE, LANES), F32),
                pltpu.VMEM((rows, LANES), F32),
                pltpu.VMEM((rows, LANES), F32),
            ],
        ),
        out_shape=[
            jax.ShapeDtypeStruct((rows, group), BF),
            jax.ShapeDtypeStruct((rows, LANES), BF),
            jax.ShapeDtypeStruct((rows, LANES), BF),
        ],
        name="attention_back",
        cost_estimate=pl.CostEstimate(
            flops=4 * 10 * rows * rows * LANES,
            bytes_accessed=5 << 20,
            transcendentals=4 * rows * rows,
        ),
    )(first, query, keys, values, d_out, out, lse, doc_col, doc_row, cos_tab, sin_tab, cos_tab, sin_tab)


def fast_attention(
    x, weights, la_q, la_k, la_v, exit_q, exit_k, exit_v, document_line
):
    rows = x.shape[0]
    half = HEAD_WIDTH // 2
    cos_tab, sin_tab = rope_tables(jnp.arange(rows, dtype=jnp.int32), HEAD_WIDTH)
    cos_tab = jnp.tile(cos_tab.reshape(rows, half), (1, 4))
    sin_tab = sin_tab.reshape(rows, half)
    sin_tab = jnp.tile(jnp.concatenate([-sin_tab, sin_tab], axis=1), (1, 2))
    first_docs = document_line[::TILE]
    first = jnp.sum((document_line[None, :] < first_docs[:, None]).astype(jnp.int32), axis=1)
    first = first // TILE
    doc_col, doc_row = document_line[:, None], document_line[None, :]
    query, keys, values = qkv_call(
        x, weights, la_q, la_k, la_v, exit_q, jnp.stack([exit_k, exit_v]), cos_tab, sin_tab
    )
    early = attention_call(0, first, query, keys, values, doc_col, doc_row)
    found = [early]

    def finish(*deps):
        query_late = after(query, early[0], *deps)
        found.append(attention_call(1, first, query_late, keys, values, doc_col, doc_row))
        return jnp.concatenate([early[0], found[1][0]], axis=1)

    def backward(d_heads, between, behind):
        back = []
        for j in range(2):
            if j:
                d_heads = after(d_heads, back[0][1], *between)
            args = (first, query, keys, values, d_heads, *found[j], doc_col, doc_row)
            back.append(attention_back_call(j, *args, cos_tab, sin_tab))
        back[1] = after(back[1], *behind)
        lane = jnp.arange(LANES, dtype=jnp.int32)[None, :] < HEAD_WIDTH
        d_query = jnp.concatenate([back[0][0], back[1][0]], axis=1)
        d_key = jnp.where(lane, back[0][1], back[1][1])
        d_value = jnp.where(lane, back[0][2], back[1][2])
        return d_query, d_key, d_value

    return early[0], finish, backward


def units_rows(at_own, own, other):
    return jnp.where(at_own, own[...], other[...])


def mlp_body(owners, add, sc, n2, w_own, w_other, la_gate, la_up, exit_gate, exit_up, d_mlp,
             low_own, low_other, high_own, high_other, d_la_d, entry, *rest):
    if add:
        sum_in, la_in, mixed_ref, gate_ref, up_ref, sum_ref, la_ref = rest
    else:
        mixed_ref, gate_ref, up_ref, sum_ref, la_ref = rest
    half = w_own.shape[0]
    size = TILE * len(owners)
    both = low_dot(n2[:, :half], w_own[...]) + low_dot(n2[:, half:], w_other[...])
    gate = both[:, :size] + low_dot(la_gate[...], exit_gate[...])
    up = both[:, size:] + low_dot(la_up[...], exit_up[...])
    parts = []
    for w in owners:
        at_own = sc[1] == w % 2
        parts.append(
            reverse_product(d_mlp[:, :half], units_rows(at_own, low_own, low_other))
            + reverse_product(d_mlp[:, half:], units_rows(at_own, high_own, high_other))
        )
    d_mixed = jnp.concatenate(parts, axis=1) + low_dot(d_la_d[...], entry[...])
    sigma = jax.nn.sigmoid(gate)
    swish = gate * sigma
    mixed_ref[...] = (swish * up).astype(BF)
    d_gate = (d_mixed * up * sigma * (1.0 + gate * (1.0 - sigma))).astype(BF)
    d_up = (d_mixed * swish).astype(BF)
    gate_ref[...] = d_gate
    up_ref[...] = d_up
    d_both = jnp.concatenate([d_gate, d_up], axis=1)
    sum_own, sum_other = reverse_product(d_both, w_own[...]), reverse_product(d_both, w_other[...])
    back_gate, back_up = reverse_product(d_gate, exit_gate[...]), reverse_product(d_up, exit_up[...])
    if add:
        sum_own, sum_other = sum_own + sum_in[:, :half], sum_other + sum_in[:, half:]
        back_gate, back_up = back_gate + la_in[:, :LANES], back_up + la_in[:, LANES:]
    sum_ref[:, :half] = sum_own
    sum_ref[:, half:] = sum_other
    la_ref[:, :LANES] = back_gate
    la_ref[:, LANES:] = back_up


def mlp_call(owners, block, x, n2, weights, la_gate, la_up, exit_gate, exit_up, d_mlp, low, high,
             d_la_d, entry, sums):
    rows = d_mlp.shape[0]
    half = weights[0].shape[0]
    size = TILE * len(owners)

    def tile(columns):
        return pl.BlockSpec((TILE, columns), lambda t, _: (t, 0))

    def whole(array):
        return pl.BlockSpec(array.shape, lambda t, _: (0, 0))

    units = pl.BlockSpec((TILE, half), lambda t, sc: (sc[0], 0))
    args = [n2, *weights, la_gate, la_up, exit_gate, exit_up, d_mlp, *low, *high, d_la_d, entry]
    in_specs = [tile(2 * half), whole(weights[0]), whole(weights[1]), tile(LANES), tile(LANES)]
    in_specs += [whole(exit_gate), whole(exit_up), tile(2 * half)] + [units] * 4
    in_specs += [tile(LANES), whole(entry)]
    aliases = {}
    if sums is not None:
        aliases = {1 + len(args): 3, 2 + len(args): 4}
        args += sums
        in_specs += [tile(2 * half), tile(2 * LANES)]
    return pl.pallas_call(
        lambda *refs: mlp_body(owners, sums is not None, *refs),
        grid_spec=pltpu.PrefetchScalarGridSpec(
            num_scalar_prefetch=1,
            grid=(rows // TILE,),
            in_specs=in_specs,
            out_specs=[tile(size)] * 3 + [tile(2 * half), tile(2 * LANES)],
        ),
        out_shape=[jax.ShapeDtypeStruct((rows, size), BF)] * 3
        + [
            jax.ShapeDtypeStruct((rows, 2 * half), F32),
            jax.ShapeDtypeStruct((rows, 2 * LANES), F32),
        ],
        input_output_aliases=aliases,
        name="units",
        cost_estimate=pl.CostEstimate(
            flops=20 * rows * half * size, bytes_accessed=32 << 20, transcendentals=rows * size
        ),
    )(jnp.stack([block, x]).astype(jnp.int32), *args)


def mlp_out_body(chunks, sc, *refs):
    mixed = refs[: len(chunks)]
    low_own, low_other, high_own, high_other, out_ref = refs[len(chunks) :]
    half = low_own.shape[1]
    low = high = None
    for (owners, ref) in zip(chunks, mixed):
        for n, w in enumerate(owners):
            at = pl.ds(pl.multiple_of(sc[w // 2] * TILE, TILE), TILE)
            at_own = sc[4] == w % 2
            part = ref[:, n * TILE : (n + 1) * TILE]
            more_low = low_dot(part, jnp.where(at_own, low_own[at, :], low_other[at, :]))
            more_high = low_dot(part, jnp.where(at_own, high_own[at, :], high_other[at, :]))
            low = more_low if low is None else low + more_low
            high = more_high if high is None else high + more_high
    out_ref[:, :half] = low
    out_ref[:, half:] = high


def mlp_out_call(chunks, z_slots, x, mixed, low, high):
    rows, half = mixed[0].shape[0], low[0].shape[1]
    places = jnp.stack([*z_slots, x]).astype(jnp.int32)
    return pl.pallas_call(
        lambda *refs: mlp_out_body(chunks, *refs),
        grid_spec=pltpu.PrefetchScalarGridSpec(
            num_scalar_prefetch=1,
            grid=(rows // TILE,),
            in_specs=[pl.BlockSpec((TILE, m.shape[1]), lambda t, _: (t, 0)) for m in mixed]
            + [pl.BlockSpec(low[0].shape, lambda t, _: (0, 0))] * 4,
            out_specs=pl.BlockSpec((TILE, 2 * half), lambda t, _: (t, 0)),
        ),
        out_shape=jax.ShapeDtypeStruct((rows, 2 * half), F32),
        name="units_out",
        cost_estimate=pl.CostEstimate(
            flops=4 * rows * half * 8 * TILE, bytes_accessed=20 << 20, transcendentals=0
        ),
    )(places, *mixed, *low, *high)


def attention_forward(query_heads, key_heads, value_heads, document_line):
    token_length = query_heads.shape[0]
    kv_dev = key_heads.shape[1] // HEAD_WIDTH
    per_kv = query_heads.shape[1] // key_heads.shape[1]
    block_rows = min(512, token_length)
    query_four = query_heads.reshape(token_length, kv_dev, per_kv, HEAD_WIDTH)
    key_three = key_heads.reshape(token_length, kv_dev, HEAD_WIDTH)
    value_three = value_heads.reshape(token_length, kv_dev, HEAD_WIDTH)
    key_pos = jnp.arange(token_length, dtype=jnp.int32)

    def scores_of(first_row):
        query_rows = lax.dynamic_slice_in_dim(query_four, first_row, block_rows, 0)
        row_docs = lax.dynamic_slice_in_dim(document_line, first_row, block_rows, 0)
        row_pos = first_row + jnp.arange(block_rows, dtype=jnp.int32)
        allowed = (row_docs[:, None] == document_line[None, :]) & (
            key_pos[None, :] <= row_pos[:, None]
        )
        raw_scores = jnp.einsum(
            "qkgd,skd->kgqs", query_rows, key_three, preferred_element_type=F32
        )
        return (jnp.where(allowed[None, None], SCORE_MULT * raw_scores, MASKED), query_rows)

    def forward_block(running_totals, block_index):
        logits, query_rows = scores_of(block_index * block_rows)
        row_max = jnp.max(logits, axis=-1, keepdims=True)
        shifted = jnp.exp(logits - row_max)
        row_sum = jnp.sum(shifted, axis=-1, keepdims=True)
        probs_low = (shifted / row_sum).astype(BF)
        mixed_rows = jnp.einsum(
            "kgqs,skd->qkgd", probs_low, value_three, preferred_element_type=F32
        )
        log_total = row_max[..., 0] + jnp.log(row_sum[..., 0])
        return (running_totals, (mixed_rows.reshape(block_rows, -1).astype(BF), log_total))

    block_ids = jnp.arange(token_length // block_rows, dtype=jnp.int32)
    _, (attn_blocks, log_totals) = lax.scan(forward_block, 0, block_ids)

    def backward(d_heads):
        d_heads_four = d_heads.reshape(token_length, kv_dev, per_kv, HEAD_WIDTH)

        def backward_block(running_totals, block_items):
            d_key_sum, d_value_sum = running_totals
            block_index, log_total = block_items
            first_row = block_index * block_rows
            logits, query_rows = scores_of(first_row)
            probs = jnp.exp(logits - log_total[..., None])
            d_rows = lax.dynamic_slice_in_dim(d_heads_four, first_row, block_rows, 0)
            d_probs = jnp.einsum(
                "qkgd,skd->kgqs", d_rows, value_three, preferred_element_type=F32
            )
            inner = jnp.sum(probs * d_probs, axis=-1, keepdims=True)
            d_logits = (probs * (d_probs - inner)).astype(BF)
            d_query_rows = SCORE_MULT * jnp.einsum(
                "kgqs,skd->qkgd", d_logits, key_three, preferred_element_type=F32
            )
            d_key_sum = d_key_sum + SCORE_MULT * jnp.einsum(
                "kgqs,qkgd->skd", d_logits, query_rows, preferred_element_type=F32
            )
            d_value_sum = d_value_sum + jnp.einsum(
                "kgqs,qkgd->skd", probs.astype(BF), d_rows, preferred_element_type=F32
            )
            return (
                (d_key_sum, d_value_sum),
                d_query_rows.astype(BF).reshape(block_rows, -1),
            )

        zero_keys = jnp.zeros((token_length, kv_dev, HEAD_WIDTH), F32)
        (d_key_sum, d_value_sum), d_query_blocks = lax.scan(
            backward_block, (zero_keys, zero_keys), (block_ids, log_totals)
        )
        return (
            d_query_blocks.reshape(token_length, -1),
            d_key_sum.astype(BF).reshape(token_length, -1),
            d_value_sum.astype(BF).reshape(token_length, -1),
        )

    return attn_blocks.reshape(token_length, -1), backward


def rope(values, cos_tab, sin_tab):
    rows, width = values.shape
    heads = values.astype(F32).reshape(rows, width // HEAD_WIDTH, HEAD_WIDTH)
    return rotate(heads, cos_tab, sin_tab).astype(BF).reshape(rows, width)


def plain_attention(
    x, weights, la_q, la_k, la_v, exit_q, exit_k, exit_v, document_line, *_
):
    rows = x.shape[0]
    q_cols, kv_cols = exit_q.shape[1], exit_k.shape[1]
    projected = low_dot(x[:, : weights[0].shape[0]], weights[0])
    cos_tab, sin_tab = rope_tables(jnp.arange(rows, dtype=jnp.int32), HEAD_WIDTH)
    query_rot = rope(projected[:, :q_cols] + low_dot(la_q, exit_q), cos_tab, sin_tab)
    key_rot = rope(
        projected[:, q_cols : q_cols + kv_cols] + low_dot(la_k, exit_k), cos_tab, sin_tab
    )
    value_low = (projected[:, q_cols + kv_cols :] + low_dot(la_v, exit_v)).astype(BF)
    attended, attention_back = attention_forward(query_rot, key_rot, value_low, document_line)

    def backward(d_heads, *_):
        d_query, d_key, d_value = attention_back(d_heads)
        return rope(d_query, cos_tab, -sin_tab), rope(d_key, cos_tab, -sin_tab), d_value

    return attended, lambda: attended, backward


def layer(mover, args):
    (
        tokens,
        token_document,
        document_adapter,
        attention_norm_gain,
        feedforward_norm_gain,
        query_weight,
        key_weight,
        value_weight,
        output_weight,
        gate_weight,
        up_weight,
        down_weight,
        attention_down_maps,
        query_exit_maps,
        key_value_exit_maps,
        output_entry_maps,
        output_exit_maps,
        feedforward_entry_maps,
        feedforward_exit_maps,
        down_entry_maps,
        down_exit_maps,
        cotangent,
    ) = args
    seq_size, wsh_size, s = mover.seq_size, mover.wsh_size, mover.s
    own_rows = tokens.shape[1]
    width = tokens.shape[2]
    adapters = attention_down_maps.shape[1]
    rank = query_exit_maps.shape[1]
    flat = adapters * rank
    doc_count = document_adapter.shape[1]
    q_cols = query_weight.shape[1] // seq_size
    kv_cols = key_weight.shape[1] // seq_size
    feature = width // seq_size
    row_block = width // wsh_size
    hidden = gate_weight.shape[1]
    hid_block = hidden // (wsh_size * seq_size)
    hid_own = hidden // seq_size

    def owners(docs):
        hot = (docs[:, None] == jnp.arange(doc_count, dtype=jnp.int32)[None, :]).astype(jnp.int32)
        return jnp.sum(hot * document_adapter[0][None, :], axis=1)

    def turned(maps):
        return maps.transpose(1, 2, 0).reshape(-1, maps.shape[0])

    def own_hidden(values, lower=0, upper=hid_own):
        parts, at = [], lower
        while at < upper:
            w = at // hid_block
            stop = min(upper, (w + 1) * hid_block)
            start = (w * seq_size + s) * hid_block + at - w * hid_block
            parts.append(cut(values, start, stop - at, 1))
            at = stop
        return parts

    qkv_local = jnp.concatenate(
        [
            cut(query_weight, s * q_cols, q_cols, 1),
            cut(key_weight, s * kv_cols, kv_cols, 1),
            cut(value_weight, s * kv_cols, kv_cols, 1),
        ],
        axis=1,
    )
    local_docs = token_document[0]
    own_owner = owners(local_docs)
    hidden_state = tokens[0].astype(F32)
    first_normed, scale_one = normed(hidden_state, attention_norm_gain)
    first_normed = first_normed.astype(BF)
    input_maps = turned(attention_down_maps)
    picked_first = reverse_product(first_normed, input_maps)
    picked_first = picked_first * adapter_mask(own_owner, 3 * rank, adapters)
    picked_first = fold(picked_first, 3 * rank, 0)
    last_lane = jnp.arange(LANES, dtype=jnp.int32)[None, :] == LANES - 1
    picked_first = jnp.where(last_lane, local_docs.astype(F32)[:, None], picked_first).astype(BF)

    half_width = width // 2
    down_local = cut(down_weight, s * hid_block, hid_block, 0)
    if mover.fast:
        chunks = [(0, 1), (2, 3), (4, 5), (6,), (7,)]
    else:
        chunks = [tuple(range(wsh_size))]
    chunk_bounds = [(c[0] * hid_block, (c[-1] + 1) * hid_block) for c in chunks]

    def gate_up_far(i, *deps):
        gate_late, up_late = after((gate_weight, up_weight), *deps)
        parts = own_hidden(gate_late, *chunk_bounds[i]) + own_hidden(up_late, *chunk_bounds[i])
        return mover.far(jnp.concatenate(parts, axis=1))

    output_gradient = cotangent[0].astype(F32)
    d_mlp_local = (RESIDUAL_MULT * output_gradient).astype(BF)
    first_cols = jnp.concatenate([mover.to_slots(first_normed, row_block), picked_first], axis=1)
    qkv_pair = mover.far(qkv_local)
    if mover.fast:
        d_mlp_other = lax.ppermute(d_mlp_local, "seq", Y_SWAP)
        first_other = after(lax.ppermute(first_cols, "seq", Y_SWAP), d_mlp_other)
        out_piece = mover.head_rows(output_weight)
        qkv_four = mover.near(qkv_pair)
        out_pair = mover.far(out_piece, qkv_pair)
        qkv_full = mover.across(qkv_four)
        first_all = mover.gather_rest(first_cols, first_other)
        out_four = mover.near(out_pair, qkv_four)
        low_pair = mover.far(down_local[:, :half_width], qkv_four)
        out_swapped = mover.across(out_four, qkv_full[1])
        out_full = mover.head_rows_done(out_swapped, output_weight.shape[0])
        d_mlp = mover.gather_rest(d_mlp_local, after(d_mlp_other, first_all))
        low_near = lax.ppermute(after(low_pair, out_four), "wsh", NEAR_SWAP)
        high_local = after(down_local[:, half_width:], low_pair, qkv_full[1])
        high_far = lax.ppermute(high_local, "wsh", FAR_SWAP)
    else:
        qkv_full = mover.across(qkv_pair)
        first_all = mover.gather_tokens(first_cols)
        d_mlp = mover.gather_tokens(d_mlp_local)
        out_full = mover.head_rows(output_weight)
        down_full = mover.across(down_local)[0]
    document_line = first_all[:, width + LANES - 1].astype(jnp.int32)
    owner = owners(document_line)
    mask_rank = adapter_mask(owner, rank, adapters)

    (
        query_exit_maps,
        key_value_exit_maps,
    ) = after((query_exit_maps, key_value_exit_maps), first_normed)
    query_exit = cut(query_exit_maps.reshape(flat, -1), s * q_cols, q_cols, 1)
    key_exit = cut(key_value_exit_maps[0].reshape(flat, -1), s * kv_cols, kv_cols, 1)
    value_exit = cut(key_value_exit_maps[1].reshape(flat, -1), s * kv_cols, kv_cols, 1)
    la_one = first_all[:, width:]
    la_q = spread(la_one, owner, rank, 0, adapters)
    la_k = spread(la_one, owner, rank, rank, adapters)
    la_v = spread(la_one, owner, rank, 2 * rank, adapters)
    token_length = first_all.shape[0]
    attend = fast_attention if mover.fast else plain_attention
    early, attend_rest, attention_back = attend(
        first_all, qkv_full, la_q, la_k, la_v, query_exit, key_exit, value_exit, document_line,
    )

    (
        feedforward_entry_maps,
        feedforward_exit_maps,
        down_entry_maps,
        down_exit_maps,
        output_entry_maps,
        output_exit_maps,
    ) = after(
        (
            feedforward_entry_maps,
            feedforward_exit_maps,
            down_entry_maps,
            down_exit_maps,
            output_entry_maps,
            output_exit_maps,
        ),
        early,
    )
    if mover.fast:
        low_four = jnp.concatenate([low_pair, after(low_near, early)], axis=0)
        high_pair = jnp.concatenate([high_local, after(high_far, early)], axis=0)
        low_rows = low_four.shape[0] // 2
        low_early = after(low_four[:low_rows], out_swapped[1], early)
        low_other = [
            lax.ppermute(low_early, "wsh", X_SWAP),
            lax.ppermute(after(low_four[low_rows:], early), "wsh", X_SWAP),
        ]
        down_low = (low_four, jnp.concatenate(low_other, axis=0))
        high_near = lax.ppermute(after(high_pair, low_four, early), "wsh", NEAR_SWAP)
        attended = attend_rest(out_full, high_pair, d_mlp)
        high_four = jnp.concatenate([high_pair, after(high_near, attended)], axis=0)
        chunk_pairs = [gate_up_far(0, high_four)]
        attended = after(attended, high_four, low_other[0])
        down_high = mover.across(high_four)
        chunk_fours = [mover.near(chunk_pairs[0], high_four)]
        chunk_pairs.append(gate_up_far(1, chunk_pairs[0]))
    else:
        attended = attend_rest()

    out_entry = cut(turned(output_entry_maps), s * q_cols, q_cols, 1)
    out_exit = output_exit_maps.reshape(flat, -1)
    la_out_part = fold(reverse_product(attended, out_entry) * mask_rank, rank, 0)
    attn_sum = mover.scatter_tokens(low_dot(attended, out_full), la_out_part)
    la_out_own = attn_sum[1].astype(BF)
    attention_path = attn_sum[0] + low_dot(
        spread(la_out_own, own_owner, rank, 0, adapters), out_exit
    )
    middle = hidden_state + RESIDUAL_MULT * attention_path
    if mover.fast:
        middle = after(middle, low_other[1], chunk_pairs[0])

    second_normed, scale_two = normed(middle, feedforward_norm_gain)
    second_normed = second_normed.astype(BF)
    entry_maps = turned(feedforward_entry_maps)
    picked_second = reverse_product(second_normed, entry_maps) * adapter_mask(
        own_owner, 2 * rank, adapters
    )
    picked_second = fold(picked_second, 2 * rank, rank) + la_out_own.astype(F32)
    second_cols = jnp.concatenate(
        [mover.to_slots(second_normed, row_block), picked_second.astype(BF)], axis=1
    )
    if mover.fast:
        second_other = lax.ppermute(second_cols, "seq", Y_SWAP)
        second_all = mover.gather_rest(
            second_cols, after(second_other, down_high[1], chunk_fours[0], chunk_pairs[1])
        )
    else:
        second_all = mover.gather_tokens(second_cols)
    la_out = spread(second_all[:, width:], owner, rank, 0, adapters)
    la_gate = spread(second_all[:, width:], owner, rank, rank, adapters)
    la_up = spread(second_all[:, width:], owner, rank, 2 * rank, adapters)

    down_exit = down_exit_maps.reshape(flat, -1)
    d_la_d = (reverse_product(d_mlp, down_exit) * mask_rank).astype(BF)
    down_entry = jnp.concatenate(own_hidden(turned(down_entry_maps)), axis=1)
    all_exits = feedforward_exit_maps.reshape(2, flat, -1)
    exits = [jnp.concatenate(own_hidden(all_exits[i]), axis=1) for i in range(2)]
    units_found = []
    if mover.fast:
        chunk_weights = [mover.across(chunk_fours[0])]
        sums = None
        for i, units in enumerate(chunks):
            if i + 1 < len(chunks):
                deps = [chunk_fours[i], second_all if sums is None else sums[0]]
                chunk_fours.append(mover.near(chunk_pairs[i + 1], *deps))
                chunk_weights.append(mover.across(chunk_fours[i + 1]))
            if i + 2 < len(chunks):
                deps = [chunk_pairs[i + 1], second_all if sums is None else sums[0]]
                chunk_pairs.append(gate_up_far(i + 2, *deps))
            lower, upper = chunk_bounds[i]
            units_in = after(second_all, *chunk_fours[i + 1 : i + 2], *chunk_pairs[i + 2 : i + 3])
            mixed, d_gate, d_up, *sums = mlp_call(
                units,
                mover.z_slot(units[0] // 2),
                mover.x,
                units_in,
                chunk_weights[i],
                la_gate,
                la_up,
                exits[0][:, lower:upper],
                exits[1][:, lower:upper],
                d_mlp,
                down_low,
                down_high,
                d_la_d,
                down_entry[:, lower:upper],
                sums,
            )
            units_found.append((mixed, d_gate, d_up))
        d_second, d_la_both = sums
        d_la_gate, d_la_up = d_la_both[:, :flat], d_la_both[:, flat:]
    else:
        weights = mover.across(gate_up_far(0))[0]
        both = low_dot(second_all[:, :width], weights)
        gate = both[:, :hid_own] + low_dot(la_gate, exits[0])
        up = both[:, hid_own:] + low_dot(la_up, exits[1])
        d_mixed = reverse_product(d_mlp, down_full) + low_dot(d_la_d, down_entry)
        sigma = jax.nn.sigmoid(gate)
        swish = gate * sigma
        mixed = (swish * up).astype(BF)
        d_gate = (d_mixed * up * sigma * (1.0 + gate * (1.0 - sigma))).astype(BF)
        d_up = (d_mixed * swish).astype(BF)
        d_second = reverse_product(jnp.concatenate([d_gate, d_up], axis=1), weights)
        d_la_gate = reverse_product(d_gate, exits[0])
        d_la_up = reverse_product(d_up, exits[1])
        units_found.append((mixed, d_gate, d_up))
    d_la_two_part = fold(d_la_gate * mask_rank, rank, 0) + fold(d_la_up * mask_rank, rank, rank)
    d_second_sum = mover.scatter_tokens(d_second, d_la_two_part, mark="second")
    units_found[-1] = after(units_found[-1], mover.marks.get("second_away"))
    mixed_parts = [found[0] for found in units_found]
    gate_grads = [gradient_product(la_gate, found[1]) for found in units_found]
    up_grads = [gradient_product(la_up, found[2]) for found in units_found]
    entry_grads = [gradient_product(d_la_d, found[0]) for found in units_found]
    d_la_two_own = d_second_sum[1].astype(BF)
    d_second_own = mover.from_slots(d_second_sum[0], row_block) + low_dot(
        spread(d_la_two_own, own_owner, 2 * rank, 0, adapters), entry_maps
    )
    grad_middle = output_gradient + normed_back(
        middle, scale_two, feedforward_norm_gain, d_second_own
    )
    d_attn_own = (RESIDUAL_MULT * grad_middle).astype(BF)
    gate_grad = jnp.concatenate(gate_grads, axis=1)
    up_grad = jnp.concatenate(up_grads, axis=1)
    down_in_grad = jnp.concatenate(entry_grads, axis=1)
    d_attn_cols = jnp.concatenate([d_attn_own, d_la_two_own], axis=1)
    if mover.fast:
        packed = jnp.concatenate([pack(v) for v in (gate_grad, up_grad, down_in_grad)], axis=0)
        hidden_half = mover.sum_start(packed, (mover.marks["second"],))
        d_attn_other = lax.ppermute(d_attn_cols, "seq", Y_SWAP)
        d_attn_all = mover.gather_rest(d_attn_cols, after(d_attn_other, hidden_half))
    else:
        d_attn_all = mover.gather_tokens(d_attn_cols)
    d_attn = d_attn_all[:, :width]

    mixed_all = jnp.concatenate(mixed_parts, axis=1)
    la_down_part = fold(reverse_product(mixed_all, down_entry) * mask_rank, rank, 0)
    if mover.fast:
        mlp_part = mlp_out_call(
            chunks, [mover.z_slot(i) for i in range(4)], mover.x, mixed_parts, down_low, down_high
        )
    else:
        mlp_part = low_dot(mixed_all, down_full)
    mlp_sum = mover.scatter_tokens(mlp_part, la_down_part, deps=(d_attn_all,), mark="mlp")
    if mover.fast:
        hidden_grads = mover.sum_hidden(
            hidden_half, (mover.marks["mlp"],), "hidden", (d_attn_all,)
        )
    else:
        hidden_grads = mover.plain_hidden([gate_grad, up_grad, down_in_grad], hid_block)
    hidden_sent = mover.marks.get("hidden", (None, None))
    la_down_own = mlp_sum[1].astype(BF)
    feedforward_path = mlp_sum[0] + low_dot(
        spread(la_down_own, own_owner, rank, 0, adapters), down_exit
    )
    layer_out = (middle + RESIDUAL_MULT * feedforward_path).astype(BF)[None]
    la_down = spread(mover.gather_tokens(la_down_own), owner, rank, 0, adapters)

    def own_features(slots):
        per = wsh_size // seq_size
        parts = [
            cut(slots, mover.slot_of(s * per + i) * row_block, row_block, 1) for i in range(per)
        ]
        return jnp.concatenate(parts, axis=1)

    d_la_two = spread(d_attn_all[:, width:], owner, 2 * rank, 0, adapters)
    entry_grad = gradient_product(d_la_two, own_features(second_all))
    down_out_grad = gradient_product(la_down, cut(d_mlp, s * feature, feature, 1))
    d_la_o = (reverse_product(d_attn, out_exit) * mask_rank).astype(BF)
    out_in_grad = gradient_product(d_la_o, attended)
    out_out_grad = gradient_product(la_out, cut(d_attn, s * feature, feature, 1))

    d_attended = (reverse_product(d_attn, out_full) + low_dot(d_la_o, out_entry)).astype(BF)
    d_query, d_key, d_value = attention_back(
        d_attended, (mover.marks.get("mlp"),), hidden_sent[:1]
    )
    d_la_one_part = (
        fold(reverse_product(d_query, query_exit) * mask_rank, rank, 0)
        + fold(reverse_product(d_key, key_exit) * mask_rank, rank, rank)
        + fold(reverse_product(d_value, value_exit) * mask_rank, rank, 2 * rank)
    )
    d_la_one = mover.sum_small(d_la_one_part.astype(BF), hidden_sent[1:]).astype(BF)
    d_qkv = jnp.concatenate([d_query, d_key, d_value], axis=1)
    d_qkv = after(d_qkv, d_la_one_part)
    d_first_sum = jnp.concatenate(
        mover.scatter_tokens(
            *[reverse_product(d_qkv, half) for half in qkv_full],
            deps=(d_la_one,),
            late=hidden_grads,
            mark="first",
        ),
        axis=1,
    )
    d_la_one_own = cut(d_la_one, s * own_rows, own_rows, 0)
    d_first = mover.from_slots(d_first_sum, row_block) + low_dot(
        spread(d_la_one_own, own_owner, 3 * rank, 0, adapters), input_maps
    )
    hidden_gradient = grad_middle + normed_back(
        hidden_state, scale_one, attention_norm_gain, d_first
    )
    attention_in_grad = gradient_product(
        spread(d_la_one, owner, 3 * rank, 0, adapters), own_features(first_all)
    )
    query_out_grad = gradient_product(la_q, d_query)
    key_out_grad = gradient_product(la_k, d_key)
    value_out_grad = gradient_product(la_v, d_value)
    first_sent = mover.marks.get("first")
    early_grads = mover.sum_features(
        [query_out_grad, down_out_grad, entry_grad, out_in_grad, out_out_grad],
        key_out_grad,
        value_out_grad,
        deps=(first_sent,),
        mark="features",
    )
    (last_grad,) = mover.sum_features(
        [attention_in_grad],
        mid=(mover.marks.get("first_away"),),
        back=(first_sent,),
        deps=(mover.marks.get("features"),),
        late=early_grads,
    )

    def back(values, shape):
        return values.reshape(shape[1], shape[2], shape[0]).transpose(2, 0, 1)

    return (
        layer_out,
        hidden_gradient[None],
        back(last_grad, attention_down_maps.shape),
        early_grads[0].reshape(query_exit_maps.shape),
        early_grads[5].reshape(key_value_exit_maps.shape),
        back(early_grads[3], output_entry_maps.shape),
        early_grads[4].reshape(output_exit_maps.shape),
        back(early_grads[2], feedforward_entry_maps.shape),
        hidden_grads[0].reshape(feedforward_exit_maps.shape),
        back(hidden_grads[1], down_entry_maps.shape),
        early_grads[1].reshape(down_exit_maps.shape),
    )


def solution(mesh):
    seq_size, wsh_size = mesh.shape["seq"], mesh.shape["wsh"]

    def on_device(*args):
        return layer(Mover(seq_size, wsh_size), args)

    rows = P("wsh", None)
    stream = P("wsh", "seq", None)
    in_specs = (stream, P("wsh", "seq"), rows, P(), P()) + (rows,) * 7 + (P(),) * 9 + (stream,)
    out_specs = (stream, stream) + (P(),) * 9
    return jax.shard_map(
        on_device, mesh=mesh, in_specs=in_specs, out_specs=out_specs, check_vma=False
    )
```
